512 devices in a mesh: bead: 4 (over x), space: 128 (over z, y, core).
Axes of the slice: x: 4, y: 4, z: 16, core: 2. Of those that a mesh axis runs over, the one named last changes fastest.
Arguments:
- positions: float32 [16, 3, 8192], P('bead', None, 'space'), may hold values from -6 to 6
- momenta: float32 [16, 3, 8192], P('bead', None, 'space'), may hold values from -6 to 6
- forces: float32 [16, 3, 8192], P('bead', None, 'space'), may hold values from -6 to 6
- species: int32 [8192], P('space'), may hold values 0 or 1
- neighbours: int32 [16, 4, 8192], P('bead', None, 'space'), may hold values from 0 to 95
- counts: int32 [16, 8192], P('bead', 'space'), may hold values from 1 to 4, as said below
- ghost_rows: int32 [128, 2, 16], P('space'), may hold values from 0 to 63, as said below
- embed: float32 [2, 128], replicated, may hold values from -6 to 6
- radial_one: float32 [8, 128], replicated, may hold values from -2 to 2
- radial_two: float32 [8, 128], replicated, may hold values from -2 to 2
- mix_one: float32 [384, 128], replicated, may hold values from -0.3125 to 0.3125
- mix_two: float32 [384, 128], replicated, may hold values from -0.3125 to 0.3125
- projection: float32 [128, 128], replicated, may hold values from -0.5 to 0.5
- readout: float32 [2, 128], replicated, may hold values from -6 to 6
Outputs:
- positions_next: float32 [16, 3, 8192], P('bead', None, 'space')
- momenta_next: float32 [16, 3, 8192], P('bead', None, 'space')
- forces_next: float32 [16, 3, 8192], P('bead', None, 'space')
The draws below stay inside these ranges and needn't reach their ends.
Inputs may be any that keep to these rules, and one draw needn't show every extreme that they name: `counts`: slots 0 to count - 1 of an atom are live. In every bead the first atom of every domain has 4 live slots. `ghost_rows`: each block names 16 distinct atoms of its own domain, given by their place among the domain's 64 atoms.
All inputs are finite; a program needn't handle non-finite values. No bound on the sum of `species` on one device may be relied on, other than what follows from the above.
Results may differ from the reference program's by a relative error of at most 0.0003.
Values sent between devices are 32-bit elements; how exact they have to be, the bound alone decides.
No kernel may reach another device: no remote copies, remote signals or barrier semaphores. Data moves between devices by JAX's collectives and lax.ppermute only.
A program may use at most 64 MiB of HBM per device.

```python
import math
import jax
import jax.numpy as jnp
from jax import lax

P_SIZE = 16
C = 128
NB = 8
K = 4
A_DEV = 64
GHOST = 16
DOMAINS = 128
ATOMS = 8192


def draw_counts(key, part):
    key_one, key_two = jax.random.split(key)
    density = jax.random.randint(key_one, (DOMAINS,), 1, 5)
    raw_count = jax.random.randint(key_two, (P_SIZE, ATOMS), 0, K)
    domain = jnp.arange(ATOMS) // A_DEV
    filled = 1 + raw_count * density[domain][None, :] // 4
    leading = jnp.arange(ATOMS) % A_DEV == 0
    return jnp.where(leading[None, :], K, filled).astype(jnp.int32)


def draw_ghost_rows(key, part):
    key_list = jax.random.split(key, DOMAINS * 2)

    def single_block(block_key):
        key_one, key_two = jax.random.split(block_key)
        inner_rows = jax.random.permutation(key_one, A_DEV - 2) + 1
        picked = jnp.concatenate([jnp.array([0, A_DEV - 1], dtype=jnp.int32), inner_rows[:GHOST - 2].astype(jnp.int32)])
        return picked[jax.random.permutation(key_two, GHOST)]
    return jax.vmap(single_block)(key_list).reshape(DOMAINS, 2, GHOST).astype(jnp.int32)


def plant(values, stream_key, least, largest):
    shape = values.shape
    place = [jax.random.randint(jax.random.fold_in(stream_key, axis), (), 0, shape[axis]) for axis in range(len(shape))]
    values = values.at[tuple(place)].set(least)
    longest = shape.index(max(shape))
    place[longest] = (place[longest] + 1) % shape[longest]
    return values.at[tuple(place)].set(largest)


def block_scale(rng, extent, shards, least, high):
    def one(position, shards_of):
        steps = jax.random.uniform(jax.random.fold_in(jax.random.fold_in(rng, 6), position), (shards_of,), jnp.float32, least / len(shards), high / len(shards))
        return jnp.repeat(jnp.exp(steps), extent[position] // shards_of).reshape((-1,) + (1,) * (len(extent) - position - 1))

    factor_of = one(*shards[0])
    for cut in shards[1:]:
        factor_of = factor_of * one(*cut)
    return factor_of


def gaussian(key, extent, deviation, bound, cuts=(), kind=jnp.bfloat16):
    factor_of = block_scale(key, extent, cuts, -0.22, 0.18) if cuts else 1.0
    drawn = jax.random.normal(key, extent, jnp.float32) * deviation * factor_of
    return jnp.minimum(jnp.maximum(drawn, -bound), bound).astype(kind)


def setup_inputs(seed: int = 0) -> dict:
    keys = jax.random.split(jax.random.key(seed), 15)
    return {
        "positions": gaussian(keys[0], (P_SIZE, 3, ATOMS), 1.0, 6.0, ((0, 4), (2, 128)), jnp.float32),
        "momenta": gaussian(keys[1], (P_SIZE, 3, ATOMS), 1.0, 6.0, ((0, 4), (2, 128)), jnp.float32),
        "forces": gaussian(keys[2], (P_SIZE, 3, ATOMS), 1.0, 6.0, ((0, 4), (2, 128)), jnp.float32),
        "species": plant((jax.random.randint(keys[3], (ATOMS,), 0, 3) < 1).astype(jnp.int32), jax.random.fold_in(keys[3], 1), 0, 1),
        "neighbours": plant(jax.random.randint(keys[4], (P_SIZE, K, ATOMS), 0, A_DEV + 2 * GHOST), jax.random.fold_in(keys[4], 1), 0, (A_DEV + 2 * GHOST) - 1).astype(jnp.int32),
        "counts": draw_counts(jax.random.fold_in(keys[14], 71), 0),
        "ghost_rows": draw_ghost_rows(jax.random.fold_in(keys[14], 71), 0),
        "embed": gaussian(keys[7], (2, C), 1.0, 6.0, (), jnp.float32),
        "radial_one": gaussian(keys[8], (NB, C), NB ** -0.5, 2.0, (), jnp.float32),
        "radial_two": gaussian(keys[9], (NB, C), NB ** -0.5, 2.0, (), jnp.float32),
        "mix_one": gaussian(keys[10], (3 * C, C), (3 * C) ** -0.5, 0.3125, (), jnp.float32),
        "mix_two": gaussian(keys[11], (3 * C, C), (3 * C) ** -0.5, 0.3125, (), jnp.float32),
        "projection": gaussian(keys[12], (C, C), C ** -0.5, 0.5, (), jnp.float32),
        "readout": gaussian(keys[13], (2, C), 1.0, 6.0, (), jnp.float32),
    }


exact_prec = lax.Precision.HIGHEST
time_step = 1.0
cycle_freq = 0.75

def mode_matrix(bead_count):
    mode_index = jnp.arange(bead_count, dtype=jnp.int32)
    phase_angle = 2.0 * math.pi * (mode_index[:, None] * mode_index[None, :]).astype(jnp.float32) / bead_count
    cosine = math.sqrt(2.0 / bead_count) * jnp.cos(phase_angle)
    sine_part = math.sqrt(2.0 / bead_count) * jnp.sin(phase_angle)
    column = mode_index[None, :]
    half_mode = bead_count // 2
    alternating = jnp.where(mode_index % 2 == 0, 1.0, -1.0)[:, None] / math.sqrt(bead_count)
    inner_part = jnp.where(column < half_mode, cosine, jnp.where(column == half_mode, alternating, sine_part))
    return jnp.where(column == 0, 1.0 / math.sqrt(bead_count), inner_part).astype(jnp.float32)

def propagate(normal, mode_ids, masses, bead_count):
    frequency = 2.0 * cycle_freq * jnp.sin(math.pi * mode_ids.astype(jnp.float32) / bead_count)
    phase_angle = frequency * time_step
    cosine = jnp.cos(phase_angle)[:, None, None]
    stiffness = (frequency * jnp.sin(phase_angle))[:, None, None]
    safe_freq = jnp.where(mode_ids == 0, 1.0, frequency)
    drift_gain = jnp.where(mode_ids == 0, time_step, jnp.sin(phase_angle) / safe_freq)[:, None, None]
    coords = normal[:, 0]
    moment = normal[:, 1]
    new_coords = cosine * coords + drift_gain * moment / masses
    new_moment = cosine * moment - stiffness * masses * coords
    return jnp.stack([new_coords, new_moment], axis=1)

def radial_rates(count):
    return 0.25 * 16.0 ** (jnp.arange(count, dtype=jnp.float32) / (count - 1))

def harmonics(coord_x, coord_y, coord_z):
    sqrt_three = math.sqrt(3.0)
    dist_sq = coord_x * coord_x + coord_y * coord_y + coord_z * coord_z
    return [jnp.ones_like(coord_x), coord_x, coord_y, coord_z, sqrt_three * coord_x * coord_y, sqrt_three * coord_y * coord_z, 0.5 * (3.0 * coord_z * coord_z - dist_sq), sqrt_three * coord_x * coord_z, 0.5 * sqrt_three * (coord_x * coord_x - coord_y * coord_y)]

def edge_geometry(pos_ext, neighbour_ids, live_slots, radial):
    atom_count = neighbour_ids.shape[1]
    offsets = pos_ext[:, neighbour_ids] - pos_ext[:, :atom_count][:, None, :]
    coord_x, coord_y, coord_z = (offsets[0], offsets[1], offsets[2])
    dist_sq = coord_x * coord_x + coord_y * coord_y + coord_z * coord_z
    harmonic = jnp.stack(harmonics(coord_x, coord_y, coord_z), axis=-1) * live_slots[..., None]
    gaussians = jnp.exp(-dist_sq[..., None] * radial_rates(radial.shape[0]))
    weights = jnp.einsum('kab,bc->kac', gaussians, radial, precision=exact_prec)
    return (harmonic, weights)

def invariants(harmonic, weights, values, neighbour_ids):
    gathered = values[neighbour_ids]
    moments = jnp.einsum('kal,kac->alc', harmonic, weights * gathered, precision=exact_prec) / neighbour_ids.shape[0]
    squares = moments * moments
    scalar_part = squares[:, 0]
    vector_part = lax.optimization_barrier(jnp.sum(squares[:, 1:4], axis=1))
    tensor_part = lax.optimization_barrier(jnp.sum(squares[:, 4:9], axis=1))
    return jnp.concatenate([scalar_part, vector_part, tensor_part], axis=1)

def layer_one(pos_ext, h0_ext, neighbour_ids, live_slots, radial, mixing):
    atom_count = neighbour_ids.shape[1]
    harmonic, weights = edge_geometry(pos_ext, neighbour_ids, live_slots, radial)
    feats = invariants(harmonic, weights, h0_ext, neighbour_ids)
    return h0_ext[:atom_count] + jax.nn.silu(jnp.dot(feats, mixing, precision=exact_prec))

def layer_two(pos_ext, hidden_one, u2_ext, neighbour_ids, live_slots, radial, mixing, readout):
    harmonic, weights = edge_geometry(pos_ext, neighbour_ids, live_slots, radial)
    feats = invariants(harmonic, weights, u2_ext, neighbour_ids)
    hidden_two = hidden_one + jax.nn.silu(jnp.dot(feats, mixing, precision=exact_prec))
    return jnp.sum(hidden_one * readout[0]) + jnp.sum(hidden_two * readout[1])

def reference(positions, momenta, forces, species, neighbours, counts, ghost_rows, embed, radial_one, radial_two, mix_one, mix_two, projection, readout):
    bead_count = positions.shape[0]
    atom_count = positions.shape[2]
    domain_count = ghost_rows.shape[0]
    per_domain = atom_count // domain_count
    slot_count = neighbours.shape[1]
    masses = 1.0 + 15.0 * species.astype(jnp.float32)
    half_kick = momenta + 0.5 * time_step * forces
    phase_space = jnp.stack([positions, half_kick], axis=1)
    matrix = mode_matrix(bead_count)
    normal = jnp.einsum('bk,bsxa->ksxa', matrix, phase_space, precision=exact_prec)
    moved = propagate(normal, jnp.arange(bead_count, dtype=jnp.int32), masses, bead_count)
    phase_space = jnp.einsum('bk,ksxa->bsxa', matrix, moved, precision=exact_prec)
    positions_next = phase_space[:, 0]
    momenta_mid = phase_space[:, 1]
    domain_base = jnp.arange(domain_count, dtype=jnp.int32) * per_domain
    local_ids = domain_base[:, None] + jnp.arange(per_domain, dtype=jnp.int32)[None, :]
    from_left = jnp.roll(domain_base[:, None] + ghost_rows[:, 0], 1, axis=0)
    from_right = jnp.roll(domain_base[:, None] + ghost_rows[:, 1], -1, axis=0)
    table = jnp.concatenate([local_ids, from_left, from_right], axis=1).astype(jnp.int32)
    domain_of = (jnp.arange(atom_count, dtype=jnp.int32) // per_domain).astype(jnp.int32)
    global_ids = table[domain_of[None, None, :], neighbours].astype(jnp.int32)
    live = (jnp.arange(slot_count, dtype=jnp.int32)[None, :, None] < counts[:, None, :]).astype(jnp.float32)
    kinds = species.astype(jnp.float32)
    hidden_zero = embed[0][None, :] + kinds[:, None] * (embed[1] - embed[0])[None, :]

    def bead_energy(pos, ids, live_slots):
        hidden_one = layer_one(pos, hidden_zero, ids, live_slots, radial_one, mix_one)
        u2_all = jnp.dot(hidden_one, projection, precision=exact_prec)
        return layer_two(pos, hidden_one, u2_all, ids, live_slots, radial_two, mix_two, readout)

    def bead_force(inputs):
        pos, ids, live_slots = inputs
        return -jax.grad(bead_energy)(pos, ids, live_slots)
    forces_next = lax.map(bead_force, (positions_next, global_ids, live))
    momenta_next = momenta_mid + 0.5 * time_step * forces_next
    return (positions_next, momenta_next, forces_next)
```

```python
import numpy as np

import jax
import jax.numpy as jnp
from jax import lax
from jax.experimental import pallas as pl
from jax.experimental.pallas import tpu as pltpu
from jax.sharding import PartitionSpec as P


F32 = jnp.float32
BF16 = jnp.bfloat16
BEADS = 16
TILES = 6
ROOT3 = float(np.sqrt(3.0))
VM = pl.BlockSpec(memory_space=pltpu.VMEM)
SM = pl.BlockSpec(memory_space=pltpu.SMEM)
RATES = 0.25 * 16.0 ** (np.arange(8) / 7.0)


def propagators():
    n = BEADS
    b = np.arange(n)
    phase = 2.0 * np.pi * np.outer(b, b) / n
    matrix = np.where(b[None] < n // 2, np.cos(phase), np.sin(phase)) * np.sqrt(2.0 / n)
    matrix[:, n // 2] = np.where(b % 2 == 0, 1.0, -1.0) / np.sqrt(n)
    matrix[:, 0] = 1.0 / np.sqrt(n)
    w = 1.5 * np.sin(np.pi * b / n)
    drift = np.where(b == 0, 1.0, np.sin(w) / np.where(b == 0, 1.0, w))
    return [(matrix * d) @ matrix.T for d in (np.cos(w), drift, w * np.sin(w))]


def mode_tables():
    cosine, drift, stiff = propagators()
    one = np.zeros((BEADS, 2, 8, 64), np.float32)
    four = np.zeros((4, 64, 64), np.float32)
    for bead in range(BEADS):
        for src in range(BEADS):
            for c in range(3):
                col = (src // 4) * 16 + (src % 4) * 3 + c
                one[bead, 0, c, col] = cosine[bead, src]
                one[bead, 1, c, col] = drift[bead, src]
                row = (bead % 4) * 4 + c
                four[bead // 4, row, col] = cosine[bead, src]
                four[bead // 4, 16 + row, col] = drift[bead, src]
                four[bead // 4, 32 + row, col] = cosine[bead, src]
                four[bead // 4, 48 + row, col] = stiff[bead, src]
    return one, four


def split(x):
    high = x.astype(BF16)
    return high, (x - high.astype(F32)).astype(BF16)


def dot(a, b):
    return lax.dot_general(a, b, (((1,), (0,)), ((), ())), preferred_element_type=F32)


def dot_t(a, b):
    return lax.dot_general(a, b, (((1,), (1,)), ((), ())), preferred_element_type=F32)


def dot3(a, b):
    return dot(a[0], b[0]) + (dot(a[0], b[1]) + dot(a[1], b[0]))


def lanes(rows):
    return lax.broadcasted_iota(jnp.int32, (rows, 128), 1)


def turn(x):
    return pltpu.roll(x, 64, 1)


def pack_kernel(place, pos, mom, force, species, nbr, counts, ghost, out):
    side = place[2]
    raw = [jnp.concatenate([pos[b], mom[b] + 0.5 * force[b]], axis=1) for b in range(4)]
    kind = species[...].astype(F32)
    ghosts = ghost[0].astype(F32)
    last = jnp.concatenate([ghosts[0:1], ghosts[1:2], jnp.zeros((1, 96), F32)], axis=1)
    for i in range(4):
        bead = i ^ (2 * side)
        e = nbr[bead].astype(F32)
        n = counts[pl.ds(bead, 1), :].astype(F32)
        rows = raw + [
            jnp.concatenate([e[0:1], e[1:2]], axis=1),
            jnp.concatenate([e[2:3], e[3:4]], axis=1),
            jnp.concatenate([n, kind], axis=1),
            last,
        ]
        block = jnp.concatenate(rows, axis=0)
        for r in range(4):
            out[r * 4 + i] = block


def modes_kernel(place, got, one, four, packed, pos_out, mom_out):
    r, dom, side = place[0], place[1], place[2]
    bead = 4 * r + (dom ^ (2 * side))
    low = lanes(8) < 64

    def stacked(d):
        return jnp.concatenate([got[s * 4 + d] for s in range(4)], axis=0)

    def exact(a, b):
        return jnp.dot(a, b, precision=lax.Precision.HIGHEST, preferred_element_type=F32)

    for t in range(2):
        even, odd = stacked(2 * t), stacked(2 * t + 1)
        info_even = got[r * 4 + 2 * t][8:16]
        info_odd = got[r * 4 + 2 * t + 1][8:16]
        left = jnp.where(low, info_even, turn(info_odd))
        right = jnp.where(low, turn(info_even), info_odd)
        kind = right[6:7]
        mass = 1.0 + 15.0 * kind
        cos_part = jnp.where(low, exact(one[bead, 0], even), turn(exact(one[bead, 0], odd)))
        drift_part = jnp.where(low, turn(exact(one[bead, 1], even)), exact(one[bead, 1], odd))
        coords = cos_part + drift_part / mass
        row = lax.broadcasted_iota(jnp.int32, (8, 128), 0)
        packed[t, 0:8] = jnp.where(row == 3, jnp.broadcast_to(kind, (8, 128)), coords)
        packed[t, 8:12] = left[4:8]
        packed[t, 12:16] = right[4:8]
    own = exact(four[r], stacked(dom))
    mass = 1.0 + 15.0 * turn(got[r * 4 + dom][8:16])[6:7]
    coords = own[0:16] + turn(own[16:32]) / mass
    moment = turn(own[32:48]) - mass * own[48:64]
    for b in range(4):
        pos_out[b] = coords[4 * b : 4 * b + 3, 0:64]
        mom_out[b] = moment[4 * b : 4 * b + 3, 0:64]


def force_kernel(
    place, own, plane_half, next_half, embed, radial_one, radial_two, mix_one, mix_two, proj, readout,
    out,
    pk, hot, ys, gp, mom_one, slope_one, u_two, du_two, tk, gk, rk, mom_two, dp, dyq,
):
    side = place[2]
    low = lanes(8) < 64
    low1 = lanes(1) < 64
    low_wide = lanes(128) < 64

    in_plane, across = plane_half[...], next_half[...]
    before = jnp.where(side == 1, in_plane, across)
    after = jnp.where(side == 1, across, in_plane)
    pk[0] = before[0]
    pk[1:3] = before
    pk[3:5] = own[...]
    pk[5:7] = after
    pk[7] = after[1]

    def column(row):
        return jnp.broadcast_to(row, (128, 128)).T

    base, step = embed[0:1], embed[1:2] - embed[0:1]
    base_col, step_col = column(base), column(step)
    top_col = column(readout[1:2])
    both_col = column(readout[0:1] + readout[1:2])
    w_one = jnp.concatenate([radial_one[...] * base, radial_one[...] * step], axis=0)
    w_one2 = split(w_one)
    w_one_cat = jnp.concatenate([w_one2[0], w_one2[0], w_one2[1]], axis=0).astype(F32).T.astype(BF16)
    w_two2 = split(radial_two[...])
    wh, wl = w_two2[0].astype(F32), w_two2[1].astype(F32)
    w_two_cat = jnp.concatenate([wh, wh, wl, jnp.zeros((8, 128), F32)], axis=0).T.astype(BF16)
    mix1, mix2, prj = split(mix_one[...]), split(mix_two[...]), split(proj[...])
    mix1_t = split(mix_one[...].T)
    mix2_t = split(mix_two[...].T)
    prj_t = split(proj[...].T)
    rate_row = lax.broadcasted_iota(jnp.int32, (8, 128), 0)
    rate = jnp.zeros((8, 128), F32)
    for n in range(8):
        rate = jnp.where(rate_row == n, float(RATES[n]), rate)
    spot = lax.broadcasted_iota(jnp.int32, (256, 128), 0).astype(F32)
    ghost_spot = lax.broadcasted_iota(jnp.int32, (32, 128), 0).astype(F32) + 64.0

    def sigmoid(v):
        return 1.0 / (1.0 + jnp.exp(-v))

    def first(t, _):
        here = pk[t + 1, 0:8]
        info = pk[t + 1, 8:16]
        beside = jnp.where(low, pk[t + 2, 0:8], pk[t, 0:8])
        wide = jnp.concatenate([here, beside], axis=1)
        a = wide.astype(BF16).astype(F32)
        b = (wide - a).astype(BF16).astype(F32)
        c = (wide - a - b).astype(BF16).astype(F32)
        parts = jnp.concatenate([a, b, c, jnp.zeros((8, 256), F32)], axis=0).astype(BF16)
        g_prev, g_here, g_next = pk[t, 11:12], info[3:4], pk[t + 2, 11:12]
        head = lanes(1) < 16
        table = jnp.concatenate(
            [
                jnp.where(head, turn(g_prev) + 192.0, turn(g_here) + 64.0),
                jnp.where(head, g_here, g_next + 128.0),
                jnp.zeros((14, 128), F32),
            ],
            axis=0,
        )[:, 0:32].astype(BF16)
        count = info[2:3]
        sums = [None] * 9
        for k, row in enumerate((0, 4, 1, 5)):
            e = info[row : row + 1]
            hit = jnp.where(ghost_spot == e, 1.0, 0.0).astype(BF16)
            far = dot(table, hit)
            n = jnp.where(
                e < 64.0, e + jnp.where(low1, 0.0, 64.0), jnp.where(low1, far[0:1], far[1:2])
            )
            one_hot = jnp.where(spot == n, 1.0, 0.0).astype(BF16)
            hot[t, :, k * 128 : (k + 1) * 128] = one_hot
            got = dot(parts, one_hot)
            there = got[0:8] + (got[8:16] + got[16:24])
            off = there - here
            x, y, z = off[0:1], off[1:2], off[2:3]
            q = x * x + y * y + z * z
            live = jnp.where(count > float(k), 0.25, 0.0)
            g = jnp.exp(-rate * q) * live
            both = jnp.concatenate([g, g * there[3:4]], axis=0)
            harmonic = [
                None, x, y, z, ROOT3 * x * y, ROOT3 * y * z, 0.5 * (3.0 * z * z - q), ROOT3 * x * z,
                (0.5 * ROOT3) * (x * x - y * y),
            ]
            gp[t, k] = both
            ys[t, k, 0:8] = jnp.concatenate(harmonic[1:9], axis=0)
            for l in range(9):
                term = both if l == 0 else harmonic[l] * both
                sums[l] = term if sums[l] is None else sums[l] + term
        high, lo = split(jnp.concatenate(sums, axis=1))
        moments = dot(w_one_cat, jnp.concatenate([high, lo, high], axis=0))
        m = [moments[:, l * 128 : (l + 1) * 128] for l in range(9)]
        for l in range(9):
            mom_one[t, l] = m[l]
        inv = jnp.concatenate(
            [m[0] * m[0], sum(m[l] * m[l] for l in (1, 2, 3)), sum(m[l] * m[l] for l in range(4, 9))],
            axis=0,
        )
        v = dot3(mix1_t, split(inv))
        sig = sigmoid(v)
        slope_one[t] = sig * (1.0 + v * (1.0 - sig))
        h = base_col + here[3:4] * step_col + v * sig
        u_two[t] = dot3(prj_t, split(h))
        return 0

    lax.fori_loop(0, TILES, first, 0)

    du_two[...] = jnp.zeros_like(du_two)
    dp[...] = jnp.zeros_like(dp)

    def second(t, _):
        near = u_two[t]
        beside = jnp.where(low_wide, u_two[t + 1], u_two[t - 1])
        high, lo = split(jnp.concatenate([near, beside], axis=1))
        parts = jnp.concatenate([high, lo], axis=0)
        for k in range(4):
            got = dot(parts, hot[t, :, k * 128 : (k + 1) * 128])
            nodes = got[0:128] + got[128:256]
            g = gp[t, k, 0:8]
            gh = g.astype(BF16).astype(F32)
            rows = jnp.concatenate([gh, g - gh, gh, jnp.zeros((8, 128), F32)], axis=0).astype(BF16)
            weight = dot(w_two_cat, rows)
            gk[k] = nodes
            rk[k] = weight
            tk[k] = nodes * weight
        squares = [None] * 3
        for l in range(9):
            m = None
            for k in range(4):
                term = tk[k] if l == 0 else ys[t, k, l - 1 : l] * tk[k]
                m = term if m is None else m + term
            mom_two[l] = m
            part = 0 if l == 0 else 1 if l < 4 else 2
            squares[part] = m * m if squares[part] is None else squares[part] + m * m
        v = dot3(mix2_t, split(jnp.concatenate(squares, axis=0)))
        sig = sigmoid(v)
        dv = top_col * (sig * (1.0 + v * (1.0 - sig)))
        dinv = 2.0 * dot3(mix2, split(dv))
        for l in range(9):
            part = 0 if l == 0 else 1 if l < 4 else 2
            mom_two[l] = mom_two[l] * dinv[part * 128 : (part + 1) * 128]
        back = None
        for k in range(4):
            dt = mom_two[0]
            dys = []
            for l in range(1, 9):
                dm = mom_two[l]
                dt = dt + ys[t, k, l - 1 : l] * dm
                dys.append(jnp.sum(dm * tk[k], axis=0, keepdims=True))
            g = gp[t, k, 0:8]
            dg = dot3(w_two2, split(dt * gk[k]))
            dq = jnp.sum(-rate * g * dg, axis=0, keepdims=True)
            dyq[t, k, 0:8] = jnp.concatenate(dys, axis=0)
            dyq[t, k, 8:16] = jnp.broadcast_to(dq, (8, 128))
            high, lo = split(dt * rk[k])
            term = dot_t(jnp.concatenate([high, lo], axis=0), hot[t, :, k * 128 : (k + 1) * 128])
            back = term if back is None else back + term
        back = back[0:128] + back[128:256]
        du_two[t] += back[:, 0:128]
        aside = back[:, 128:256]
        du_two[t + 1] += jnp.where(low_wide, aside, 0.0)
        du_two[t - 1] += jnp.where(low_wide, 0.0, aside)
        return 0

    lax.fori_loop(1, TILES - 1, second, 0)

    def third(t, _):
        dh = both_col + dot3(prj, split(du_two[t]))
        dinv = 2.0 * dot3(mix1, split(dh * slope_one[t]))
        parts = []
        for l in range(9):
            part = 0 if l == 0 else 1 if l < 4 else 2
            parts.append(mom_one[t, l] * dinv[part * 128 : (part + 1) * 128])
        dm = dot3(w_one2, split(jnp.concatenate(parts, axis=1)))
        dm = [dm[:, l * 128 : (l + 1) * 128] for l in range(9)]
        rate2 = jnp.concatenate([rate, rate], axis=0)
        back = None
        centre = None
        for k in range(4):
            g = gp[t, k]
            dg = dm[0]
            dys = []
            for l in range(1, 9):
                dg = dg + ys[t, k, l - 1 : l] * dm[l]
                dys.append(dyq[t, k, l - 1 : l] + jnp.sum(g * dm[l], axis=0, keepdims=True))
            dq = dyq[t, k, 8:9] - jnp.sum(rate2 * g * dg, axis=0, keepdims=True)
            x, y, z = ys[t, k, 0:1], ys[t, k, 1:2], ys[t, k, 2:3]
            d1, d2, d3, d4, d5, d6, d7, d8 = dys
            dx = d1 + ROOT3 * (y * d4 + z * d7 + x * d8) + x * (2.0 * dq - d6)
            dy = d2 + ROOT3 * (x * d4 + z * d5 - y * d8) + y * (2.0 * dq - d6)
            dz = d3 + ROOT3 * (y * d5 + x * d7) + 2.0 * z * (dq + d6)
            d = jnp.concatenate([dx, dy, dz, jnp.zeros((5, 128), F32)], axis=0)
            centre = d if centre is None else centre + d
            dh_ = d.astype(BF16).astype(F32)
            rows = jnp.concatenate([dh_, d - dh_], axis=0).astype(BF16)
            term = dot_t(rows, hot[t, :, k * 128 : (k + 1) * 128])
            back = term if back is None else back + term
        back = back[0:8] + back[8:16]
        dp[t] += back[:, 0:128] - centre
        aside = back[:, 128:256]
        dp[t + 1] += jnp.where(low, aside, 0.0)
        dp[t - 1] += jnp.where(low, 0.0, aside)
        return 0

    lax.fori_loop(1, TILES - 1, third, 0)

    for t in range(2):
        f = -dp[t + 2]
        out[2 * t] = f
        out[2 * t + 1] = turn(f)


def finish_kernel(place, got, mid, force_out, mom_out):
    side = place[2]
    for b in range(4):
        f = got[b ^ (2 * side)][0:3, 0:64]
        force_out[b] = f
        mom_out[b] = mid[b] + 0.5 * f


def shape(*dims):
    return jax.ShapeDtypeStruct(dims, F32)


def on_device(
    positions, momenta, forces, species, neighbours, counts, ghost_rows,
    embed, radial_one, radial_two, mix_one, mix_two, projection, readout,
):
    count = lax.axis_size("space")
    r = lax.axis_index("bead")
    s = lax.axis_index("space")
    place = jnp.stack([r, s % 4, (s // 4) % 2]).astype(jnp.int32)
    both = ("bead", "space")
    halves = [[b * count + h * 4 + i for b in range(4) for i in range(4)] for h in range(count // 4)]
    quads = [[b * count + h * 4 + i for i in range(4)] for b in range(4) for h in range(count // 4)]
    in_plane, across = [], []
    for b in range(4):
        for z in range(count // 8):
            for i in range(4):
                here = b * count + z * 8 + i
                mate = b * count + z * 8 + 4 + (i ^ 2)
                back = b * count + (z * 8 - 4) % count + (i ^ 2)
                in_plane += [(here, mate), (mate, here)]
                across += [(here, back), (back, here)]

    sent = pl.pallas_call(
        pack_kernel, out_shape=shape(16, 16, 128), in_specs=[SM] + [VM] * 7, out_specs=VM, name="pack",
    )(place, positions, momenta, forces, species[None, :], neighbours, counts, ghost_rows)
    got = lax.all_to_all(sent, both, 0, 0, axis_index_groups=halves)
    one, four = mode_tables()
    own, positions_next, mid = pl.pallas_call(
        modes_kernel,
        out_shape=(shape(2, 16, 128), shape(4, 3, 64), shape(4, 3, 64)),
        in_specs=[SM] + [VM] * 3,
        out_specs=(VM, VM, VM),
        name="modes",
    )(place, got, jnp.asarray(one), jnp.asarray(four))
    next_half = lax.ppermute(own, both, across)
    plane_half = lax.ppermute(own, both, in_plane)
    block = lambda *dims: pltpu.VMEM(dims, F32)
    grad = pl.pallas_call(
        force_kernel,
        out_shape=shape(4, 8, 128),
        in_specs=[SM] + [VM] * 10,
        out_specs=VM,
        scratch_shapes=[
            block(8, 16, 128),
            pltpu.VMEM((TILES, 256, 512), BF16),
            block(TILES, 4, 8, 128),
            block(TILES, 4, 16, 128),
            block(TILES, 9, 128, 128),
            block(TILES, 128, 128),
            block(TILES, 128, 128),
            block(TILES, 128, 128),
            block(4, 128, 128),
            block(4, 128, 128),
            block(4, 128, 128),
            block(9, 128, 128),
            block(TILES, 8, 128),
            block(TILES, 4, 16, 128),
        ],
        name="force",
    )(place, own, plane_half, next_half, embed, radial_one, radial_two, mix_one, mix_two, projection, readout)
    back = lax.all_to_all(grad, both, 0, 0, axis_index_groups=quads)
    forces_next, momenta_next = pl.pallas_call(
        finish_kernel,
        out_shape=(shape(4, 3, 64), shape(4, 3, 64)),
        in_specs=[SM] + [VM] * 2,
        out_specs=(VM, VM),
        name="finish",
    )(place, back, mid)
    return positions_next, momenta_next, forces_next


def solution(mesh):
    spread = P("bead", None, "space")
    placed = (
        spread, spread, spread, P("space"), spread, P("bead", "space"), P("space", None, None),
    ) + (P(),) * 7
    return jax.shard_map(
        on_device, mesh=mesh, in_specs=placed, out_specs=(spread,) * 3, check_vma=False
    )
```

```python
import numpy as np

import jax
import jax.numpy as jnp
from jax import lax
from jax.experimental import pallas as pl
from jax.experimental.pallas import tpu as pltpu
from jax.sharding import PartitionSpec as P


F32 = jnp.float32
BF16 = jnp.bfloat16
BEADS = 16
TILES = 6
ROOT3 = float(np.sqrt(3.0))
VM = pl.BlockSpec(memory_space=pltpu.VMEM)
SM = pl.BlockSpec(memory_space=pltpu.SMEM)
RATES = 0.25 * 16.0 ** (np.arange(8) / 7.0)


def propagators():
    n = BEADS
    b = np.arange(n)
    phase = 2.0 * np.pi * np.outer(b, b) / n
    matrix = np.where(b[None] < n // 2, np.cos(phase), np.sin(phase)) * np.sqrt(2.0 / n)
    matrix[:, n // 2] = np.where(b % 2 == 0, 1.0, -1.0) / np.sqrt(n)
    matrix[:, 0] = 1.0 / np.sqrt(n)
    w = 1.5 * np.sin(np.pi * b / n)
    drift = np.where(b == 0, 1.0, np.sin(w) / np.where(b == 0, 1.0, w))
    return [(matrix * d) @ matrix.T for d in (np.cos(w), drift, w * np.sin(w))]


def mode_tables():
    cosine, drift, stiff = propagators()
    one = np.zeros((BEADS, 16, 64), np.float32)
    four = np.zeros((4, 64, 64), np.float32)
    for bead in range(BEADS):
        for src in range(BEADS):
            for c in range(3):
                col = (src // 4) * 16 + c * 4 + src % 4
                one[bead, c, col] = cosine[bead, src]
                one[bead, 8 + c, col] = drift[bead, src]
                row = c * 4 + bead % 4
                four[bead // 4, row, col] = cosine[bead, src]
                four[bead // 4, 16 + row, col] = drift[bead, src]
                four[bead // 4, 32 + row, col] = cosine[bead, src]
                four[bead // 4, 48 + row, col] = stiff[bead, src]
    return one, four

def split(x):
    high = x.astype(BF16)
    return high, (x - high.astype(F32)).astype(BF16)


def dot(a, b):
    return lax.dot_general(a, b, (((1,), (0,)), ((), ())), preferred_element_type=F32)


def dot_t(a, b):
    return lax.dot_general(a, b, (((1,), (1,)), ((), ())), preferred_element_type=F32)


def dot3(a, b):
    return dot(a[0], b[0]) + (dot(a[0], b[1]) + dot(a[1], b[0]))


def lanes(rows):
    return lax.broadcasted_iota(jnp.int32, (rows, 128), 1)


def turn(x):
    return pltpu.roll(x, 64, 1)


def exact(a, b):
    return jnp.dot(a, b, precision=lax.Precision.HIGHEST, preferred_element_type=F32)


def pick(y):
    return (y % 4) ^ (2 * (y // 4))


def pack_kernel(pos, mom, force, species, nbr, counts, ghost, out):
    raw = [jnp.concatenate([pos[c], mom[c] + 0.5 * force[c]], axis=1) for c in range(3)]
    kind = species[...].astype(F32)
    ghosts = ghost[0].astype(F32)
    last = jnp.concatenate([ghosts[0:1], ghosts[1:2], jnp.zeros((1, 96), F32)], axis=1)
    for bead in range(4):
        e = nbr[bead].astype(F32)
        rows = raw + [
            jnp.concatenate([e[0:1], e[1:2]], axis=1),
            jnp.concatenate([e[2:3], e[3:4]], axis=1),
            jnp.concatenate([counts[bead : bead + 1].astype(F32), kind], axis=1),
            last,
        ]
        block = jnp.concatenate(rows, axis=0)
        for r in range(4):
            for y in range(8):
                if pick(y) == bead:
                    out[r * 8 + y] = block


def modes_kernel(place, got, one, packed, own):
    r, side, local = place[0], place[1], place[2]
    low = lanes(8) < 64
    wide = jnp.concatenate(
        [jnp.concatenate([got[s * 8 + d] for s in range(4)], axis=0) for d in range(8)], axis=1
    )
    parts = exact(one[4 * r + local], wide)
    row = lax.broadcasted_iota(jnp.int32, (8, 128), 0)
    for t in range(4):
        info_even = got[r * 8 + 2 * t][8:16]
        info_odd = got[r * 8 + 2 * t + 1][8:16]
        left = jnp.where(low, info_even, turn(info_odd))
        right = jnp.where(low, turn(info_even), info_odd)
        kind = right[6:7]
        even, odd = parts[:, 256 * t : 256 * t + 128], parts[:, 256 * t + 128 : 256 * t + 256]
        cos_part = jnp.where(low, even[0:8], turn(odd[0:8]))
        drift_part = jnp.where(low, turn(even[8:16]), odd[8:16])
        coords = cos_part + drift_part / (1.0 + 15.0 * kind)
        packed[t, 0:8] = jnp.where(row == 3, jnp.broadcast_to(kind, (8, 128)), coords)
        packed[t, 8:12] = left[4:8]
        packed[t, 12:16] = right[4:8]
    own[...] = packed[pl.ds(2 * side, 2)]


def rates():
    row = lax.broadcasted_iota(jnp.int32, (8, 128), 0)
    rate = jnp.zeros((8, 128), F32)
    for n in range(8):
        rate = jnp.where(row == n, float(RATES[n]), rate)
    return rate


def sigmoid(v):
    return 1.0 / (1.0 + jnp.exp(-v))


def layer_one(pk, tiles, weights, hot, ys, gp, mom_one, slope_one, u_two):
    w_one_cat, mix1_t, prj_t, base_col, step_col = weights
    low = lanes(8) < 64
    low1 = lanes(1) < 64
    head = lanes(1) < 16
    rate = rates()
    spot = lax.broadcasted_iota(jnp.int32, (256, 128), 0).astype(F32)
    ghost_spot = lax.broadcasted_iota(jnp.int32, (32, 128), 0).astype(F32) + 64.0
    for t in tiles:
        here = pk[t + 1, 0:8]
        info = pk[t + 1, 8:16]
        beside = jnp.where(low, pk[t + 2, 0:8], pk[t, 0:8])
        wide = jnp.concatenate([here, beside], axis=1)
        a = wide.astype(BF16).astype(F32)
        b = (wide - a).astype(BF16).astype(F32)
        c = (wide - a - b).astype(BF16).astype(F32)
        parts = jnp.concatenate([a, b, c, jnp.zeros((8, 256), F32)], axis=0).astype(BF16)
        g_prev, g_here, g_next = pk[t, 11:12], info[3:4], pk[t + 2, 11:12]
        table = jnp.concatenate(
            [
                jnp.where(head, turn(g_prev) + 192.0, turn(g_here) + 64.0),
                jnp.where(head, g_here, g_next + 128.0),
                jnp.zeros((14, 128), F32),
            ],
            axis=0,
        )[:, 0:32].astype(BF16)
        count = info[2:3]
        sums = [None] * 9
        for k, row in enumerate((0, 4, 1, 5)):
            e = info[row : row + 1]
            hit = jnp.where(ghost_spot == e, 1.0, 0.0).astype(BF16)
            far = dot(table, hit)
            n = jnp.where(
                e < 64.0, e + jnp.where(low1, 0.0, 64.0), jnp.where(low1, far[0:1], far[1:2])
            )
            one_hot = jnp.where(spot == n, 1.0, 0.0).astype(BF16)
            hot[t, :, k * 128 : (k + 1) * 128] = one_hot
            got = dot(parts, one_hot)
            there = got[0:8] + (got[8:16] + got[16:24])
            off = there - here
            x, y, z = off[0:1], off[1:2], off[2:3]
            q = x * x + y * y + z * z
            live = jnp.where(count > float(k), 0.25, 0.0)
            g = jnp.exp(-rate * q) * live
            both = jnp.concatenate([g, g * there[3:4]], axis=0)
            harmonic = [
                None, x, y, z, ROOT3 * x * y, ROOT3 * y * z, 0.5 * (3.0 * z * z - q), ROOT3 * x * z,
                (0.5 * ROOT3) * (x * x - y * y),
            ]
            gp[t, k] = both
            ys[t, k] = jnp.concatenate(harmonic[1:9], axis=0)
            for l in range(9):
                term = both if l == 0 else harmonic[l] * both
                sums[l] = term if sums[l] is None else sums[l] + term
        high, lo = split(jnp.concatenate(sums, axis=1))
        moments = dot(w_one_cat, jnp.concatenate([high, lo, high], axis=0))
        m = [moments[:, l * 128 : (l + 1) * 128] for l in range(9)]
        for l in range(9):
            mom_one[t, l] = m[l]
        inv = jnp.concatenate(
            [m[0] * m[0], sum(m[l] * m[l] for l in (1, 2, 3)), sum(m[l] * m[l] for l in range(4, 9))],
            axis=0,
        )
        v = dot3(mix1_t, split(inv))
        sig = sigmoid(v)
        slope_one[t] = sig * (1.0 + v * (1.0 - sig))
        h = base_col + here[3:4] * step_col + v * sig
        u_two[t] = dot3(prj_t, split(h))


def forms_kernel(
    sent, one, four, embed, radial_one, radial_two, mix_one, mix_two, proj, readout,
    one_out, four_out, mix_back, mix_fwd, prj_all, columns, first_cat, first_parts, second_cat, second_parts,
):
    del sent

    def column(row):
        return jnp.broadcast_to(row, (128, 128)).T

    one_out[...] = one[...]
    four_out[...] = four[...]
    columns[0] = column(embed[0:1])
    columns[1] = column(embed[1:2] - embed[0:1])
    columns[2] = column(readout[1:2])
    columns[3] = column(readout[0:1] + readout[1:2])
    for n, mix in enumerate((mix_one, mix_two)):
        mix_back[2 * n], mix_back[2 * n + 1] = split(mix[...])
        mix_fwd[2 * n], mix_fwd[2 * n + 1] = split(mix[...].T)
    prj_all[0], prj_all[1] = split(proj[...])
    prj_all[2], prj_all[3] = split(proj[...].T)
    base, step = embed[0:1], embed[1:2] - embed[0:1]
    high, lo = split(jnp.concatenate([radial_one[...] * base, radial_one[...] * step], axis=0))
    first_parts[0], first_parts[1] = high, lo
    first_cat[...] = jnp.concatenate([high, high, lo], axis=0).astype(F32).T.astype(BF16)
    high, lo = split(radial_two[...])
    second_parts[0], second_parts[1] = high, lo
    high, lo = high.astype(F32), lo.astype(F32)
    second_cat[...] = jnp.concatenate([high, high, lo, jnp.zeros((8, 128), F32)], axis=0).T.astype(BF16)


def plane_kernel(
    place, packed, got, four, mix_fwd, prj_all, columns, first_cat,
    pos_out, mom_out, hot, ys, gp, mom_one, slope_one, u_two,
    pk,
):
    r, side, y = place[0], place[1], place[3]

    first = 2 * (1 - side)
    for t in range(2):
        pk[t] = packed[0]
        pk[6 + t] = packed[3]
    pk[pl.ds(first + 1, 4)] = packed[...]
    weights = (first_cat[...], (mix_fwd[0], mix_fwd[1]), (prj_all[2], prj_all[3]), columns[0], columns[1])
    start = 3 * (1 - side)
    layer_one(pk, [start + i for i in range(3)], weights, hot, ys, gp, mom_one, slope_one, u_two)

    own = exact(four[r], jnp.concatenate([got[s * 8 + y] for s in range(4)], axis=0))
    mass = 1.0 + 15.0 * turn(got[r * 8 + y][8:16])[6:7]
    coords = own[0:16] + turn(own[16:32]) / mass
    moment = turn(own[32:48]) - mass * own[48:64]
    for c in range(3):
        pos_out[c] = coords[4 * c : 4 * c + 4, 0:64]
        mom_out[c] = moment[4 * c : 4 * c + 4, 0:64]


def force_kernel(
    place, packed, across, hot_in, ys_in, gp_in, mom_in, slope_in, u_in, mix_back, mix_fwd, prj_all, columns,
    first_cat, first_parts, second_cat, second_parts,
    out, hot, ys, gp, mom_one, slope_one, u_two,
    pk, du_two, tk, gk, rk, v_one, v_two, dvec,
):
    side = place[1]
    low = lanes(8) < 64
    low1 = lanes(1) < 64
    low_wide = lanes(128) < 64
    first = 2 * (1 - side)
    other = 4 * side
    pk[0] = across[0]
    pk[7] = across[1]
    pk[pl.ds(first + 1, 4)] = packed[...]
    pk[pl.ds(other + 1, 2)] = across[...]
    w_one2 = (first_parts[0], first_parts[1])
    w_two2 = (second_parts[0], second_parts[1])
    w_two_cat = second_cat[...]
    weights = (first_cat[...], (mix_fwd[0], mix_fwd[1]), (prj_all[2], prj_all[3]), columns[0], columns[1])
    start = 3 * side
    layer_one(pk, [start + i for i in range(3)], weights, hot, ys, gp, mom_one, slope_one, u_two)
    rate = rates()
    pairs = [(i, j) for i in range(4) for j in range(i, 4)]

    du_two[...] = jnp.zeros_like(du_two)

    def second(t, _):
        near = u_two[t]
        beside = jnp.where(low_wide, u_two[t + 1], u_two[t - 1])
        high, lo = split(jnp.concatenate([near, beside], axis=1))
        parts = jnp.concatenate([high, lo], axis=0)
        for k in range(4):
            got = dot(parts, hot[t, :, k * 128 : (k + 1) * 128])
            nodes = got[0:128] + got[128:256]
            g = gp[t, k, 0:8]
            gh = g.astype(BF16).astype(F32)
            rows = jnp.concatenate([gh, g - gh, gh, jnp.zeros((8, 128), F32)], axis=0).astype(BF16)
            weight = dot(w_two_cat, rows)
            gk[k] = nodes
            rk[k] = weight
            tk[k] = nodes * weight
        edge = [[ys[t, k, c : c + 1] for c in range(3)] for k in range(4)]
        scalar = {}
        for i, j in pairs:
            scalar[i, j] = scalar[j, i] = sum(edge[i][c] * edge[j][c] for c in range(3))
        legendre = {}
        for i, j in pairs:
            legendre[i, j] = legendre[j, i] = 1.5 * scalar[i, j] * scalar[i, j] - 0.5 * scalar[i, i] * scalar[j, j]
        total = (tk[0] + tk[1]) + (tk[2] + tk[3])
        inv1 = inv2 = None
        for i in range(4):
            va = sum(scalar[i, j] * tk[j] for j in range(4))
            vb = sum(legendre[i, j] * tk[j] for j in range(4))
            v_one[i], v_two[i] = va, vb
            inv1 = va * tk[i] if inv1 is None else inv1 + va * tk[i]
            inv2 = vb * tk[i] if inv2 is None else inv2 + vb * tk[i]
        inv = jnp.concatenate([total * total, inv1, inv2], axis=0)
        v = dot3((mix_fwd[2], mix_fwd[3]), split(inv))
        sig = sigmoid(v)
        dv = columns[2] * (sig * (1.0 + v * (1.0 - sig)))
        dinv = 2.0 * dot3((mix_back[2], mix_back[3]), split(dv))
        d0, d1, d2 = dinv[0:128] * total, dinv[128:256], dinv[256:384]
        pull, bend = {}, {}
        for i in range(4):
            wa, wb = d1 * tk[i], d2 * tk[i]
            for j in range(i, 4):
                pull[i, j] = pull[j, i] = jnp.sum(wa * tk[j], axis=0, keepdims=True)
                bend[i, j] = bend[j, i] = jnp.sum(wb * tk[j], axis=0, keepdims=True)
        back = None
        for k in range(4):
            dt = d0 + d1 * v_one[k] + d2 * v_two[k]
            g = gp[t, k, 0:8]
            dg = dot3(w_two2, split(dt * gk[k]))
            dq = 0.5 * pull[k, k] + bend[k, k] * scalar[k, k] - jnp.sum(rate * g * dg, axis=0, keepdims=True)
            d = [None] * 3
            for j in range(4):
                if j != k:
                    dq = dq - 0.5 * bend[k, j] * scalar[j, j]
                    tie = pull[k, j] + 3.0 * bend[k, j] * scalar[k, j]
                    d = [tie * edge[j][c] if d[c] is None else d[c] + tie * edge[j][c] for c in range(3)]
            d = [d[c] + 2.0 * dq * edge[k][c] for c in range(3)]
            dvec[t, k] = jnp.concatenate(d + [jnp.zeros((5, 128), F32)], axis=0)
            high, lo = split(dt * rk[k])
            term = dot_t(jnp.concatenate([high, lo], axis=0), hot[t, :, k * 128 : (k + 1) * 128])
            back = term if back is None else back + term
        back = back[0:128] + back[128:256]
        du_two[t] += back[:, 0:128]
        aside = back[:, 128:256]
        du_two[t + 1] += jnp.where(low_wide, aside, 0.0)
        du_two[t - 1] += jnp.where(low_wide, 0.0, aside)
        return 0

    for t in range(1, TILES - 1):
        second(t, 0)

    def third(du, slope, mom, gs, harmonics, pushes, spots):
        dh = columns[3] + dot3((prj_all[0], prj_all[1]), split(du))
        dinv = 2.0 * dot3((mix_back[0], mix_back[1]), split(dh * slope))
        parts = []
        for l in range(9):
            part = 0 if l == 0 else 1 if l < 4 else 2
            parts.append(mom(l) * dinv[part * 128 : (part + 1) * 128])
        dm = dot3(w_one2, split(jnp.concatenate(parts, axis=1)))
        dm = [dm[:, l * 128 : (l + 1) * 128] for l in range(9)]
        rate2 = jnp.concatenate([rate, rate], axis=0)
        back = None
        centre = None
        for k in range(4):
            g, yk, push = gs(k), harmonics(k), pushes(k)
            dg = dm[0]
            dys = []
            for l in range(1, 9):
                dg = dg + yk[l - 1 : l] * dm[l]
                dys.append(jnp.sum(g * dm[l], axis=0, keepdims=True))
            dq = -jnp.sum(rate2 * g * dg, axis=0, keepdims=True)
            x, y, z = yk[0:1], yk[1:2], yk[2:3]
            e1, e2, e3, e4, e5, e6, e7, e8 = dys
            dx = e1 + ROOT3 * (y * e4 + z * e7 + x * e8) + x * (2.0 * dq - e6)
            dy = e2 + ROOT3 * (x * e4 + z * e5 - y * e8) + y * (2.0 * dq - e6)
            dz = e3 + ROOT3 * (y * e5 + x * e7) + 2.0 * z * (dq + e6)
            d = push + jnp.concatenate([dx, dy, dz, jnp.zeros((5, 128), F32)], axis=0)
            centre = d if centre is None else centre + d
            d_high = d.astype(BF16).astype(F32)
            rows = jnp.concatenate([d_high, d - d_high], axis=0).astype(BF16)
            term = dot_t(rows, spots(k))
            back = term if back is None else back + term
        return back[0:8] + back[8:16], centre

    def own_tile(t):
        return third(
            du_two[t], slope_one[t], lambda l: mom_one[t, l], lambda k: gp[t, k], lambda k: ys[t, k],
            lambda k: dvec[t, k], lambda k: hot[t, :, k * 128 : (k + 1) * 128],
        )

    def mixed(ref, *at):
        right, left = ref[(4,) + at], ref[(1,) + at]
        keep = lax.broadcasted_iota(jnp.int32, right.shape, 1) < 64
        return jnp.where(keep, right, left)

    def mixed_spots(k):
        at = (slice(128, 256), slice(k * 128, (k + 1) * 128))
        keep = lanes(128) < 64
        return jnp.where(keep, hot[(4,) + at].astype(F32), hot[(1,) + at].astype(F32)).astype(BF16)

    back2, centre2 = own_tile(2)
    back3, centre3 = own_tile(3)
    rim, _ = third(
        mixed(du_two), mixed(slope_one), lambda l: mixed(mom_one, l), lambda k: mixed(gp, k), lambda k: mixed(ys, k),
        lambda k: mixed(dvec, k), mixed_spots,
    )
    f2 = centre2 - back2[:, 0:128] - jnp.where(low, rim, back3[:, 128:256])
    f3 = centre3 - back3[:, 0:128] - jnp.where(low, back2[:, 128:256], rim)
    for t, f in enumerate((f2, f3)):
        out[2 * t] = f
        out[2 * t + 1] = turn(f)


def finish_kernel(place, got, mid, force_out, mom_out):
    side = place[1]
    for b in range(4):
        f = got[b ^ (2 * side)]
        for c in range(3):
            force_out[c, b : b + 1] = f[c : c + 1, 0:64]
    mom_out[...] = mid[...] + 0.5 * force_out[...]


def shape(*dims):
    return jax.ShapeDtypeStruct(dims, F32)


def room(mib):
    return pltpu.CompilerParams(vmem_limit_bytes=mib << 20)


def near(*dims, dtype=F32):
    return pltpu.VMEM(dims, dtype)


def far(x):
    return pltpu.with_memory_space_constraint(x, pltpu.HBM)


def keep(x):
    return pltpu.with_memory_space_constraint(x, pltpu.VMEM)


def on_device(
    positions, momenta, forces, species, neighbours, counts, ghost_rows,
    embed, radial_one, radial_two, mix_one, mix_two, projection, readout,
):
    count = lax.axis_size("space")
    r = lax.axis_index("bead")
    s = lax.axis_index("space")
    y = s & 7
    side = y >> 2
    place = jnp.stack([r, side, (y & 3) ^ (2 * side), y]).astype(jnp.int32)
    both = ("bead", "space")
    planes = [[b * count + z * 8 + i for b in range(4) for i in range(8)] for z in range(count // 8)]
    quads = [[b * count + h * 4 + i for i in range(4)] for b in range(4) for h in range(count // 4)]
    beside = []
    for b in range(4):
        for z in range(count // 8):
            for i in range(4):
                here = b * count + z * 8 + i
                back = b * count + (z * 8 - 4) % count + (i ^ 2)
                beside += [(here, back), (back, here)]

    turned = [jnp.transpose(x, (1, 0, 2)) for x in (positions, momenta, forces)]
    sent = pl.pallas_call(
        pack_kernel, out_shape=shape(32, 16, 128), in_specs=[VM] * 7, out_specs=VM, name="pack",
    )(*[far(x) for x in (*turned, species[None, :], neighbours, counts, ghost_rows)])
    got = keep(lax.all_to_all(sent, both, 0, 0, axis_index_groups=planes))
    one, four = mode_tables()
    one, four, *forms = pl.pallas_call(
        forms_kernel,
        out_shape=(
            near(BEADS, 16, 64), near(4, 64, 64), near(4, 384, 128, dtype=BF16), near(4, 128, 384, dtype=BF16),
            near(4, 128, 128, dtype=BF16), near(4, 128, 128), near(128, 48, dtype=BF16),
            near(2, 16, 128, dtype=BF16), near(128, 32, dtype=BF16), near(2, 8, 128, dtype=BF16),
        ),
        in_specs=[pl.BlockSpec(memory_space=pl.ANY)] + [VM] * 9,
        out_specs=(VM,) * 10,
        compiler_params=room(8),
        cost_estimate=pl.CostEstimate(flops=2_000_000_000, bytes_accessed=4_000_000, transcendentals=0),
        name="forms",
    )(*[far(x) for x in (
        sent, jnp.asarray(one), jnp.asarray(four), embed, radial_one, radial_two, mix_one, mix_two, projection, readout,
    )])
    mix_back, mix_fwd, prj_all, columns, first_cat, first_parts, second_cat, second_parts = forms
    packed, own = pl.pallas_call(
        modes_kernel,
        out_shape=(near(4, 16, 128), near(2, 16, 128)),
        in_specs=[SM] + [VM] * 2,
        out_specs=(VM,) * 2,
        compiler_params=room(16),
        name="modes",
    )(place, got, one)
    across = keep(lax.ppermute(own, both, beside))
    saved = (
        near(TILES, 256, 512, dtype=BF16),
        near(TILES, 4, 8, 128),
        near(TILES, 4, 16, 128),
        near(TILES, 9, 128, 128),
        near(TILES, 128, 128),
        near(TILES, 128, 128),
    )
    res = pl.pallas_call(
        plane_kernel,
        out_shape=(shape(3, 4, 64), near(3, 4, 64)) + saved,
        in_specs=[SM] + [VM] * 7,
        out_specs=(VM,) * 8,
        scratch_shapes=[near(8, 16, 128)],
        compiler_params=room(24),
        cost_estimate=pl.CostEstimate(flops=4_000_000_000, bytes_accessed=8_000_000, transcendentals=0),
        name="plane",
    )(place, packed, got, four, mix_fwd, prj_all, columns, first_cat)
    positions_next, mid, kept = res[0], res[1], res[2:8]
    grad = pl.pallas_call(
        force_kernel,
        out_shape=(near(4, 8, 128),) + saved,
        in_specs=[SM] + [VM] * 16,
        out_specs=(VM,) * 7,
        scratch_shapes=[
            near(8, 16, 128),
            near(TILES, 128, 128),
            near(4, 128, 128),
            near(4, 128, 128),
            near(4, 128, 128),
            near(4, 128, 128),
            near(4, 128, 128),
            near(TILES, 4, 8, 128),
        ],
        input_output_aliases={3 + i: 1 + i for i in range(6)},
        compiler_params=room(24), name="force",
    )(place, packed, across, *kept, *forms)[0]
    back = keep(lax.all_to_all(grad, both, 0, 0, axis_index_groups=quads))
    forces_next, momenta_next = pl.pallas_call(
        finish_kernel,
        out_shape=(shape(3, 4, 64), shape(3, 4, 64)),
        in_specs=[SM] + [VM] * 2,
        out_specs=(VM, VM),
        compiler_params=room(8), name="finish",
    )(place, back, mid)
    return tuple(jnp.transpose(x, (1, 0, 2)) for x in (positions_next, momenta_next, forces_next))


def solution(mesh):
    spread = P("bead", None, "space")
    placed = (
        spread, spread, spread, P("space"), spread, P("bead", "space"), P("space", None, None),
    ) + (P(),) * 7
    return jax.shard_map(
        on_device, mesh=mesh, in_specs=placed, out_specs=(spread,) * 3, check_vma=False
    )
```

```python
import numpy as np

import jax
import jax.numpy as jnp
from jax import lax
from jax.experimental import pallas as pl
from jax.experimental.pallas import tpu as pltpu
from jax.sharding import PartitionSpec as P


F32 = jnp.float32
BF16 = jnp.bfloat16
BEADS = 16
TILES = 6
ROOT3 = float(np.sqrt(3.0))
VM = pl.BlockSpec(memory_space=pltpu.VMEM)
RATES = 0.25 * 16.0 ** (np.arange(8) / 7.0)


def propagators():
    n = BEADS
    b = np.arange(n)
    phase = 2.0 * np.pi * np.outer(b, b) / n
    matrix = np.where(b[None] < n // 2, np.cos(phase), np.sin(phase)) * np.sqrt(2.0 / n)
    matrix[:, n // 2] = np.where(b % 2 == 0, 1.0, -1.0) / np.sqrt(n)
    matrix[:, 0] = 1.0 / np.sqrt(n)
    w = 1.5 * np.sin(np.pi * b / n)
    drift = np.where(b == 0, 1.0, np.sin(w) / np.where(b == 0, 1.0, w))
    return [(matrix * d) @ matrix.T for d in (np.cos(w), drift, w * np.sin(w))]


def mode_tables():
    cosine, drift, stiff = propagators()
    rows = np.zeros((4, 4, 64, 16))
    for sender in range(4):
        for bead in range(BEADS):
            for c in range(3):
                for b in range(4):
                    for n, values in enumerate((cosine, drift, cosine, stiff)):
                        rows[sender, n, 4 * bead + c, 4 * c + b] = values[bead, 4 * sender + b]
    rows = rows.astype(np.float32).reshape(4, 2, 128, 16)
    one = rows.astype(BF16)
    two = (rows - one.astype(np.float32)).astype(BF16)
    three = (rows - one.astype(np.float32) - two.astype(np.float32)).astype(BF16)
    return np.concatenate([one, one, two, two, one, three], axis=-1)


def parts_of(x):
    one = x.astype(BF16)
    rest = x - one.astype(F32)
    two = rest.astype(BF16)
    three = (rest - two.astype(F32)).astype(BF16)
    return jnp.concatenate([one, two, one, two, three, one], axis=0)

def split(x):
    high = x.astype(BF16)
    return high, (x - high.astype(F32)).astype(BF16)


def dot(a, b):
    return lax.dot_general(a, b, (((1,), (0,)), ((), ())), preferred_element_type=F32)


def dot_t(a, b):
    return lax.dot_general(a, b, (((1,), (1,)), ((), ())), preferred_element_type=F32)


def dot3(a, b):
    return dot(a[0], b[0]) + (dot(a[0], b[1]) + dot(a[1], b[0]))


def lanes(rows):
    return lax.broadcasted_iota(jnp.int32, (rows, 128), 1)


def turn(x):
    return pltpu.roll(x, 64, 1)


def pick(y):
    return (y % 4) ^ (2 * (y // 4))


def whereabouts():
    s = lax.axis_index("space")
    return lax.axis_index("bead"), (s & 7) >> 2, s


def pack_kernel(table, pos, mom, force, species, nbr, counts, ghost, out):
    r, _, _ = whereabouts()
    low = lanes(64) < 64
    kind = species[...].astype(F32)
    mass = 1.0 + 15.0 * kind
    blank = jnp.zeros((4, 64), F32)
    coords = jnp.concatenate([pos[0], pos[1], pos[2], blank], axis=0)
    kicked = jnp.concatenate([mom[c] + 0.5 * force[c] for c in range(3)] + [blank], axis=0)
    moved = dot(table[r, 0], parts_of(jnp.concatenate([coords, kicked / mass], axis=1)))
    driven = dot(table[r, 1], parts_of(jnp.concatenate([mass * coords, kicked], axis=1)))
    shares = jnp.where(low, moved[0:64] + turn(moved[64:128]), driven[0:64] - turn(driven[64:128]))
    ghosts = ghost[0].astype(F32)
    last = jnp.concatenate([ghosts[0:1], ghosts[1:2], jnp.zeros((1, 96), F32)], axis=1)
    row = lax.broadcasted_iota(jnp.int32, (8, 128), 0)
    for bead in range(4):
        e = nbr[bead].astype(F32)
        info = jnp.concatenate(
            [
                jnp.zeros((3, 128), F32),
                jnp.concatenate([counts[bead : bead + 1].astype(F32), kind], axis=1),
                jnp.concatenate([e[0:1], e[1:2]], axis=1),
                jnp.concatenate([e[2:3], e[3:4]], axis=1),
                last,
                jnp.zeros((1, 128), F32),
            ],
            axis=0,
        )
        for to in range(4):
            n = (4 * to + bead) // 2
            share = shares[8 * n : 8 * n + 8]
            if bead % 2:
                share = pltpu.roll(share, 4, 0)
            block = jnp.where(row < 3, share, info)
            for y in range(8):
                if pick(y) == bead:
                    out[to * 8 + y] = block


def modes_kernel(got, packed, own, moment):
    r, side, _ = whereabouts()
    low = lanes(8) < 64
    row = lax.broadcasted_iota(jnp.int32, (8, 128), 0)
    moments = []
    for t in range(4):
        even, odd = (
            (got[d] + got[8 + d]) + (got[16 + d] + got[24 + d]) for d in (2 * t, 2 * t + 1)
        )
        info_even, info_odd = got[r * 8 + 2 * t], got[r * 8 + 2 * t + 1]
        left = jnp.where(low, info_even, turn(info_odd))
        right = jnp.where(low, turn(info_even), info_odd)
        coords = jnp.where(low, even, turn(odd))
        moments.append(jnp.where(low, turn(even), odd))
        packed[t, 0:8] = jnp.where(row < 3, coords, jnp.broadcast_to(right[3:4], (8, 128)))
        packed[t, 8:16] = jnp.where(row < 3, pltpu.roll(right, 5, 0), left)
    for t in range(2):
        moment[t] = jnp.where(side == 1, moments[2 + t], moments[t])
    own[...] = packed[pl.ds(2 * side, 2)]


ORDER = ((0, 0), (0, 1), (1, 0), (2, 0), (0, 2), (1, 1), (2, 1), (3, 0), (1, 2), (2, 2), (3, 1), (3, 2))


def rates():
    row = lax.broadcasted_iota(jnp.int32, (8, 128), 0)
    rate = jnp.zeros((8, 128), F32)
    for n in range(8):
        rate = jnp.where(row == n, float(RATES[n]), rate)
    return rate


def sigmoid(v):
    return 1.0 / (1.0 + jnp.exp(-v))


def layer_one(pk, tiles, weights, hot, ys, gp, mom_one, slope_one, u_two):
    w_one_cat, mix1_t, prj_t, base_col, step_col = weights
    low = lanes(8) < 64
    low1 = lanes(1) < 64
    head = lanes(1) < 16
    rate = rates()
    spot = lax.broadcasted_iota(jnp.int32, (256, 128), 0).astype(F32)
    ghost_spot = lax.broadcasted_iota(jnp.int32, (32, 128), 0).astype(F32) + 64.0
    for t in tiles:
        here = pk[t + 1, 0:8]
        info = pk[t + 1, 8:16]
        beside = jnp.where(low, pk[t + 2, 0:8], pk[t, 0:8])
        wide = jnp.concatenate([here, beside], axis=1)
        a = wide.astype(BF16).astype(F32)
        b = (wide - a).astype(BF16).astype(F32)
        c = (wide - a - b).astype(BF16).astype(F32)
        parts = jnp.concatenate([a, b, c, jnp.zeros((8, 256), F32)], axis=0).astype(BF16)
        g_prev, g_here, g_next = pk[t, 14:15], info[6:7], pk[t + 2, 14:15]
        table = jnp.concatenate(
            [
                jnp.where(head, turn(g_prev) + 192.0, turn(g_here) + 64.0),
                jnp.where(head, g_here, g_next + 128.0),
                jnp.zeros((14, 128), F32),
            ],
            axis=0,
        )[:, 0:32].astype(BF16)
        count = info[3:4]
        sums = [None] * 9
        for k, row in enumerate((4, 1, 5, 2)):
            e = info[row : row + 1]
            hit = jnp.where(ghost_spot == e, 1.0, 0.0).astype(BF16)
            far = dot(table, hit)
            n = jnp.where(
                e < 64.0, e + jnp.where(low1, 0.0, 64.0), jnp.where(low1, far[0:1], far[1:2])
            )
            one_hot = jnp.where(spot == n, 1.0, 0.0).astype(BF16)
            hot[t, :, k * 128 : (k + 1) * 128] = one_hot
            got = dot(parts, one_hot)
            there = got[0:8] + (got[8:16] + got[16:24])
            off = there - here
            x, y, z = off[0:1], off[1:2], off[2:3]
            q = x * x + y * y + z * z
            live = jnp.where(count > float(k), 0.25, 0.0)
            g = jnp.exp(-rate * q) * live
            both = jnp.concatenate([g, g * there[3:4]], axis=0)
            harmonic = [
                None, x, y, z, ROOT3 * x * y, ROOT3 * y * z, 0.5 * (3.0 * z * z - q), ROOT3 * x * z,
                (0.5 * ROOT3) * (x * x - y * y),
            ]
            gp[t, k] = both
            ys[t, k] = jnp.concatenate(harmonic[1:9], axis=0)
            for l in range(9):
                term = both if l == 0 else harmonic[l] * both
                sums[l] = term if sums[l] is None else sums[l] + term
        high, lo = split(jnp.concatenate(sums, axis=1))
        moments = dot(w_one_cat, jnp.concatenate([high, lo, high], axis=0))
        m = [moments[:, l * 128 : (l + 1) * 128] for l in range(9)]
        for l in range(9):
            mom_one[t, l] = m[l]
        inv = jnp.concatenate(
            [m[0] * m[0], sum(m[l] * m[l] for l in (1, 2, 3)), sum(m[l] * m[l] for l in range(4, 9))],
            axis=0,
        )
        v = dot3(mix1_t, split(inv))
        sig = sigmoid(v)
        slope_one[t] = sig * (1.0 + v * (1.0 - sig))
        h = base_col + here[3:4] * step_col + v * sig
        u_two[t] = dot3(prj_t, split(h))


def forms_kernel(
    sent, embed, radial_one, radial_two, mix_one, mix_two, proj, readout,
    mix_back, mix_fwd, prj_all, columns, first_cat, first_parts, second_cat, second_parts,
):
    del sent

    def column(row):
        return jnp.broadcast_to(row, (128, 128)).T

    columns[0] = column(embed[0:1])
    columns[1] = column(embed[1:2] - embed[0:1])
    columns[2] = column(readout[1:2])
    columns[3] = column(readout[0:1] + readout[1:2])
    for n, mix in enumerate((mix_one, mix_two)):
        mix_back[2 * n], mix_back[2 * n + 1] = split(mix[...])
        mix_fwd[2 * n], mix_fwd[2 * n + 1] = split(mix[...].T)
    prj_all[0], prj_all[1] = split(proj[...])
    prj_all[2], prj_all[3] = split(proj[...].T)
    base, step = embed[0:1], embed[1:2] - embed[0:1]
    high, lo = split(jnp.concatenate([radial_one[...] * base, radial_one[...] * step], axis=0))
    first_parts[0], first_parts[1] = high, lo
    first_cat[...] = jnp.concatenate([high, high, lo], axis=0).astype(F32).T.astype(BF16)
    high, lo = split(radial_two[...])
    second_parts[0], second_parts[1] = high, lo
    high, lo = high.astype(F32), lo.astype(F32)
    second_cat[...] = jnp.concatenate([high, high, lo, jnp.zeros((8, 128), F32)], axis=0).T.astype(BF16)


def nodes_of_edges(t, m, hot, gp, u_two, second_cat, tk, gk, rk):
    low_wide = lanes(128) < 64
    beside = jnp.where(low_wide, u_two[t + 1], u_two[t - 1])
    high, lo = split(jnp.concatenate([u_two[t], beside], axis=1))
    parts = jnp.concatenate([high, lo], axis=0)
    for k in range(4):
        got = dot(parts, hot[t, :, k * 128 : (k + 1) * 128])
        nodes = got[0:128] + got[128:256]
        g = gp[t, k, 0:8]
        gh = g.astype(BF16).astype(F32)
        rows = jnp.concatenate([gh, g - gh, gh, jnp.zeros((8, 128), F32)], axis=0).astype(BF16)
        weight = dot(second_cat[...], rows)
        gk[m, k] = nodes
        rk[m, k] = weight
        tk[m, k] = nodes * weight


def edge_sums(t, ys):
    edge = [[ys[t, k, c : c + 1] for c in range(3)] for k in range(4)]
    scalar, legendre = {}, {}
    for i in range(4):
        for j in range(i, 4):
            scalar[i, j] = scalar[j, i] = sum(edge[i][c] * edge[j][c] for c in range(3))
    for i in range(4):
        for j in range(i, 4):
            legendre[i, j] = legendre[j, i] = 1.5 * scalar[i, j] * scalar[i, j] - 0.5 * scalar[i, i] * scalar[j, j]
    return edge, scalar, legendre


def invariants_two(t, m, ys, tk, v_one, v_two):
    _, scalar, legendre = edge_sums(t, ys)
    total = (tk[m, 0] + tk[m, 1]) + (tk[m, 2] + tk[m, 3])
    inv1 = inv2 = None
    for i in range(4):
        va = sum(scalar[i, j] * tk[m, j] for j in range(4))
        vb = sum(legendre[i, j] * tk[m, j] for j in range(4))
        v_one[m, i], v_two[m, i] = va, vb
        inv1 = va * tk[m, i] if inv1 is None else inv1 + va * tk[m, i]
        inv2 = vb * tk[m, i] if inv2 is None else inv2 + vb * tk[m, i]
    return split(jnp.concatenate([total * total, inv1, inv2], axis=0))


def mixing_back(m, inv, mix_back, mix_fwd, columns, dinv):
    v = dot3((mix_fwd[2], mix_fwd[3]), inv)
    sig = sigmoid(v)
    dv = columns[2] * (sig * (1.0 + v * (1.0 - sig)))
    dinv[m] = 2.0 * dot3((mix_back[2], mix_back[3]), split(dv))


def edges_back(t, m, hot, ys, gp, second_parts, tk, gk, rk, v_one, v_two, dinv, du_two, dvec):
    low_wide = lanes(128) < 64
    edge, scalar, _ = edge_sums(t, ys)
    rate = rates()
    w_two2 = (second_parts[0], second_parts[1])
    d1, d2 = dinv[m, 128:256], dinv[m, 256:384]
    d0 = dinv[m, 0:128] * ((tk[m, 0] + tk[m, 1]) + (tk[m, 2] + tk[m, 3]))
    pull, bend = {}, {}
    for i in range(4):
        wa, wb = d1 * tk[m, i], d2 * tk[m, i]
        for j in range(i, 4):
            pull[i, j] = pull[j, i] = jnp.sum(wa * tk[m, j], axis=0, keepdims=True)
            bend[i, j] = bend[j, i] = jnp.sum(wb * tk[m, j], axis=0, keepdims=True)
    back = None
    for k in range(4):
        dt = d0 + d1 * v_one[m, k] + d2 * v_two[m, k]
        dg = dot3(w_two2, split(dt * gk[m, k]))
        high, lo = split(dt * rk[m, k])
        term = dot_t(jnp.concatenate([high, lo], axis=0), hot[t, :, k * 128 : (k + 1) * 128])
        back = term if back is None else back + term
        dq = 0.5 * pull[k, k] + bend[k, k] * scalar[k, k] - jnp.sum(rate * gp[t, k, 0:8] * dg, axis=0, keepdims=True)
        d = [None] * 3
        for j in range(4):
            if j != k:
                dq = dq - 0.5 * bend[k, j] * scalar[j, j]
                tie = pull[k, j] + 3.0 * bend[k, j] * scalar[k, j]
                d = [tie * edge[j][c] if d[c] is None else d[c] + tie * edge[j][c] for c in range(3)]
        d = [d[c] + 2.0 * dq * edge[k][c] for c in range(3)]
        dvec[t, k] = jnp.concatenate(d + [jnp.zeros((5, 128), F32)], axis=0)
    back = back[0:128] + back[128:256]
    du_two[t] += back[:, 0:128]
    aside = back[:, 128:256]
    du_two[t + 1] += jnp.where(low_wide, aside, 0.0)
    du_two[t - 1] += jnp.where(low_wide, 0.0, aside)


def plane_work(
    packed, forms, hot, ys, gp, mom_one, slope_one, u_two, du_two, dvec,
    pk, tk, gk, rk, v_one, v_two, dinv,
):
    mix_back, mix_fwd, prj_all, columns, first_cat, first_parts, second_cat, second_parts = forms
    _, side, _ = whereabouts()
    first = 2 * (1 - side)
    for t in range(2):
        pk[t] = packed[0]
        pk[6 + t] = packed[3]
    pk[pl.ds(first + 1, 4)] = packed[...]
    weights = (first_cat[...], (mix_fwd[0], mix_fwd[1]), (prj_all[2], prj_all[3]), columns[0], columns[1])
    start = 3 * (1 - side)
    layer_one(pk, [start + i for i in range(3)], weights, hot, ys, gp, mom_one, slope_one, u_two)

    du_two[...] = jnp.zeros_like(du_two)
    t = start + 1
    nodes_of_edges(t, 0, hot, gp, u_two, second_cat, tk, gk, rk)
    inv = invariants_two(t, 0, ys, tk, v_one, v_two)
    mixing_back(0, inv, mix_back, mix_fwd, columns, dinv)
    edges_back(t, 0, hot, ys, gp, second_parts, tk, gk, rk, v_one, v_two, dinv, du_two, dvec)


def is_early(s):
    return s < 4


def early_kernel(packed, *refs):
    forms, rest = refs[0:8], refs[10:]

    @pl.when(is_early(whereabouts()[2]))
    def _():
        plane_work(packed, forms, *rest)


def late_kernel(packed, *refs):
    forms, rest = refs[0:8], refs[16:]

    @pl.when(jnp.logical_not(is_early(whereabouts()[2])))
    def _():
        plane_work(packed, forms, *rest)


def force_kernel(packed, across, moment, *refs):
    mix_back, mix_fwd, prj_all, columns, first_cat, first_parts, second_cat, second_parts = refs[0:8]
    out, hot, ys, gp, mom_one, slope_one, u_two, du_two, dvec, pk, tk, gk, rk, v_one, v_two, dinv = refs[16:]
    _, side, _ = whereabouts()
    low = lanes(8) < 64
    first = 2 * (1 - side)
    other = 4 * side
    pk[0] = across[0]
    pk[7] = across[1]
    pk[pl.ds(first + 1, 4)] = packed[...]
    pk[pl.ds(other + 1, 2)] = across[...]
    w_one2 = (first_parts[0], first_parts[1])
    weights = (first_cat[...], (mix_fwd[0], mix_fwd[1]), (prj_all[2], prj_all[3]), columns[0], columns[1])
    start = 3 * side
    layer_one(pk, [start + i for i in range(3)], weights, hot, ys, gp, mom_one, slope_one, u_two)
    rate = rates()

    turns = [side + 1 + i for i in range(3)]
    inv = {}

    def stage(n, m):
        t = turns[m]
        if n == 0:
            nodes_of_edges(t, m, hot, gp, u_two, second_cat, tk, gk, rk)
        elif n == 1:
            inv[m] = invariants_two(t, m, ys, tk, v_one, v_two)
        elif n == 2:
            mixing_back(m, inv[m], mix_back, mix_fwd, columns, dinv)
        else:
            edges_back(t, m, hot, ys, gp, second_parts, tk, gk, rk, v_one, v_two, dinv, du_two, dvec)

    for n, m in ORDER:
        stage(n, m)

    def third(du, slope, mom, gs, harmonics, pushes, spots):
        dh = columns[3] + dot3((prj_all[0], prj_all[1]), split(du))
        dinv = 2.0 * dot3((mix_back[0], mix_back[1]), split(dh * slope))
        parts = []
        for l in range(9):
            part = 0 if l == 0 else 1 if l < 4 else 2
            parts.append(mom(l) * dinv[part * 128 : (part + 1) * 128])
        dm = dot3(w_one2, split(jnp.concatenate(parts, axis=1)))
        dm = [dm[:, l * 128 : (l + 1) * 128] for l in range(9)]
        rate2 = jnp.concatenate([rate, rate], axis=0)
        back = None
        centre = None
        for k in range(4):
            g, yk, push = gs(k), harmonics(k), pushes(k)
            dg = dm[0]
            dys = []
            for l in range(1, 9):
                dg = dg + yk[l - 1 : l] * dm[l]
                dys.append(jnp.sum(g * dm[l], axis=0, keepdims=True))
            dq = -jnp.sum(rate2 * g * dg, axis=0, keepdims=True)
            x, y, z = yk[0:1], yk[1:2], yk[2:3]
            e1, e2, e3, e4, e5, e6, e7, e8 = dys
            dx = e1 + ROOT3 * (y * e4 + z * e7 + x * e8) + x * (2.0 * dq - e6)
            dy = e2 + ROOT3 * (x * e4 + z * e5 - y * e8) + y * (2.0 * dq - e6)
            dz = e3 + ROOT3 * (y * e5 + x * e7) + 2.0 * z * (dq + e6)
            d = push + jnp.concatenate([dx, dy, dz, jnp.zeros((5, 128), F32)], axis=0)
            centre = d if centre is None else centre + d
            d_high = d.astype(BF16).astype(F32)
            rows = jnp.concatenate([d_high, d - d_high], axis=0).astype(BF16)
            term = dot_t(rows, spots(k))
            back = term if back is None else back + term
        return back[0:8] + back[8:16], centre

    def own_tile(t):
        return third(
            du_two[t], slope_one[t], lambda l: mom_one[t, l], lambda k: gp[t, k], lambda k: ys[t, k],
            lambda k: dvec[t, k], lambda k: hot[t, :, k * 128 : (k + 1) * 128],
        )

    def mixed(ref, *at):
        right, left = ref[(4,) + at], ref[(1,) + at]
        keep = lax.broadcasted_iota(jnp.int32, right.shape, 1) < 64
        return jnp.where(keep, right, left)

    def mixed_spots(k):
        at = (slice(128, 256), slice(k * 128, (k + 1) * 128))
        keep = lanes(128) < 64
        return jnp.where(keep, hot[(4,) + at].astype(F32), hot[(1,) + at].astype(F32)).astype(BF16)

    back2, centre2 = own_tile(2)
    back3, centre3 = own_tile(3)
    rim, _ = third(
        mixed(du_two), mixed(slope_one), lambda l: mixed(mom_one, l), lambda k: mixed(gp, k), lambda k: mixed(ys, k),
        lambda k: mixed(dvec, k), mixed_spots,
    )
    f2 = centre2 - back2[:, 0:128] - jnp.where(low, rim, back3[:, 128:256])
    f3 = centre3 - back3[:, 0:128] - jnp.where(low, back2[:, 128:256], rim)
    row = lax.broadcasted_iota(jnp.int32, (8, 128), 0)
    for t, f in enumerate((f2, f3)):
        coords, drift = pk[t + 3, 0:8], pltpu.roll(moment[t], 3, 0)
        out[2 * t] = jnp.where(row < 3, jnp.where(low, f, turn(coords)), drift)
        out[2 * t + 1] = jnp.where(row < 3, jnp.where(low, turn(f), coords), turn(drift))


def finish_kernel(got, pos_out, mom_out, force_out):
    _, side, _ = whereabouts()
    for b in range(4):
        block = got[b ^ (2 * side)]
        turned = turn(block)
        for c in range(3):
            force = block[c : c + 1, 0:64]
            pos_out[c, b : b + 1] = turned[c : c + 1, 0:64]
            mom_out[c, b : b + 1] = block[3 + c : 4 + c, 0:64] + 0.5 * force
            force_out[c, b : b + 1] = force


def shape(*dims):
    return jax.ShapeDtypeStruct(dims, F32)


def room(mib):
    return pltpu.CompilerParams(vmem_limit_bytes=mib << 20)


def near(*dims, dtype=F32):
    return pltpu.VMEM(dims, dtype)


def far(x):
    return pltpu.with_memory_space_constraint(x, pltpu.HBM)


def keep(x):
    return pltpu.with_memory_space_constraint(x, pltpu.VMEM)


def on_device(
    positions, momenta, forces, species, neighbours, counts, ghost_rows,
    embed, radial_one, radial_two, mix_one, mix_two, projection, readout,
):
    count = lax.axis_size("space")
    both = ("bead", "space")
    planes = [[b * count + z * 8 + i for b in range(4) for i in range(8)] for z in range(count // 8)]
    quads = [[b * count + h * 4 + i for i in range(4)] for b in range(4) for h in range(count // 4)]
    beside = []
    for b in range(4):
        for z in range(count // 8):
            for i in range(4):
                here = b * count + z * 8 + i
                back = b * count + (z * 8 - 4) % count + (i ^ 2)
                beside += [(here, back), (back, here)]

    turned = [jnp.transpose(x, (1, 0, 2)) for x in (positions, momenta, forces)]
    sent = pl.pallas_call(
        pack_kernel, out_shape=shape(32, 8, 128), in_specs=[VM] * 8, out_specs=VM, name="pack",
    )(*[far(x) for x in (jnp.asarray(mode_tables()), *turned, species[None, :], neighbours, counts, ghost_rows)])
    got = keep(lax.all_to_all(sent, both, 0, 0, axis_index_groups=planes))
    forms = pl.pallas_call(
        forms_kernel,
        out_shape=(
            near(4, 384, 128, dtype=BF16), near(4, 128, 384, dtype=BF16),
            near(4, 128, 128, dtype=BF16), near(4, 128, 128), near(128, 48, dtype=BF16),
            near(2, 16, 128, dtype=BF16), near(128, 32, dtype=BF16), near(2, 8, 128, dtype=BF16),
        ),
        in_specs=[pl.BlockSpec(memory_space=pl.ANY)] + [VM] * 7,
        out_specs=(VM,) * 8,
        compiler_params=room(8),
        cost_estimate=pl.CostEstimate(flops=2_000_000_000, bytes_accessed=4_000_000, transcendentals=0),
        name="forms",
    )(*[far(x) for x in (sent, embed, radial_one, radial_two, mix_one, mix_two, projection, readout)])
    packed, own, moment = pl.pallas_call(
        modes_kernel,
        out_shape=(near(4, 16, 128), near(2, 16, 128), near(2, 8, 128)),
        in_specs=[VM],
        out_specs=(VM,) * 3,
        compiler_params=room(16),
        name="modes",
    )(got)
    kept = (
        near(TILES, 256, 512, dtype=BF16),
        near(TILES, 4, 8, 128),
        near(TILES, 4, 16, 128),
        near(TILES, 9, 128, 128),
        near(TILES, 128, 128),
        near(TILES, 128, 128),
        near(TILES, 128, 128),
        near(TILES, 4, 8, 128),
    )

    def scratch(n):
        return [near(8, 16, 128)] + [near(n, 4, 128, 128)] * 5 + [near(n, 384, 128)]

    own, *state = pl.pallas_call(
        early_kernel,
        out_shape=(near(2, 16, 128),) + kept,
        in_specs=[VM] * 10,
        out_specs=(VM,) * 9,
        scratch_shapes=scratch(1),
        input_output_aliases={9: 0},
        compiler_params=room(24),
        name="early",
    )(packed, *forms, own)
    across = keep(lax.ppermute(own, both, beside))
    state = pl.pallas_call(
        late_kernel,
        out_shape=kept,
        in_specs=[VM] * 17,
        out_specs=(VM,) * 8,
        scratch_shapes=scratch(1),
        input_output_aliases={9 + i: i for i in range(8)},
        compiler_params=room(24),
        cost_estimate=pl.CostEstimate(flops=4_000_000_000, bytes_accessed=8_000_000, transcendentals=0),
        name="late",
    )(packed, *forms, *state)
    grad = pl.pallas_call(
        force_kernel,
        out_shape=(near(4, 8, 128),) + kept,
        in_specs=[VM] * 19,
        out_specs=(VM,) * 9,
        scratch_shapes=scratch(3),
        input_output_aliases={11 + i: 1 + i for i in range(8)},
        compiler_params=room(24),
        name="force",
    )(packed, across, moment, *forms, *state)[0]
    back = keep(lax.all_to_all(grad, both, 0, 0, axis_index_groups=quads))
    outs = pl.pallas_call(
        finish_kernel,
        out_shape=(shape(3, 4, 64),) * 3,
        in_specs=[VM],
        out_specs=(VM,) * 3,
        compiler_params=room(8),
        name="finish",
    )(back)
    return tuple(jnp.transpose(x, (1, 0, 2)) for x in outs)


def solution(mesh):
    spread = P("bead", None, "space")
    placed = (
        spread, spread, spread, P("space"), spread, P("bead", "space"), P("space", None, None),
    ) + (P(),) * 7
    return jax.shard_map(
        on_device, mesh=mesh, in_specs=placed, out_specs=(spread,) * 3, check_vma=False
    )
```

```python
import numpy as np

import jax
import jax.numpy as jnp
from jax import lax
from jax.experimental import pallas as pl
from jax.experimental.pallas import tpu as pltpu
from jax.sharding import PartitionSpec as P


F32 = jnp.float32
BF16 = jnp.bfloat16
BEADS = 16
TILES = 6
ROOT3 = float(np.sqrt(3.0))
VM = pl.BlockSpec(memory_space=pltpu.VMEM)
RATES = 0.25 * 16.0 ** (np.arange(8) / 7.0)


def propagators():
    n = BEADS
    b = np.arange(n)
    phase = 2.0 * np.pi * np.outer(b, b) / n
    matrix = np.where(b[None] < n // 2, np.cos(phase), np.sin(phase)) * np.sqrt(2.0 / n)
    matrix[:, n // 2] = np.where(b % 2 == 0, 1.0, -1.0) / np.sqrt(n)
    matrix[:, 0] = 1.0 / np.sqrt(n)
    w = 1.5 * np.sin(np.pi * b / n)
    drift = np.where(b == 0, 1.0, np.sin(w) / np.where(b == 0, 1.0, w))
    return [(matrix * d) @ matrix.T for d in (np.cos(w), drift, w * np.sin(w))]


def mode_tables():
    cosine, drift, stiff = propagators()
    rows = np.zeros((4, 4, 64, 16))
    for sender in range(4):
        for bead in range(BEADS):
            for c in range(3):
                for b in range(4):
                    for n, values in enumerate((cosine, drift, cosine, stiff)):
                        rows[sender, n, 4 * bead + c, 4 * c + b] = values[bead, 4 * sender + b]
    rows = rows.astype(np.float32).reshape(4, 2, 128, 16)
    one = rows.astype(BF16)
    two = (rows - one.astype(np.float32)).astype(BF16)
    three = (rows - one.astype(np.float32) - two.astype(np.float32)).astype(BF16)
    return np.concatenate([one, one, two, two, one, three], axis=-1)


def parts_of(x):
    one = x.astype(BF16)
    rest = x - one.astype(F32)
    two = rest.astype(BF16)
    three = (rest - two.astype(F32)).astype(BF16)
    return jnp.concatenate([one, two, one, two, three, one], axis=0)

def split(x):
    high = x.astype(BF16)
    return high, (x - high.astype(F32)).astype(BF16)


def dot(a, b):
    return lax.dot_general(a, b, (((1,), (0,)), ((), ())), preferred_element_type=F32)


def dot_t(a, b):
    return lax.dot_general(a, b, (((1,), (1,)), ((), ())), preferred_element_type=F32)


def thrice(x):
    high, lo = split(x)
    return jnp.concatenate([high, high, lo], axis=1)


def dot3(a, b):
    high, lo = split(b)
    return dot(a, jnp.concatenate([high, lo, high], axis=0))


def lanes(rows):
    return lax.broadcasted_iota(jnp.int32, (rows, 128), 1)


def turn(x):
    return pltpu.roll(x, 64, 1)


def pick(y):
    return (y % 4) ^ (2 * (y // 4))


def whereabouts():
    s = lax.axis_index("space")
    return lax.axis_index("bead"), (s & 7) >> 2, s


def pack_kernel(table, pos, mom, force, species, nbr, counts, ghost, out):
    r, _, _ = whereabouts()
    low = lanes(64) < 64
    kind = species[...].astype(F32)
    mass = 1.0 + 15.0 * kind
    blank = jnp.zeros((4, 64), F32)
    coords = jnp.concatenate([pos[0], pos[1], pos[2], blank], axis=0)
    kicked = jnp.concatenate([mom[c] + 0.5 * force[c] for c in range(3)] + [blank], axis=0)
    moved = dot(table[r, 0], parts_of(jnp.concatenate([coords, kicked / mass], axis=1)))
    driven = dot(table[r, 1], parts_of(jnp.concatenate([mass * coords, kicked], axis=1)))
    shares = jnp.where(low, moved[0:64] + turn(moved[64:128]), driven[0:64] - turn(driven[64:128]))
    ghosts = ghost[0].astype(F32)
    last = jnp.concatenate([ghosts[0:1], ghosts[1:2], jnp.zeros((1, 96), F32)], axis=1)
    row = lax.broadcasted_iota(jnp.int32, (8, 128), 0)
    for bead in range(4):
        e = nbr[bead].astype(F32)
        info = jnp.concatenate(
            [
                jnp.zeros((3, 128), F32),
                jnp.concatenate([counts[bead : bead + 1].astype(F32), kind], axis=1),
                jnp.concatenate([e[0:1], e[1:2]], axis=1),
                jnp.concatenate([e[2:3], e[3:4]], axis=1),
                last,
                jnp.zeros((1, 128), F32),
            ],
            axis=0,
        )
        for to in range(4):
            n = (4 * to + bead) // 2
            share = shares[8 * n : 8 * n + 8]
            if bead % 2:
                share = pltpu.roll(share, 4, 0)
            block = jnp.where(row < 3, share, info)
            for y in range(8):
                if pick(y) == bead:
                    out[to * 8 + y] = block


def modes_kernel(got, packed, own, moment):
    r, side, _ = whereabouts()
    low = lanes(8) < 64
    row = lax.broadcasted_iota(jnp.int32, (8, 128), 0)
    moments = []
    for t in range(4):
        even, odd = (
            (got[d] + got[8 + d]) + (got[16 + d] + got[24 + d]) for d in (2 * t, 2 * t + 1)
        )
        info_even, info_odd = got[r * 8 + 2 * t], got[r * 8 + 2 * t + 1]
        left = jnp.where(low, info_even, turn(info_odd))
        right = jnp.where(low, turn(info_even), info_odd)
        coords = jnp.where(low, even, turn(odd))
        moments.append(jnp.where(low, turn(even), odd))
        packed[t, 0:8] = jnp.where(row < 3, coords, jnp.broadcast_to(right[3:4], (8, 128)))
        packed[t, 8:16] = jnp.where(row < 3, pltpu.roll(right, 5, 0), left)
    for t in range(2):
        moment[t] = jnp.where(side == 1, moments[2 + t], moments[t])
    own[...] = packed[pl.ds(2 * side, 2)]


ORDER = ((0, 0), (0, 1), (1, 0), (2, 0), (0, 2), (1, 1), (2, 1), (3, 0), (1, 2), (2, 2), (3, 1), (3, 2))


def rates():
    row = lax.broadcasted_iota(jnp.int32, (8, 128), 0)
    rate = jnp.zeros((8, 128), F32)
    for n in range(8):
        rate = jnp.where(row == n, float(RATES[n]), rate)
    return rate


def abreast(jobs):
    results = [None] * len(jobs)
    left = list(range(len(jobs)))
    while left:
        for n in list(left):
            try:
                next(jobs[n])
            except StopIteration as stop:
                results[n] = stop.value
                left.remove(n)
    return results


def sigmoid(v):
    return 1.0 / (1.0 + jnp.exp(-v))


def layer_one(pk, tiles, weights, hot, ys, gp, mom_one, slope_one, u_two):
    w_one_cat, mix1_t, prj_t, base_col, step_col = weights
    low = lanes(8) < 64
    low1 = lanes(1) < 64
    head = lanes(1) < 16
    rate = rates()
    spot = lax.broadcasted_iota(jnp.int32, (256, 128), 0).astype(F32)
    ghost_spot = lax.broadcasted_iota(jnp.int32, (32, 128), 0).astype(F32) + 64.0
    def one(t):
        here = pk[t + 1, 0:8]
        info = pk[t + 1, 8:16]
        beside = jnp.where(low, pk[t + 2, 0:8], pk[t, 0:8])
        wide = jnp.concatenate([here, beside], axis=1)
        a = wide.astype(BF16).astype(F32)
        b = (wide - a).astype(BF16).astype(F32)
        c = (wide - a - b).astype(BF16).astype(F32)
        parts = jnp.concatenate([a, b, c, jnp.zeros((8, 256), F32)], axis=0).astype(BF16)
        g_prev, g_here, g_next = pk[t, 14:15], info[6:7], pk[t + 2, 14:15]
        table = jnp.concatenate(
            [
                jnp.where(head, turn(g_prev) + 192.0, turn(g_here) + 64.0),
                jnp.where(head, g_here, g_next + 128.0),
                jnp.zeros((14, 128), F32),
            ],
            axis=0,
        )[:, 0:32].astype(BF16)
        count = info[3:4]
        sums = [None] * 9
        for k, row in enumerate((4, 1, 5, 2)):
            e = info[row : row + 1]
            hit = jnp.where(ghost_spot == e, 1.0, 0.0).astype(BF16)
            far = dot(table, hit)
            n = jnp.where(
                e < 64.0, e + jnp.where(low1, 0.0, 64.0), jnp.where(low1, far[0:1], far[1:2])
            )
            one_hot = jnp.where(spot == n, 1.0, 0.0).astype(BF16)
            hot[t, :, k * 128 : (k + 1) * 128] = one_hot
            got = dot(parts, one_hot)
            there = got[0:8] + (got[8:16] + got[16:24])
            off = there - here
            x, y, z = off[0:1], off[1:2], off[2:3]
            q = x * x + y * y + z * z
            live = jnp.where(count > float(k), 0.25, 0.0)
            g = jnp.exp(-rate * q) * live
            both = jnp.concatenate([g, g * there[3:4]], axis=0)
            harmonic = [
                None, x, y, z, ROOT3 * x * y, ROOT3 * y * z, 0.5 * (3.0 * z * z - q), ROOT3 * x * z,
                (0.5 * ROOT3) * (x * x - y * y),
            ]
            gp[t, k] = both
            ys[t, k] = jnp.concatenate(harmonic[1:9], axis=0)
            for l in range(9):
                term = both if l == 0 else harmonic[l] * both
                sums[l] = term if sums[l] is None else sums[l] + term
            yield
        high, lo = split(jnp.concatenate(sums, axis=1))
        moments = dot(w_one_cat, jnp.concatenate([high, lo, high], axis=0))
        yield
        m = [moments[:, l * 128 : (l + 1) * 128] for l in range(9)]
        for l in range(9):
            mom_one[t, l] = m[l]
        inv = jnp.concatenate(
            [m[0] * m[0], sum(m[l] * m[l] for l in (1, 2, 3)), sum(m[l] * m[l] for l in range(4, 9))],
            axis=0,
        )
        v = dot3(mix1_t, inv)
        yield
        sig = sigmoid(v)
        slope_one[t] = sig * (1.0 + v * (1.0 - sig))
        h = base_col + here[3:4] * step_col + v * sig
        u_two[t] = dot3(prj_t, h)
        yield

    abreast([one(t) for t in tiles])


def forms_kernel(
    sent, embed, radial_one, radial_two, mix_one, mix_two, proj, readout,
    mix_back, mix_fwd, prj_all, columns, first_cat, first_parts, second_cat, second_parts,
):
    del sent

    def column(row):
        return jnp.broadcast_to(row, (128, 128)).T

    columns[0] = column(embed[0:1])
    columns[1] = column(embed[1:2] - embed[0:1])
    columns[2] = column(readout[1:2])
    columns[3] = column(readout[0:1] + readout[1:2])
    for n, mix in enumerate((mix_one, mix_two)):
        mix_back[n] = thrice(mix[...])
        mix_fwd[n] = thrice(mix[...].T)
    prj_all[0] = thrice(proj[...])
    prj_all[1] = thrice(proj[...].T)
    base, step = embed[0:1], embed[1:2] - embed[0:1]
    high, lo = split(jnp.concatenate([radial_one[...] * base, radial_one[...] * step], axis=0))
    first_parts[...] = jnp.concatenate([high, high, lo], axis=1)
    first_cat[...] = jnp.concatenate([high, high, lo], axis=0).astype(F32).T.astype(BF16)
    high, lo = split(radial_two[...])
    second_parts[...] = jnp.concatenate([high, high, lo], axis=1)
    high, lo = high.astype(F32), lo.astype(F32)
    second_cat[...] = jnp.concatenate([high, high, lo, jnp.zeros((8, 128), F32)], axis=0).T.astype(BF16)


def nodes_of_edges(t, m, hot, gp, u_two, second_cat, tk, gk, rk):
    low_wide = lanes(128) < 64
    beside = jnp.where(low_wide, u_two[t + 1], u_two[t - 1])
    high, lo = split(jnp.concatenate([u_two[t], beside], axis=1))
    parts = jnp.concatenate([high, lo], axis=0)
    for k in range(4):
        got = dot(parts, hot[t, :, k * 128 : (k + 1) * 128])
        nodes = got[0:128] + got[128:256]
        g = gp[t, k, 0:8]
        gh = g.astype(BF16).astype(F32)
        rows = jnp.concatenate([gh, g - gh, gh, jnp.zeros((8, 128), F32)], axis=0).astype(BF16)
        weight = dot(second_cat[...], rows)
        gk[m, k] = nodes
        rk[m, k] = weight
        tk[m, k] = nodes * weight


def edge_sums(t, ys):
    edge = [[ys[t, k, c : c + 1] for c in range(3)] for k in range(4)]
    scalar, legendre = {}, {}
    for i in range(4):
        for j in range(i, 4):
            scalar[i, j] = scalar[j, i] = sum(edge[i][c] * edge[j][c] for c in range(3))
    for i in range(4):
        for j in range(i, 4):
            legendre[i, j] = legendre[j, i] = 1.5 * scalar[i, j] * scalar[i, j] - 0.5 * scalar[i, i] * scalar[j, j]
    return edge, scalar, legendre


def invariants_two(t, m, ys, tk, v_one, v_two):
    _, scalar, legendre = edge_sums(t, ys)
    total = (tk[m, 0] + tk[m, 1]) + (tk[m, 2] + tk[m, 3])
    inv1 = inv2 = None
    for i in range(4):
        va = sum(scalar[i, j] * tk[m, j] for j in range(4))
        vb = sum(legendre[i, j] * tk[m, j] for j in range(4))
        v_one[m, i], v_two[m, i] = va, vb
        inv1 = va * tk[m, i] if inv1 is None else inv1 + va * tk[m, i]
        inv2 = vb * tk[m, i] if inv2 is None else inv2 + vb * tk[m, i]
    return jnp.concatenate([total * total, inv1, inv2], axis=0)


def mixing_back(m, inv, mix_back, mix_fwd, columns, dinv):
    v = dot3(mix_fwd[1], inv)
    sig = sigmoid(v)
    dv = columns[2] * (sig * (1.0 + v * (1.0 - sig)))
    dinv[m] = 2.0 * dot3(mix_back[1], dv)


def edges_back(t, m, hot, ys, gp, second_parts, tk, gk, rk, v_one, v_two, dinv, du_two, dvec):
    low_wide = lanes(128) < 64
    edge, scalar, _ = edge_sums(t, ys)
    rate = rates()
    d1, d2 = dinv[m, 128:256], dinv[m, 256:384]
    d0 = dinv[m, 0:128] * ((tk[m, 0] + tk[m, 1]) + (tk[m, 2] + tk[m, 3]))
    pull, bend = {}, {}
    for i in range(4):
        wa, wb = d1 * tk[m, i], d2 * tk[m, i]
        for j in range(i, 4):
            pull[i, j] = pull[j, i] = jnp.sum(wa * tk[m, j], axis=0, keepdims=True)
            bend[i, j] = bend[j, i] = jnp.sum(wb * tk[m, j], axis=0, keepdims=True)
    back = []
    for k in range(4):
        dt = d0 + d1 * v_one[m, k] + d2 * v_two[m, k]
        dg = dot3(second_parts[...], dt * gk[m, k])
        back.append(jnp.concatenate(split(dt * rk[m, k]), axis=0))
        dq = 0.5 * pull[k, k] + bend[k, k] * scalar[k, k] - jnp.sum(rate * gp[t, k, 0:8] * dg, axis=0, keepdims=True)
        d = [None] * 3
        for j in range(4):
            if j != k:
                dq = dq - 0.5 * bend[k, j] * scalar[j, j]
                tie = pull[k, j] + 3.0 * bend[k, j] * scalar[k, j]
                d = [tie * edge[j][c] if d[c] is None else d[c] + tie * edge[j][c] for c in range(3)]
        d = [d[c] + 2.0 * dq * edge[k][c] for c in range(3)]
        dvec[t, k] = jnp.concatenate(d + [jnp.zeros((5, 128), F32)], axis=0)
    back = dot_t(jnp.concatenate(back, axis=1), hot[t])
    back = back[0:128] + back[128:256]
    du_two[t] += back[:, 0:128]
    aside = back[:, 128:256]
    du_two[t + 1] += jnp.where(low_wide, aside, 0.0)
    du_two[t - 1] += jnp.where(low_wide, 0.0, aside)


def plane_work(
    packed, forms, hot, ys, gp, mom_one, slope_one, u_two, du_two, dvec,
    pk, tk, gk, rk, v_one, v_two, dinv,
):
    mix_back, mix_fwd, prj_all, columns, first_cat, first_parts, second_cat, second_parts = forms
    _, side, _ = whereabouts()
    first = 2 * (1 - side)
    for t in range(2):
        pk[t] = packed[0]
        pk[6 + t] = packed[3]
    pk[pl.ds(first + 1, 4)] = packed[...]
    weights = (first_cat[...], mix_fwd[0], prj_all[1], columns[0], columns[1])
    start = 3 * (1 - side)
    layer_one(pk, [start + i for i in range(3)], weights, hot, ys, gp, mom_one, slope_one, u_two)

    du_two[...] = jnp.zeros_like(du_two)
    t = start + 1
    nodes_of_edges(t, 0, hot, gp, u_two, second_cat, tk, gk, rk)
    inv = invariants_two(t, 0, ys, tk, v_one, v_two)
    mixing_back(0, inv, mix_back, mix_fwd, columns, dinv)
    edges_back(t, 0, hot, ys, gp, second_parts, tk, gk, rk, v_one, v_two, dinv, du_two, dvec)


def is_early(s):
    return s < 4


def early_kernel(packed, *refs):
    forms, rest = refs[0:8], refs[10:]

    @pl.when(is_early(whereabouts()[2]))
    def _():
        plane_work(packed, forms, *rest)


def late_kernel(packed, *refs):
    forms, rest = refs[0:8], refs[16:]

    @pl.when(jnp.logical_not(is_early(whereabouts()[2])))
    def _():
        plane_work(packed, forms, *rest)


def force_kernel(packed, across, moment, *refs):
    mix_back, mix_fwd, prj_all, columns, first_cat, first_parts, second_cat, second_parts = refs[0:8]
    out, hot, ys, gp, mom_one, slope_one, u_two, du_two, dvec, pk, tk, gk, rk, v_one, v_two, dinv = refs[16:]
    _, side, _ = whereabouts()
    low = lanes(8) < 64
    first = 2 * (1 - side)
    other = 4 * side
    pk[0] = across[0]
    pk[7] = across[1]
    pk[pl.ds(first + 1, 4)] = packed[...]
    pk[pl.ds(other + 1, 2)] = across[...]
    weights = (first_cat[...], mix_fwd[0], prj_all[1], columns[0], columns[1])
    start = 3 * side
    layer_one(pk, [start + i for i in range(3)], weights, hot, ys, gp, mom_one, slope_one, u_two)
    rate = rates()

    turns = [side + 1 + i for i in range(3)]
    inv = {}

    def stage(n, m):
        t = turns[m]
        if n == 0:
            nodes_of_edges(t, m, hot, gp, u_two, second_cat, tk, gk, rk)
        elif n == 1:
            inv[m] = invariants_two(t, m, ys, tk, v_one, v_two)
        elif n == 2:
            mixing_back(m, inv[m], mix_back, mix_fwd, columns, dinv)
        else:
            edges_back(t, m, hot, ys, gp, second_parts, tk, gk, rk, v_one, v_two, dinv, du_two, dvec)

    for n, m in ORDER:
        stage(n, m)

    def third(du, slope, mom, gs, harmonics, pushes, spots):
        dh = columns[3] + dot3(prj_all[0], du)
        yield
        dinv = 2.0 * dot3(mix_back[0], dh * slope)
        yield
        parts = []
        for l in range(9):
            part = 0 if l == 0 else 1 if l < 4 else 2
            parts.append(mom(l) * dinv[part * 128 : (part + 1) * 128])
        dm = dot3(first_parts[...], jnp.concatenate(parts, axis=1))
        yield
        dm = [dm[:, l * 128 : (l + 1) * 128] for l in range(9)]
        rate2 = jnp.concatenate([rate, rate], axis=0)
        back = None
        centre = None
        for k in range(4):
            g, yk, push = gs(k), harmonics(k), pushes(k)
            dg = dm[0]
            dys = []
            for l in range(1, 9):
                dg = dg + yk[l - 1 : l] * dm[l]
                dys.append(jnp.sum(g * dm[l], axis=0, keepdims=True))
            dq = -jnp.sum(rate2 * g * dg, axis=0, keepdims=True)
            x, y, z = yk[0:1], yk[1:2], yk[2:3]
            e1, e2, e3, e4, e5, e6, e7, e8 = dys
            dx = e1 + ROOT3 * (y * e4 + z * e7 + x * e8) + x * (2.0 * dq - e6)
            dy = e2 + ROOT3 * (x * e4 + z * e5 - y * e8) + y * (2.0 * dq - e6)
            dz = e3 + ROOT3 * (y * e5 + x * e7) + 2.0 * z * (dq + e6)
            d = push + jnp.concatenate([dx, dy, dz, jnp.zeros((5, 128), F32)], axis=0)
            centre = d if centre is None else centre + d
            d_high = d.astype(BF16).astype(F32)
            rows = jnp.concatenate([d_high, d - d_high], axis=0).astype(BF16)
            term = dot_t(rows, spots(k))
            back = term if back is None else back + term
            yield
        return back[0:8] + back[8:16], centre

    def own_tile(t):
        return third(
            du_two[t], slope_one[t], lambda l: mom_one[t, l], lambda k: gp[t, k], lambda k: ys[t, k],
            lambda k: dvec[t, k], lambda k: hot[t, :, k * 128 : (k + 1) * 128],
        )

    def mixed(ref, *at):
        right, left = ref[(4,) + at], ref[(1,) + at]
        keep = lax.broadcasted_iota(jnp.int32, right.shape, 1) < 64
        return jnp.where(keep, right, left)

    def mixed_spots(k):
        at = (slice(128, 256), slice(k * 128, (k + 1) * 128))
        keep = lanes(128) < 64
        return jnp.where(keep, hot[(4,) + at].astype(F32), hot[(1,) + at].astype(F32)).astype(BF16)

    rim = third(
        mixed(du_two), mixed(slope_one), lambda l: mixed(mom_one, l), lambda k: mixed(gp, k), lambda k: mixed(ys, k),
        lambda k: mixed(dvec, k), mixed_spots,
    )
    (back2, centre2), (back3, centre3), (rim, _) = abreast([own_tile(2), own_tile(3), rim])
    f2 = centre2 - back2[:, 0:128] - jnp.where(low, rim, back3[:, 128:256])
    f3 = centre3 - back3[:, 0:128] - jnp.where(low, back2[:, 128:256], rim)
    row = lax.broadcasted_iota(jnp.int32, (8, 128), 0)
    for t, f in enumerate((f2, f3)):
        coords, drift = pk[t + 3, 0:8], pltpu.roll(moment[t], 3, 0)
        out[2 * t] = jnp.where(row < 3, jnp.where(low, f, turn(coords)), drift)
        out[2 * t + 1] = jnp.where(row < 3, jnp.where(low, turn(f), coords), turn(drift))


def finish_kernel(got, pos_out, mom_out, force_out):
    _, side, _ = whereabouts()
    for b in range(4):
        block = got[b ^ (2 * side)]
        turned = turn(block)
        for c in range(3):
            force = block[c : c + 1, 0:64]
            pos_out[c, b : b + 1] = turned[c : c + 1, 0:64]
            mom_out[c, b : b + 1] = block[3 + c : 4 + c, 0:64] + 0.5 * force
            force_out[c, b : b + 1] = force


def shape(*dims):
    return jax.ShapeDtypeStruct(dims, F32)


def room(mib):
    return pltpu.CompilerParams(vmem_limit_bytes=mib << 20)


def near(*dims, dtype=F32):
    return pltpu.VMEM(dims, dtype)


def far(x):
    return pltpu.with_memory_space_constraint(x, pltpu.HBM)


def keep(x):
    return pltpu.with_memory_space_constraint(x, pltpu.VMEM)


def on_device(
    positions, momenta, forces, species, neighbours, counts, ghost_rows,
    embed, radial_one, radial_two, mix_one, mix_two, projection, readout,
):
    count = lax.axis_size("space")
    both = ("bead", "space")
    planes = [[b * count + z * 8 + i for b in range(4) for i in range(8)] for z in range(count // 8)]
    quads = [[b * count + h * 4 + i for i in range(4)] for b in range(4) for h in range(count // 4)]
    beside = []
    for b in range(4):
        for z in range(count // 8):
            for i in range(4):
                here = b * count + z * 8 + i
                back = b * count + (z * 8 - 4) % count + (i ^ 2)
                beside += [(here, back), (back, here)]

    turned = [jnp.transpose(x, (1, 0, 2)) for x in (positions, momenta, forces)]
    sent = pl.pallas_call(
        pack_kernel, out_shape=shape(32, 8, 128), in_specs=[VM] * 8, out_specs=VM, name="pack",
    )(*[far(x) for x in (jnp.asarray(mode_tables()), *turned, species[None, :], neighbours, counts, ghost_rows)])
    got = keep(lax.all_to_all(sent, both, 0, 0, axis_index_groups=planes))
    forms = pl.pallas_call(
        forms_kernel,
        out_shape=(
            near(2, 384, 384, dtype=BF16), near(2, 128, 1152, dtype=BF16),
            near(2, 128, 384, dtype=BF16), near(4, 128, 128), near(128, 48, dtype=BF16),
            near(16, 384, dtype=BF16), near(128, 32, dtype=BF16), near(8, 384, dtype=BF16),
        ),
        in_specs=[pl.BlockSpec(memory_space=pl.ANY)] + [VM] * 7,
        out_specs=(VM,) * 8,
        compiler_params=room(8),
        cost_estimate=pl.CostEstimate(flops=2_000_000_000, bytes_accessed=4_000_000, transcendentals=0),
        name="forms",
    )(*[far(x) for x in (sent, embed, radial_one, radial_two, mix_one, mix_two, projection, readout)])
    packed, own, moment = pl.pallas_call(
        modes_kernel,
        out_shape=(near(4, 16, 128), near(2, 16, 128), near(2, 8, 128)),
        in_specs=[VM],
        out_specs=(VM,) * 3,
        compiler_params=room(16),
        name="modes",
    )(got)
    kept = (
        near(TILES, 256, 512, dtype=BF16),
        near(TILES, 4, 8, 128),
        near(TILES, 4, 16, 128),
        near(TILES, 9, 128, 128),
        near(TILES, 128, 128),
        near(TILES, 128, 128),
        near(TILES, 128, 128),
        near(TILES, 4, 8, 128),
    )

    def scratch(n):
        return [near(8, 16, 128)] + [near(n, 4, 128, 128)] * 5 + [near(n, 384, 128)]

    own, *state = pl.pallas_call(
        early_kernel,
        out_shape=(near(2, 16, 128),) + kept,
        in_specs=[VM] * 10,
        out_specs=(VM,) * 9,
        scratch_shapes=scratch(1),
        input_output_aliases={9: 0},
        compiler_params=room(24),
        name="early",
    )(packed, *forms, own)
    across = keep(lax.ppermute(own, both, beside))
    state = pl.pallas_call(
        late_kernel,
        out_shape=kept,
        in_specs=[VM] * 17,
        out_specs=(VM,) * 8,
        scratch_shapes=scratch(1),
        input_output_aliases={9 + i: i for i in range(8)},
        compiler_params=room(24),
        cost_estimate=pl.CostEstimate(flops=4_000_000_000, bytes_accessed=8_000_000, transcendentals=0),
        name="late",
    )(packed, *forms, *state)
    grad = pl.pallas_call(
        force_kernel,
        out_shape=(near(4, 8, 128),) + kept,
        in_specs=[VM] * 19,
        out_specs=(VM,) * 9,
        scratch_shapes=scratch(3),
        input_output_aliases={11 + i: 1 + i for i in range(8)},
        compiler_params=room(24),
        name="force",
    )(packed, across, moment, *forms, *state)[0]
    back = keep(lax.all_to_all(grad, both, 0, 0, axis_index_groups=quads))
    outs = pl.pallas_call(
        finish_kernel,
        out_shape=(shape(3, 4, 64),) * 3,
        in_specs=[VM],
        out_specs=(VM,) * 3,
        compiler_params=room(8),
        name="finish",
    )(back)
    return tuple(jnp.transpose(x, (1, 0, 2)) for x in outs)


def solution(mesh):
    spread = P("bead", None, "space")
    placed = (
        spread, spread, spread, P("space"), spread, P("bead", "space"), P("space", None, None),
    ) + (P(),) * 7
    return jax.shard_map(
        on_device, mesh=mesh, in_specs=placed, out_specs=(spread,) * 3, check_vma=False
    )
```

```python
import numpy as np

import jax
import jax.numpy as jnp
from jax import lax
from jax.experimental import pallas as pl
from jax.experimental.pallas import tpu as pltpu
from jax.sharding import PartitionSpec as P


F32 = jnp.float32
BF16 = jnp.bfloat16
BEADS = 16
TILES = 6
ROOT3 = float(np.sqrt(3.0))
VM = pl.BlockSpec(memory_space=pltpu.VMEM)
RATES = 0.25 * 16.0 ** (np.arange(8) / 7.0)


def propagators():
    n = BEADS
    b = np.arange(n)
    phase = 2.0 * np.pi * np.outer(b, b) / n
    matrix = np.where(b[None] < n // 2, np.cos(phase), np.sin(phase)) * np.sqrt(2.0 / n)
    matrix[:, n // 2] = np.where(b % 2 == 0, 1.0, -1.0) / np.sqrt(n)
    matrix[:, 0] = 1.0 / np.sqrt(n)
    w = 1.5 * np.sin(np.pi * b / n)
    drift = np.where(b == 0, 1.0, np.sin(w) / np.where(b == 0, 1.0, w))
    return [(matrix * d) @ matrix.T for d in (np.cos(w), drift, w * np.sin(w))]


def mode_tables():
    cosine, drift, stiff = propagators()
    rows = np.zeros((4, 4, 64, 16))
    for sender in range(4):
        for bead in range(BEADS):
            for c in range(3):
                for b in range(4):
                    for n, values in enumerate((cosine, drift, cosine, stiff)):
                        rows[sender, n, 4 * bead + c, 4 * c + b] = values[bead, 4 * sender + b]
    rows = rows.astype(np.float32).reshape(4, 2, 128, 16)
    one = rows.astype(BF16)
    two = (rows - one.astype(np.float32)).astype(BF16)
    three = (rows - one.astype(np.float32) - two.astype(np.float32)).astype(BF16)
    return np.concatenate([one, one, two, two, one, three], axis=-1)


def parts_of(x):
    one = x.astype(BF16)
    rest = x - one.astype(F32)
    two = rest.astype(BF16)
    three = (rest - two.astype(F32)).astype(BF16)
    return jnp.concatenate([one, two, one, two, three, one], axis=0)

def split(x):
    high = x.astype(BF16)
    return high, (x - high.astype(F32)).astype(BF16)


def dot(a, b):
    return lax.dot_general(a, b, (((1,), (0,)), ((), ())), preferred_element_type=F32)


def dot_t(a, b):
    return lax.dot_general(a, b, (((1,), (1,)), ((), ())), preferred_element_type=F32)


def thrice(x):
    high, lo = split(x)
    return jnp.concatenate([high, high, lo], axis=1)


def dot3(a, b):
    high, lo = split(b)
    return dot(a, jnp.concatenate([high, lo, high], axis=0))


def lanes(rows):
    return lax.broadcasted_iota(jnp.int32, (rows, 128), 1)


def turn(x):
    return pltpu.roll(x, 64, 1)


def pick(y):
    return (y % 4) ^ (2 * (y // 4))


def whereabouts():
    s = lax.axis_index("space")
    return lax.axis_index("bead"), (s & 7) >> 2, s


def pack_kernel(table, pos, mom, force, species, nbr, counts, ghost, out):
    r, _, _ = whereabouts()
    low = lanes(64) < 64
    kind = species[...].astype(F32)
    mass = 1.0 + 15.0 * kind
    blank = jnp.zeros((4, 64), F32)
    coords = jnp.concatenate([pos[0], pos[1], pos[2], blank], axis=0)
    kicked = jnp.concatenate([mom[c] + 0.5 * force[c] for c in range(3)] + [blank], axis=0)
    moved = dot(table[r, 0], parts_of(jnp.concatenate([coords, kicked / mass], axis=1)))
    driven = dot(table[r, 1], parts_of(jnp.concatenate([mass * coords, kicked], axis=1)))
    shares = jnp.where(low, moved[0:64] + turn(moved[64:128]), driven[0:64] - turn(driven[64:128]))
    ghosts = ghost[0].astype(F32)
    last = jnp.concatenate([ghosts[0:1], ghosts[1:2], jnp.zeros((1, 96), F32)], axis=1)
    row = lax.broadcasted_iota(jnp.int32, (8, 128), 0)
    for bead in range(4):
        e = nbr[bead].astype(F32)
        info = jnp.concatenate(
            [
                jnp.zeros((3, 128), F32),
                jnp.concatenate([counts[bead : bead + 1].astype(F32), kind], axis=1),
                jnp.concatenate([e[0:1], e[1:2]], axis=1),
                jnp.concatenate([e[2:3], e[3:4]], axis=1),
                last,
                jnp.zeros((1, 128), F32),
            ],
            axis=0,
        )
        for to in range(4):
            n = (4 * to + bead) // 2
            share = shares[8 * n : 8 * n + 8]
            if bead % 2:
                share = pltpu.roll(share, 4, 0)
            block = jnp.where(row < 3, share, info)
            for y in range(8):
                if pick(y) == bead:
                    out[to * 8 + y] = block


def modes_kernel(got, packed, own, moment):
    r, side, _ = whereabouts()
    low = lanes(8) < 64
    row = lax.broadcasted_iota(jnp.int32, (8, 128), 0)
    moments = []
    for t in range(4):
        even, odd = (
            (got[d] + got[8 + d]) + (got[16 + d] + got[24 + d]) for d in (2 * t, 2 * t + 1)
        )
        info_even, info_odd = got[r * 8 + 2 * t], got[r * 8 + 2 * t + 1]
        left = jnp.where(low, info_even, turn(info_odd))
        right = jnp.where(low, turn(info_even), info_odd)
        coords = jnp.where(low, even, turn(odd))
        moments.append(jnp.where(low, turn(even), odd))
        packed[t, 0:8] = jnp.where(row < 3, coords, jnp.broadcast_to(right[3:4], (8, 128)))
        packed[t, 8:16] = jnp.where(row < 3, pltpu.roll(right, 5, 0), left)
    for t in range(2):
        moment[t] = jnp.where(side == 1, moments[2 + t], moments[t])
    own[...] = packed[pl.ds(2 * side, 2)]


ORDER = ((0, 0), (0, 1), (1, 0), (2, 0), (1, 1), (3, 0), (2, 1), (3, 1))


def rates():
    row = lax.broadcasted_iota(jnp.int32, (8, 128), 0)
    rate = jnp.zeros((8, 128), F32)
    for n in range(8):
        rate = jnp.where(row == n, float(RATES[n]), rate)
    return rate


def abreast(jobs):
    results = [None] * len(jobs)
    left = list(range(len(jobs)))
    while left:
        for n in list(left):
            try:
                next(jobs[n])
            except StopIteration as stop:
                results[n] = stop.value
                left.remove(n)
    return results


def sigmoid(v):
    return 1.0 / (1.0 + jnp.exp(-v))


def layer_one(pk, jobs, weights, hot, ys, gp, mom_one, slope_one, u_two):
    w_one_cat, mix1_t, prj_t, base_col, step_col = weights
    low = lanes(8) < 64
    low1 = lanes(1) < 64
    head = lanes(1) < 16
    rate = rates()
    spot = lax.broadcasted_iota(jnp.int32, (256, 128), 0).astype(F32)
    ghost_spot = lax.broadcasted_iota(jnp.int32, (32, 128), 0).astype(F32) + 64.0

    def thirds(wide):
        a = wide.astype(BF16).astype(F32)
        b = (wide - a).astype(BF16).astype(F32)
        c = (wide - a - b).astype(BF16).astype(F32)
        return jnp.concatenate([a, b, c, jnp.zeros((8, 256), F32)], axis=0)

    def one(job):
        whole = not isinstance(job, tuple)
        lower, upper, t, outer, mask = (job, job, job, None, None) if whole else job

        def put(ref, at, value):
            if mask is not None:
                rows = value.shape[0]
                mine = jnp.where(lanes(rows) < 64, 0, 1) == mask
                value = jnp.where(mine, value, ref[at].astype(F32))
            ref[at] = value.astype(ref.dtype)

        here_low, info = pk[lower + 1, 0:8], pk[lower + 1, 8:16]
        g_prev, g_low, g_high, g_next = (pk[n, 14:15] for n in (lower, lower + 1, upper + 1, upper + 2))
        beside = jnp.where(low, pk[upper + 2, 0:8], pk[lower, 0:8])
        parts = thirds(jnp.concatenate([here_low, beside], axis=1))
        here = here_low
        if not whole:
            here_high = pk[upper + 1, 0:8]
            here = jnp.where(low, here_low, here_high)
            info = jnp.where(low, info, pk[upper + 1, 8:16])
            parts = jnp.concatenate([parts, thirds(jnp.concatenate([here_high, beside], axis=1))], axis=0)
        parts = parts.astype(BF16)
        table = jnp.concatenate(
            [
                jnp.where(head, turn(g_prev) + 192.0, turn(g_low) + 64.0),
                jnp.where(head, g_high, g_next + 128.0),
                jnp.zeros((14, 128), F32),
            ],
            axis=0,
        )[:, 0:32].astype(BF16)
        count = info[3:4]
        sums = [None] * 9
        for k, row in enumerate((4, 1, 5, 2)):
            e = info[row : row + 1]
            hit = jnp.where(ghost_spot == e, 1.0, 0.0).astype(BF16)
            far = dot(table, hit)
            n = jnp.where(
                e < 64.0, e + jnp.where(low1, 0.0, 64.0), jnp.where(low1, far[0:1], far[1:2])
            )
            one_hot = jnp.where(spot == n, 1.0, 0.0)
            put(hot, (t, slice(None), slice(k * 128, (k + 1) * 128)), one_hot)
            got = dot(parts, one_hot.astype(BF16))
            there = got[0:8] + (got[8:16] + got[16:24])
            if not whole:
                there = jnp.where(low, there, got[32:40] + (got[40:48] + got[48:56]))
            off = there - here
            x, y, z = off[0:1], off[1:2], off[2:3]
            q = x * x + y * y + z * z
            live = jnp.where(count > float(k), 0.25, 0.0)
            g = jnp.exp(-rate * q) * live
            both = jnp.concatenate([g, g * there[3:4]], axis=0)
            harmonic = [
                None, x, y, z, ROOT3 * x * y, ROOT3 * y * z, 0.5 * (3.0 * z * z - q), ROOT3 * x * z,
                (0.5 * ROOT3) * (x * x - y * y),
            ]
            put(gp, (t, k), both)
            put(ys, (t, k), jnp.concatenate(harmonic[1:9], axis=0))
            for l in range(9):
                term = both if l == 0 else harmonic[l] * both
                sums[l] = term if sums[l] is None else sums[l] + term
            yield
        high, lo = split(jnp.concatenate(sums, axis=1))
        moments = dot(w_one_cat, jnp.concatenate([high, lo, high], axis=0))
        yield
        m = [moments[:, l * 128 : (l + 1) * 128] for l in range(9)]
        for l in range(9):
            put(mom_one, (t, l), m[l])
        inv = jnp.concatenate(
            [m[0] * m[0], sum(m[l] * m[l] for l in (1, 2, 3)), sum(m[l] * m[l] for l in range(4, 9))],
            axis=0,
        )
        v = dot3(mix1_t, inv)
        yield
        sig = sigmoid(v)
        put(slope_one, (t,), sig * (1.0 + v * (1.0 - sig)))
        h = base_col + here[3:4] * step_col + v * sig
        u = dot3(prj_t, h)
        put(u_two, (t,), u)
        if outer is not None:
            u_two[outer] = u
        yield

    abreast([one(job) for job in jobs])


def forms_kernel(
    sent, embed, radial_one, radial_two, mix_one, mix_two, proj, readout,
    mix_back, mix_fwd, prj_all, columns, first_cat, first_parts, second_cat, second_parts,
):
    del sent

    def column(row):
        return jnp.broadcast_to(row, (128, 128)).T

    columns[0] = column(embed[0:1])
    columns[1] = column(embed[1:2] - embed[0:1])
    columns[2] = column(readout[1:2])
    columns[3] = column(readout[0:1] + readout[1:2])
    for n, mix in enumerate((mix_one, mix_two)):
        mix_back[n] = thrice(mix[...])
        mix_fwd[n] = thrice(mix[...].T)
    prj_all[0] = thrice(proj[...])
    prj_all[1] = thrice(proj[...].T)
    base, step = embed[0:1], embed[1:2] - embed[0:1]
    high, lo = split(jnp.concatenate([radial_one[...] * base, radial_one[...] * step], axis=0))
    first_parts[...] = jnp.concatenate([high, high, lo], axis=1)
    first_cat[...] = jnp.concatenate([high, high, lo], axis=0).astype(F32).T.astype(BF16)
    high, lo = split(radial_two[...])
    second_parts[...] = jnp.concatenate([high, high, lo], axis=1)
    high, lo = high.astype(F32), lo.astype(F32)
    second_cat[...] = jnp.concatenate([high, high, lo, jnp.zeros((8, 128), F32)], axis=0).T.astype(BF16)


def nodes_of_edges(t, m, hot, gp, u_two, second_cat, tk, gk, rk):
    low_wide = lanes(128) < 64
    beside = jnp.where(low_wide, u_two[t + 1], u_two[t - 1])
    high, lo = split(jnp.concatenate([u_two[t], beside], axis=1))
    parts = jnp.concatenate([high, lo], axis=0)
    for k in range(4):
        got = dot(parts, hot[t, :, k * 128 : (k + 1) * 128])
        nodes = got[0:128] + got[128:256]
        g = gp[t, k, 0:8]
        gh = g.astype(BF16).astype(F32)
        rows = jnp.concatenate([gh, g - gh, gh, jnp.zeros((8, 128), F32)], axis=0).astype(BF16)
        weight = dot(second_cat[...], rows)
        gk[m, k] = nodes
        rk[m, k] = weight
        tk[m, k] = nodes * weight


def edge_sums(t, ys):
    edge = [[ys[t, k, c : c + 1] for c in range(3)] for k in range(4)]
    scalar, legendre = {}, {}
    for i in range(4):
        for j in range(i, 4):
            scalar[i, j] = scalar[j, i] = sum(edge[i][c] * edge[j][c] for c in range(3))
    for i in range(4):
        for j in range(i, 4):
            legendre[i, j] = legendre[j, i] = 1.5 * scalar[i, j] * scalar[i, j] - 0.5 * scalar[i, i] * scalar[j, j]
    return edge, scalar, legendre


def invariants_two(t, m, ys, tk, v_one, v_two):
    _, scalar, legendre = edge_sums(t, ys)
    total = (tk[m, 0] + tk[m, 1]) + (tk[m, 2] + tk[m, 3])
    inv1 = inv2 = None
    for i in range(4):
        va = sum(scalar[i, j] * tk[m, j] for j in range(4))
        vb = sum(legendre[i, j] * tk[m, j] for j in range(4))
        v_one[m, i], v_two[m, i] = va, vb
        inv1 = va * tk[m, i] if inv1 is None else inv1 + va * tk[m, i]
        inv2 = vb * tk[m, i] if inv2 is None else inv2 + vb * tk[m, i]
    return jnp.concatenate([total * total, inv1, inv2], axis=0)


def mixing_back(m, inv, mix_back, mix_fwd, columns, dinv):
    v = dot3(mix_fwd[1], inv)
    sig = sigmoid(v)
    dv = columns[2] * (sig * (1.0 + v * (1.0 - sig)))
    dinv[m] = 2.0 * dot3(mix_back[1], dv)


def edges_back(t, m, hot, ys, gp, second_parts, tk, gk, rk, v_one, v_two, dinv, du_two, dvec):
    low_wide = lanes(128) < 64
    edge, scalar, _ = edge_sums(t, ys)
    rate = rates()
    d1, d2 = dinv[m, 128:256], dinv[m, 256:384]
    d0 = dinv[m, 0:128] * ((tk[m, 0] + tk[m, 1]) + (tk[m, 2] + tk[m, 3]))
    pull, bend = {}, {}
    for i in range(4):
        wa, wb = d1 * tk[m, i], d2 * tk[m, i]
        for j in range(i, 4):
            pull[i, j] = pull[j, i] = jnp.sum(wa * tk[m, j], axis=0, keepdims=True)
            bend[i, j] = bend[j, i] = jnp.sum(wb * tk[m, j], axis=0, keepdims=True)
    back = []
    for k in range(4):
        dt = d0 + d1 * v_one[m, k] + d2 * v_two[m, k]
        dg = dot3(second_parts[...], dt * gk[m, k])
        back.append(jnp.concatenate(split(dt * rk[m, k]), axis=0))
        dq = 0.5 * pull[k, k] + bend[k, k] * scalar[k, k] - jnp.sum(rate * gp[t, k, 0:8] * dg, axis=0, keepdims=True)
        d = [None] * 3
        for j in range(4):
            if j != k:
                dq = dq - 0.5 * bend[k, j] * scalar[j, j]
                tie = pull[k, j] + 3.0 * bend[k, j] * scalar[k, j]
                d = [tie * edge[j][c] if d[c] is None else d[c] + tie * edge[j][c] for c in range(3)]
        d = [d[c] + 2.0 * dq * edge[k][c] for c in range(3)]
        dvec[t, k] = jnp.concatenate(d + [jnp.zeros((5, 128), F32)], axis=0)
    back = dot_t(jnp.concatenate(back, axis=1), hot[t])
    back = back[0:128] + back[128:256]
    du_two[t] += back[:, 0:128]
    aside = back[:, 128:256]
    du_two[t + 1] += jnp.where(low_wide, aside, 0.0)
    du_two[t - 1] += jnp.where(low_wide, 0.0, aside)


def layer_two(
    tiles, hot, ys, gp, u_two, mix_back, mix_fwd, columns, second_cat, second_parts,
    tk, gk, rk, v_one, v_two, dinv, du_two, dvec,
):
    inv = {}
    for stage, m in ORDER:
        t = tiles[m]
        if stage == 0:
            nodes_of_edges(t, m, hot, gp, u_two, second_cat, tk, gk, rk)
        elif stage == 1:
            inv[m] = invariants_two(t, m, ys, tk, v_one, v_two)
        elif stage == 2:
            mixing_back(m, inv[m], mix_back, mix_fwd, columns, dinv)
        else:
            edges_back(t, m, hot, ys, gp, second_parts, tk, gk, rk, v_one, v_two, dinv, du_two, dvec)


def plane_work(
    packed, forms, hot, ys, gp, mom_one, slope_one, u_two, du_two, dvec,
    pk, tk, gk, rk, v_one, v_two, dinv,
):
    mix_back, mix_fwd, prj_all, columns, first_cat, first_parts, second_cat, second_parts = forms
    _, side, _ = whereabouts()
    pk[pl.ds(3 - 2 * side, 4)] = packed[...]
    weights = (first_cat[...], mix_fwd[0], prj_all[1], columns[0], columns[1])
    start = 3 - 2 * side
    halves = (5 - 2 * side, 2 - 2 * side, 2 + side, 5 - 5 * side, None)
    layer_one(pk, [start, start + 1, halves], weights, hot, ys, gp, mom_one, slope_one, u_two)
    du_two[...] = jnp.zeros_like(du_two)
    layer_two(
        [start, start + 1], hot, ys, gp, u_two, mix_back, mix_fwd, columns, second_cat, second_parts,
        tk, gk, rk, v_one, v_two, dinv, du_two, dvec,
    )


def is_early(s):
    return s < 4


def early_kernel(packed, *refs):
    forms, rest = refs[0:8], refs[10:]

    @pl.when(is_early(whereabouts()[2]))
    def _():
        plane_work(packed, forms, *rest)


def late_kernel(packed, *refs):
    forms, rest = refs[0:8], refs[16:]

    @pl.when(jnp.logical_not(is_early(whereabouts()[2])))
    def _():
        plane_work(packed, forms, *rest)


def force_kernel(packed, across, moment, *refs):
    mix_back, mix_fwd, prj_all, columns, first_cat, first_parts, second_cat, second_parts = refs[0:8]
    out, hot, ys, gp, mom_one, slope_one, u_two, du_two, dvec, pk, tk, gk, rk, v_one, v_two, dinv = refs[16:]
    _, side, _ = whereabouts()
    low = lanes(8) < 64
    pk[pl.ds(3 - 2 * side, 4)] = packed[...]
    pk[pl.ds(4 * side + 1, 2)] = across[...]
    weights = (first_cat[...], mix_fwd[0], prj_all[1], columns[0], columns[1])
    halves = (2 + 3 * side, 3 * side, 2 + side, 5 * side, side)
    layer_one(pk, [1 + 3 * side, halves], weights, hot, ys, gp, mom_one, slope_one, u_two)
    layer_two(
        [1 + 2 * side, 2 + 2 * side], hot, ys, gp, u_two, mix_back, mix_fwd, columns, second_cat, second_parts,
        tk, gk, rk, v_one, v_two, dinv, du_two, dvec,
    )
    rate = rates()

    def third(du, slope, mom, gs, harmonics, pushes, spots):
        dh = columns[3] + dot3(prj_all[0], du)
        yield
        dinv = 2.0 * dot3(mix_back[0], dh * slope)
        yield
        parts = []
        for l in range(9):
            part = 0 if l == 0 else 1 if l < 4 else 2
            parts.append(mom(l) * dinv[part * 128 : (part + 1) * 128])
        dm = dot3(first_parts[...], jnp.concatenate(parts, axis=1))
        yield
        dm = [dm[:, l * 128 : (l + 1) * 128] for l in range(9)]
        rate2 = jnp.concatenate([rate, rate], axis=0)
        back = None
        centre = None
        for k in range(4):
            g, yk, push = gs(k), harmonics(k), pushes(k)
            dg = dm[0]
            dys = []
            for l in range(1, 9):
                dg = dg + yk[l - 1 : l] * dm[l]
                dys.append(jnp.sum(g * dm[l], axis=0, keepdims=True))
            dq = -jnp.sum(rate2 * g * dg, axis=0, keepdims=True)
            x, y, z = yk[0:1], yk[1:2], yk[2:3]
            e1, e2, e3, e4, e5, e6, e7, e8 = dys
            dx = e1 + ROOT3 * (y * e4 + z * e7 + x * e8) + x * (2.0 * dq - e6)
            dy = e2 + ROOT3 * (x * e4 + z * e5 - y * e8) + y * (2.0 * dq - e6)
            dz = e3 + ROOT3 * (y * e5 + x * e7) + 2.0 * z * (dq + e6)
            d = push + jnp.concatenate([dx, dy, dz, jnp.zeros((5, 128), F32)], axis=0)
            centre = d if centre is None else centre + d
            d_high = d.astype(BF16).astype(F32)
            rows = jnp.concatenate([d_high, d - d_high], axis=0).astype(BF16)
            term = dot_t(rows, spots(k))
            back = term if back is None else back + term
            yield
        return back[0:8] + back[8:16], centre

    def own_tile(t):
        return third(
            du_two[t], slope_one[t], lambda l: mom_one[t, l], lambda k: gp[t, k], lambda k: ys[t, k],
            lambda k: dvec[t, k], lambda k: hot[t, :, k * 128 : (k + 1) * 128],
        )

    def mixed(ref, *at):
        right, left = ref[(4,) + at], ref[(1,) + at]
        keep = lax.broadcasted_iota(jnp.int32, right.shape, 1) < 64
        return jnp.where(keep, right, left)

    def mixed_spots(k):
        at = (slice(128, 256), slice(k * 128, (k + 1) * 128))
        keep = lanes(128) < 64
        return jnp.where(keep, hot[(4,) + at].astype(F32), hot[(1,) + at].astype(F32)).astype(BF16)

    rim = third(
        mixed(du_two), mixed(slope_one), lambda l: mixed(mom_one, l), lambda k: mixed(gp, k), lambda k: mixed(ys, k),
        lambda k: mixed(dvec, k), mixed_spots,
    )
    (back2, centre2), (back3, centre3), (rim, _) = abreast([own_tile(2), own_tile(3), rim])
    f2 = centre2 - back2[:, 0:128] - jnp.where(low, rim, back3[:, 128:256])
    f3 = centre3 - back3[:, 0:128] - jnp.where(low, back2[:, 128:256], rim)
    row = lax.broadcasted_iota(jnp.int32, (8, 128), 0)
    for t, f in enumerate((f2, f3)):
        coords, drift = pk[t + 3, 0:8], pltpu.roll(moment[t], 3, 0)
        out[2 * t] = jnp.where(row < 3, jnp.where(low, f, turn(coords)), drift)
        out[2 * t + 1] = jnp.where(row < 3, jnp.where(low, turn(f), coords), turn(drift))


def finish_kernel(got, pos_out, mom_out, force_out):
    _, side, _ = whereabouts()
    for b in range(4):
        block = got[b ^ (2 * side)]
        turned = turn(block)
        for c in range(3):
            force = block[c : c + 1, 0:64]
            pos_out[c, b : b + 1] = turned[c : c + 1, 0:64]
            mom_out[c, b : b + 1] = block[3 + c : 4 + c, 0:64] + 0.5 * force
            force_out[c, b : b + 1] = force


def shape(*dims):
    return jax.ShapeDtypeStruct(dims, F32)


def room(mib):
    return pltpu.CompilerParams(vmem_limit_bytes=mib << 20)


def near(*dims, dtype=F32):
    return pltpu.VMEM(dims, dtype)


def far(x):
    return pltpu.with_memory_space_constraint(x, pltpu.HBM)


def keep(x):
    return pltpu.with_memory_space_constraint(x, pltpu.VMEM)


def on_device(
    positions, momenta, forces, species, neighbours, counts, ghost_rows,
    embed, radial_one, radial_two, mix_one, mix_two, projection, readout,
):
    count = lax.axis_size("space")
    both = ("bead", "space")
    planes = [[b * count + z * 8 + i for b in range(4) for i in range(8)] for z in range(count // 8)]
    quads = [[b * count + h * 4 + i for i in range(4)] for b in range(4) for h in range(count // 4)]
    beside = []
    for b in range(4):
        for z in range(count // 8):
            for i in range(4):
                here = b * count + z * 8 + i
                back = b * count + (z * 8 - 4) % count + (i ^ 2)
                beside += [(here, back), (back, here)]

    turned = [jnp.transpose(x, (1, 0, 2)) for x in (positions, momenta, forces)]
    sent = pl.pallas_call(
        pack_kernel, out_shape=shape(32, 8, 128), in_specs=[VM] * 8, out_specs=VM, name="pack",
    )(*[far(x) for x in (jnp.asarray(mode_tables()), *turned, species[None, :], neighbours, counts, ghost_rows)])
    got = keep(lax.all_to_all(sent, both, 0, 0, axis_index_groups=planes))
    forms = pl.pallas_call(
        forms_kernel,
        out_shape=(
            near(2, 384, 384, dtype=BF16), near(2, 128, 1152, dtype=BF16),
            near(2, 128, 384, dtype=BF16), near(4, 128, 128), near(128, 48, dtype=BF16),
            near(16, 384, dtype=BF16), near(128, 32, dtype=BF16), near(8, 384, dtype=BF16),
        ),
        in_specs=[pl.BlockSpec(memory_space=pl.ANY)] + [VM] * 7,
        out_specs=(VM,) * 8,
        compiler_params=room(8),
        cost_estimate=pl.CostEstimate(flops=2_000_000_000, bytes_accessed=4_000_000, transcendentals=0),
        name="forms",
    )(*[far(x) for x in (sent, embed, radial_one, radial_two, mix_one, mix_two, projection, readout)])
    packed, own, moment = pl.pallas_call(
        modes_kernel,
        out_shape=(near(4, 16, 128), near(2, 16, 128), near(2, 8, 128)),
        in_specs=[VM],
        out_specs=(VM,) * 3,
        compiler_params=room(16),
        name="modes",
    )(got)
    kept = (
        near(TILES, 256, 512, dtype=BF16),
        near(TILES, 4, 8, 128),
        near(TILES, 4, 16, 128),
        near(TILES, 9, 128, 128),
        near(TILES, 128, 128),
        near(TILES, 128, 128),
        near(TILES, 128, 128),
        near(TILES, 4, 8, 128),
    )

    def scratch():
        return [near(8, 16, 128)] + [near(2, 4, 128, 128)] * 5 + [near(2, 384, 128)]

    own, *state = pl.pallas_call(
        early_kernel,
        out_shape=(near(2, 16, 128),) + kept,
        in_specs=[VM] * 10,
        out_specs=(VM,) * 9,
        scratch_shapes=scratch(),
        input_output_aliases={9: 0},
        compiler_params=room(24),
        name="early",
    )(packed, *forms, own)
    across = keep(lax.ppermute(own, both, beside))
    state = pl.pallas_call(
        late_kernel,
        out_shape=kept,
        in_specs=[VM] * 17,
        out_specs=(VM,) * 8,
        scratch_shapes=scratch(),
        input_output_aliases={9 + i: i for i in range(8)},
        compiler_params=room(24),
        cost_estimate=pl.CostEstimate(flops=4_000_000_000, bytes_accessed=8_000_000, transcendentals=0),
        name="late",
    )(packed, *forms, *state)
    grad = pl.pallas_call(
        force_kernel,
        out_shape=(near(4, 8, 128),) + kept,
        in_specs=[VM] * 19,
        out_specs=(VM,) * 9,
        scratch_shapes=scratch(),
        input_output_aliases={11 + i: 1 + i for i in range(8)},
        compiler_params=room(24),
        name="force",
    )(packed, across, moment, *forms, *state)[0]
    back = keep(lax.all_to_all(grad, both, 0, 0, axis_index_groups=quads))
    outs = pl.pallas_call(
        finish_kernel,
        out_shape=(shape(3, 4, 64),) * 3,
        in_specs=[VM],
        out_specs=(VM,) * 3,
        compiler_params=room(8),
        name="finish",
    )(back)
    return tuple(jnp.transpose(x, (1, 0, 2)) for x in outs)


def solution(mesh):
    spread = P("bead", None, "space")
    placed = (
        spread, spread, spread, P("space"), spread, P("bead", "space"), P("space", None, None),
    ) + (P(),) * 7
    return jax.shard_map(
        on_device, mesh=mesh, in_specs=placed, out_specs=(spread,) * 3, check_vma=False
    )
```

```python
import numpy as np

import jax
import jax.numpy as jnp
from jax import lax
from jax.experimental import pallas as pl
from jax.experimental.pallas import tpu as pltpu
from jax.sharding import PartitionSpec as P


F32 = jnp.float32
BF16 = jnp.bfloat16
BEADS = 16
TILES = 6
ROOT3 = float(np.sqrt(3.0))
VM = pl.BlockSpec(memory_space=pltpu.VMEM)
RATES = 0.25 * 16.0 ** (np.arange(8) / 7.0)


def propagators():
    n = BEADS
    b = np.arange(n)
    phase = 2.0 * np.pi * np.outer(b, b) / n
    matrix = np.where(b[None] < n // 2, np.cos(phase), np.sin(phase)) * np.sqrt(2.0 / n)
    matrix[:, n // 2] = np.where(b % 2 == 0, 1.0, -1.0) / np.sqrt(n)
    matrix[:, 0] = 1.0 / np.sqrt(n)
    w = 1.5 * np.sin(np.pi * b / n)
    drift = np.where(b == 0, 1.0, np.sin(w) / np.where(b == 0, 1.0, w))
    return [(matrix * d) @ matrix.T for d in (np.cos(w), drift, w * np.sin(w))]


def mode_tables():
    cosine, drift, stiff = propagators()
    rows = np.zeros((4, 4, 64, 16))
    for sender in range(4):
        for bead in range(BEADS):
            for c in range(3):
                for b in range(4):
                    for n, values in enumerate((cosine, drift, cosine, stiff)):
                        rows[sender, n, 4 * bead + c, 4 * c + b] = values[bead, 4 * sender + b]
    rows = rows.astype(np.float32).reshape(4, 2, 128, 16)
    one = rows.astype(BF16)
    two = (rows - one.astype(np.float32)).astype(BF16)
    three = (rows - one.astype(np.float32) - two.astype(np.float32)).astype(BF16)
    return np.concatenate([one, one, two, two, one, three], axis=-1)


def parts_of(x):
    one = x.astype(BF16)
    rest = x - one.astype(F32)
    two = rest.astype(BF16)
    three = (rest - two.astype(F32)).astype(BF16)
    return jnp.concatenate([one, two, one, two, three, one], axis=0)

def split(x):
    high = x.astype(BF16)
    return high, (x - high.astype(F32)).astype(BF16)


def dot(a, b):
    return lax.dot_general(a, b, (((1,), (0,)), ((), ())), preferred_element_type=F32)


def dot_t(a, b):
    return lax.dot_general(a, b, (((1,), (1,)), ((), ())), preferred_element_type=F32)


def thrice(x):
    high, lo = split(x)
    return jnp.concatenate([high, high, lo], axis=1)


def dot3(a, b):
    high, lo = split(b)
    return dot(a, jnp.concatenate([high, lo, high], axis=0))


def lanes(rows):
    return lax.broadcasted_iota(jnp.int32, (rows, 128), 1)


def turn(x):
    return pltpu.roll(x, 64, 1)


def pick(y):
    return (y % 4) ^ (2 * (y // 4))


def whereabouts():
    s = lax.axis_index("space")
    return lax.axis_index("bead"), (s & 7) >> 2, s


def pack_kernel(table, pos, mom, force, species, nbr, counts, ghost, out):
    r, _, _ = whereabouts()
    low = lanes(64) < 64
    kind = species[...].astype(F32)
    mass = 1.0 + 15.0 * kind
    blank = jnp.zeros((4, 64), F32)
    coords = jnp.concatenate([pos[0], pos[1], pos[2], blank], axis=0)
    kicked = jnp.concatenate([mom[c] + 0.5 * force[c] for c in range(3)] + [blank], axis=0)
    moved = dot(table[r, 0], parts_of(jnp.concatenate([coords, kicked / mass], axis=1)))
    driven = dot(table[r, 1], parts_of(jnp.concatenate([mass * coords, kicked], axis=1)))
    shares = jnp.where(low, moved[0:64] + turn(moved[64:128]), driven[0:64] - turn(driven[64:128]))
    ghosts = ghost[0].astype(F32)
    last = jnp.concatenate([ghosts[0:1], ghosts[1:2], jnp.zeros((1, 96), F32)], axis=1)
    row = lax.broadcasted_iota(jnp.int32, (8, 128), 0)
    for bead in range(4):
        e = nbr[bead].astype(F32)
        info = jnp.concatenate(
            [
                jnp.zeros((3, 128), F32),
                jnp.concatenate([counts[bead : bead + 1].astype(F32), kind], axis=1),
                jnp.concatenate([e[0:1], e[1:2]], axis=1),
                jnp.concatenate([e[2:3], e[3:4]], axis=1),
                last,
                jnp.zeros((1, 128), F32),
            ],
            axis=0,
        )
        for to in range(4):
            n = (4 * to + bead) // 2
            share = shares[8 * n : 8 * n + 8]
            if bead % 2:
                share = pltpu.roll(share, 4, 0)
            block = jnp.where(row < 3, share, info)
            for y in range(8):
                if pick(y) == bead:
                    out[to * 8 + y] = block


def modes_kernel(got, packed, own, moment):
    r, side, _ = whereabouts()
    low = lanes(8) < 64
    row = lax.broadcasted_iota(jnp.int32, (8, 128), 0)
    moments = []
    for t in range(4):
        even, odd = (
            (got[d] + got[8 + d]) + (got[16 + d] + got[24 + d]) for d in (2 * t, 2 * t + 1)
        )
        info_even, info_odd = got[r * 8 + 2 * t], got[r * 8 + 2 * t + 1]
        left = jnp.where(low, info_even, turn(info_odd))
        right = jnp.where(low, turn(info_even), info_odd)
        coords = jnp.where(low, even, turn(odd))
        moments.append(jnp.where(low, turn(even), odd))
        packed[t, 0:8] = jnp.where(row < 3, coords, jnp.broadcast_to(right[3:4], (8, 128)))
        packed[t, 8:16] = jnp.where(row < 3, pltpu.roll(right, 5, 0), left)
    for t in range(2):
        moment[t] = jnp.where(side == 1, moments[2 + t], moments[t])
    own[...] = packed[pl.ds(2 * side, 2)]


ORDER = ((0, 0), (0, 1), (1, 0), (2, 0), (1, 1), (3, 0), (2, 1), (3, 1))


def rates():
    row = lax.broadcasted_iota(jnp.int32, (8, 128), 0)
    rate = jnp.zeros((8, 128), F32)
    for n in range(8):
        rate = jnp.where(row == n, float(RATES[n]), rate)
    return rate


def abreast(jobs):
    results = [None] * len(jobs)
    left = list(range(len(jobs)))
    while left:
        for n in list(left):
            try:
                next(jobs[n])
            except StopIteration as stop:
                results[n] = stop.value
                left.remove(n)
    return results


def sigmoid(v):
    return 1.0 / (1.0 + jnp.exp(-v))


def layer_one(pk, jobs, weights, hot, ys, gp, mom_one, slope_one, u_two):
    w_one_cat, mix1_t, prj_t, base_col, step_col = weights
    low = lanes(8) < 64
    low1 = lanes(1) < 64
    head = lanes(1) < 16
    rate = rates()
    spot = lax.broadcasted_iota(jnp.int32, (256, 128), 0).astype(F32)
    ghost_spot = lax.broadcasted_iota(jnp.int32, (32, 128), 0).astype(F32) + 64.0

    def thirds(wide):
        a = wide.astype(BF16).astype(F32)
        b = (wide - a).astype(BF16).astype(F32)
        c = (wide - a - b).astype(BF16).astype(F32)
        return jnp.concatenate([a, b, c, jnp.zeros((8, 256), F32)], axis=0)

    def one(job):
        whole = not isinstance(job, tuple)
        lower, upper, t, outer, mask = (job, job, job, None, None) if whole else job

        def put(ref, at, value):
            if mask is not None:
                rows = value.shape[0]
                mine = jnp.where(lanes(rows) < 64, 0, 1) == mask
                value = jnp.where(mine, value, ref[at].astype(F32))
            ref[at] = value.astype(ref.dtype)

        here_low, info = pk[lower + 1, 0:8], pk[lower + 1, 8:16]
        g_prev, g_low, g_high, g_next = (pk[n, 14:15] for n in (lower, lower + 1, upper + 1, upper + 2))
        beside = jnp.where(low, pk[upper + 2, 0:8], pk[lower, 0:8])
        parts = thirds(jnp.concatenate([here_low, beside], axis=1))
        here = here_low
        if not whole:
            here_high = pk[upper + 1, 0:8]
            here = jnp.where(low, here_low, here_high)
            info = jnp.where(low, info, pk[upper + 1, 8:16])
            parts = jnp.concatenate([parts, thirds(jnp.concatenate([here_high, beside], axis=1))], axis=0)
        parts = parts.astype(BF16)
        table = jnp.concatenate(
            [
                jnp.where(head, turn(g_prev) + 192.0, turn(g_low) + 64.0),
                jnp.where(head, g_high, g_next + 128.0),
                jnp.zeros((14, 128), F32),
            ],
            axis=0,
        )[:, 0:32].astype(BF16)
        count = info[3:4]
        sums = [None] * 9
        for k, row in enumerate((4, 1, 5, 2)):
            e = info[row : row + 1]
            hit = jnp.where(ghost_spot == e, 1.0, 0.0).astype(BF16)
            far = dot(table, hit)
            n = jnp.where(
                e < 64.0, e + jnp.where(low1, 0.0, 64.0), jnp.where(low1, far[0:1], far[1:2])
            )
            one_hot = jnp.where(spot == n, 1.0, 0.0)
            put(hot, (t, slice(None), slice(k * 128, (k + 1) * 128)), one_hot)
            got = dot(parts, one_hot.astype(BF16))
            there = got[0:8] + (got[8:16] + got[16:24])
            if not whole:
                there = jnp.where(low, there, got[32:40] + (got[40:48] + got[48:56]))
            off = there - here
            x, y, z = off[0:1], off[1:2], off[2:3]
            q = x * x + y * y + z * z
            live = jnp.where(count > float(k), 0.25, 0.0)
            g = jnp.exp(-rate * q) * live
            both = jnp.concatenate([g, g * there[3:4]], axis=0)
            harmonic = [
                None, x, y, z, ROOT3 * x * y, ROOT3 * y * z, 0.5 * (3.0 * z * z - q), ROOT3 * x * z,
                (0.5 * ROOT3) * (x * x - y * y),
            ]
            put(gp, (t, k), both)
            put(ys, (t, k), jnp.concatenate(harmonic[1:9], axis=0))
            for l in range(9):
                term = both if l == 0 else harmonic[l] * both
                sums[l] = term if sums[l] is None else sums[l] + term
            yield
        high, lo = split(jnp.concatenate(sums, axis=1))
        moments = dot(w_one_cat, jnp.concatenate([high, lo, high], axis=0))
        yield
        m = [moments[:, l * 128 : (l + 1) * 128] for l in range(9)]
        for l in range(9):
            put(mom_one, (t, l), m[l])
        inv = jnp.concatenate(
            [m[0] * m[0], sum(m[l] * m[l] for l in (1, 2, 3)), sum(m[l] * m[l] for l in range(4, 9))],
            axis=0,
        )
        v = dot3(mix1_t, inv)
        yield
        sig = sigmoid(v)
        put(slope_one, (t,), sig * (1.0 + v * (1.0 - sig)))
        h = base_col + here[3:4] * step_col + v * sig
        u = dot3(prj_t, h)
        put(u_two, (t,), u)
        if outer is not None:
            u_two[outer] = u
        yield

    abreast([one(job) for job in jobs])


def forms_kernel(
    sent, embed, radial_one, radial_two, mix_one, mix_two, proj, readout,
    mix_back, mix_fwd, prj_all, columns, first_cat, first_parts, second_cat, second_parts,
):
    del sent

    def column(row):
        return jnp.broadcast_to(row, (128, 128)).T

    columns[0] = column(embed[0:1])
    columns[1] = column(embed[1:2] - embed[0:1])
    columns[2] = column(readout[1:2])
    columns[3] = column(readout[0:1] + readout[1:2])
    for n, mix in enumerate((mix_one, mix_two)):
        mix_back[n] = thrice(mix[...])
        mix_fwd[n] = thrice(mix[...].T)
    prj_all[0] = thrice(proj[...])
    prj_all[1] = thrice(proj[...].T)
    base, step = embed[0:1], embed[1:2] - embed[0:1]
    high, lo = split(jnp.concatenate([radial_one[...] * base, radial_one[...] * step], axis=0))
    first_parts[...] = jnp.concatenate([high, high, lo], axis=1)
    first_cat[...] = jnp.concatenate([high, high, lo], axis=0).astype(F32).T.astype(BF16)
    high, lo = split(radial_two[...])
    second_parts[...] = jnp.concatenate([high, high, lo], axis=1)
    high, lo = high.astype(F32), lo.astype(F32)
    second_cat[...] = jnp.concatenate([high, high, lo, jnp.zeros((8, 128), F32)], axis=0).T.astype(BF16)


def nodes_of_edges(t, m, hot, gp, u_two, second_cat, tk, gk, rk):
    low_wide = lanes(128) < 64
    beside = jnp.where(low_wide, u_two[t + 1], u_two[t - 1])
    high, lo = split(jnp.concatenate([u_two[t], beside], axis=1))
    parts = jnp.concatenate([high, lo], axis=0)
    for k in range(4):
        got = dot(parts, hot[t, :, k * 128 : (k + 1) * 128])
        nodes = got[0:128] + got[128:256]
        g = gp[t, k, 0:8]
        gh = g.astype(BF16).astype(F32)
        rows = jnp.concatenate([gh, g - gh, gh, jnp.zeros((8, 128), F32)], axis=0).astype(BF16)
        weight = dot(second_cat[...], rows)
        gk[m, k] = nodes
        rk[m, k] = weight
        tk[m, k] = nodes * weight


def edge_sums(t, ys):
    edge = [[ys[t, k, c : c + 1] for c in range(3)] for k in range(4)]
    scalar, legendre = {}, {}
    for i in range(4):
        for j in range(i, 4):
            scalar[i, j] = scalar[j, i] = sum(edge[i][c] * edge[j][c] for c in range(3))
    for i in range(4):
        for j in range(i, 4):
            legendre[i, j] = legendre[j, i] = 1.5 * scalar[i, j] * scalar[i, j] - 0.5 * scalar[i, i] * scalar[j, j]
    return edge, scalar, legendre


def invariants_two(t, m, ys, tk, v_one, v_two):
    _, scalar, legendre = edge_sums(t, ys)
    total = (tk[m, 0] + tk[m, 1]) + (tk[m, 2] + tk[m, 3])
    inv1 = inv2 = None
    for i in range(4):
        va = sum(scalar[i, j] * tk[m, j] for j in range(4))
        vb = sum(legendre[i, j] * tk[m, j] for j in range(4))
        v_one[m, i], v_two[m, i] = va, vb
        inv1 = va * tk[m, i] if inv1 is None else inv1 + va * tk[m, i]
        inv2 = vb * tk[m, i] if inv2 is None else inv2 + vb * tk[m, i]
    return jnp.concatenate([total * total, inv1, inv2], axis=0)


def mixing_back(m, inv, mix_back, mix_fwd, columns, dinv):
    v = dot3(mix_fwd[1], inv)
    sig = sigmoid(v)
    dv = columns[2] * (sig * (1.0 + v * (1.0 - sig)))
    dinv[m] = 2.0 * dot3(mix_back[1], dv)


def edges_back(t, m, hot, ys, gp, second_parts, tk, gk, rk, v_one, v_two, dinv, du_two, dvec):
    low_wide = lanes(128) < 64
    edge, scalar, _ = edge_sums(t, ys)
    rate = rates()
    d1, d2 = dinv[m, 128:256], dinv[m, 256:384]
    d0 = dinv[m, 0:128] * ((tk[m, 0] + tk[m, 1]) + (tk[m, 2] + tk[m, 3]))
    pull, bend = {}, {}
    for i in range(4):
        wa, wb = d1 * tk[m, i], d2 * tk[m, i]
        for j in range(i, 4):
            pull[i, j] = pull[j, i] = jnp.sum(wa * tk[m, j], axis=0, keepdims=True)
            bend[i, j] = bend[j, i] = jnp.sum(wb * tk[m, j], axis=0, keepdims=True)
    back = []
    for k in range(4):
        dt = d0 + d1 * v_one[m, k] + d2 * v_two[m, k]
        dg = dot3(second_parts[...], dt * gk[m, k])
        back.append(jnp.concatenate(split(dt * rk[m, k]), axis=0))
        dq = 0.5 * pull[k, k] + bend[k, k] * scalar[k, k] - jnp.sum(rate * gp[t, k, 0:8] * dg, axis=0, keepdims=True)
        d = [None] * 3
        for j in range(4):
            if j != k:
                dq = dq - 0.5 * bend[k, j] * scalar[j, j]
                tie = pull[k, j] + 3.0 * bend[k, j] * scalar[k, j]
                d = [tie * edge[j][c] if d[c] is None else d[c] + tie * edge[j][c] for c in range(3)]
        d = [d[c] + 2.0 * dq * edge[k][c] for c in range(3)]
        dvec[t, k] = jnp.concatenate(d + [jnp.zeros((5, 128), F32)], axis=0)
    back = dot_t(jnp.concatenate(back, axis=1), hot[t])
    back = back[0:128] + back[128:256]
    du_two[t] += back[:, 0:128]
    aside = back[:, 128:256]
    du_two[t + 1] += jnp.where(low_wide, aside, 0.0)
    du_two[t - 1] += jnp.where(low_wide, 0.0, aside)


def layer_two(
    tiles, hot, ys, gp, u_two, mix_back, mix_fwd, columns, second_cat, second_parts,
    tk, gk, rk, v_one, v_two, dinv, du_two, dvec,
):
    inv = {}
    for stage, m in ORDER:
        t = tiles[m]
        if stage == 0:
            nodes_of_edges(t, m, hot, gp, u_two, second_cat, tk, gk, rk)
        elif stage == 1:
            inv[m] = invariants_two(t, m, ys, tk, v_one, v_two)
        elif stage == 2:
            mixing_back(m, inv[m], mix_back, mix_fwd, columns, dinv)
        else:
            edges_back(t, m, hot, ys, gp, second_parts, tk, gk, rk, v_one, v_two, dinv, du_two, dvec)


def plane_first(packed, forms, pk, *state):
    mix_fwd, prj_all, columns, first_cat = forms[1:5]
    _, side, _ = whereabouts()
    pk[pl.ds(3 - 2 * side, 4)] = packed[...]
    weights = (first_cat[...], mix_fwd[0], prj_all[1], columns[0], columns[1])
    start = 3 - 2 * side
    halves = (5 - 2 * side, 2 - 2 * side, 2 + side, 5 - 5 * side, None)
    layer_one(pk, [start, start + 1, halves], weights, *state)


def plane_second(forms, hot, ys, gp, u_two, du_two, dvec, *scratch):
    mix_back, mix_fwd, _, columns, _, _, second_cat, second_parts = forms
    _, side, _ = whereabouts()
    du_two[...] = jnp.zeros_like(du_two)
    layer_two(
        [3 - 2 * side, 4 - 2 * side], hot, ys, gp, u_two, mix_back, mix_fwd, columns, second_cat, second_parts,
        *scratch, du_two, dvec,
    )


def is_early(s):
    return s < 4


def early_kernel(packed, *refs):
    forms, state, pk = refs[0:8], refs[10:16], refs[16]

    @pl.when(is_early(whereabouts()[2]))
    def _():
        plane_first(packed, forms, pk, *state)


def late_kernel(packed, *refs):
    forms = refs[0:8]
    hot, ys, gp, mom_one, slope_one, u_two, du_two, dvec, pk = refs[14:23]

    @pl.when(jnp.logical_not(is_early(whereabouts()[2])))
    def _():
        plane_first(packed, forms, pk, hot, ys, gp, mom_one, slope_one, u_two)

    plane_second(forms, hot, ys, gp, u_two, du_two, dvec, *refs[23:])


def force_kernel(packed, across, moment, *refs):
    mix_back, mix_fwd, prj_all, columns, first_cat, first_parts, second_cat, second_parts = refs[0:8]
    out, hot, ys, gp, mom_one, slope_one, u_two, du_two, dvec, pk, tk, gk, rk, v_one, v_two, dinv = refs[16:]
    _, side, _ = whereabouts()
    low = lanes(8) < 64
    pk[pl.ds(3 - 2 * side, 4)] = packed[...]
    pk[pl.ds(4 * side + 1, 2)] = across[...]
    weights = (first_cat[...], mix_fwd[0], prj_all[1], columns[0], columns[1])
    halves = (2 + 3 * side, 3 * side, 2 + side, 5 * side, side)
    layer_one(pk, [1 + 3 * side, halves], weights, hot, ys, gp, mom_one, slope_one, u_two)
    layer_two(
        [1 + 2 * side, 2 + 2 * side], hot, ys, gp, u_two, mix_back, mix_fwd, columns, second_cat, second_parts,
        tk, gk, rk, v_one, v_two, dinv, du_two, dvec,
    )
    rate = rates()

    def third(du, slope, mom, gs, harmonics, pushes, spots):
        dh = columns[3] + dot3(prj_all[0], du)
        yield
        dinv = 2.0 * dot3(mix_back[0], dh * slope)
        yield
        parts = []
        for l in range(9):
            part = 0 if l == 0 else 1 if l < 4 else 2
            parts.append(mom(l) * dinv[part * 128 : (part + 1) * 128])
        dm = dot3(first_parts[...], jnp.concatenate(parts, axis=1))
        yield
        dm = [dm[:, l * 128 : (l + 1) * 128] for l in range(9)]
        rate2 = jnp.concatenate([rate, rate], axis=0)
        back = None
        centre = None
        for k in range(4):
            g, yk, push = gs(k), harmonics(k), pushes(k)
            dg = dm[0]
            dys = []
            for l in range(1, 9):
                dg = dg + yk[l - 1 : l] * dm[l]
                dys.append(jnp.sum(g * dm[l], axis=0, keepdims=True))
            dq = -jnp.sum(rate2 * g * dg, axis=0, keepdims=True)
            x, y, z = yk[0:1], yk[1:2], yk[2:3]
            e1, e2, e3, e4, e5, e6, e7, e8 = dys
            dx = e1 + ROOT3 * (y * e4 + z * e7 + x * e8) + x * (2.0 * dq - e6)
            dy = e2 + ROOT3 * (x * e4 + z * e5 - y * e8) + y * (2.0 * dq - e6)
            dz = e3 + ROOT3 * (y * e5 + x * e7) + 2.0 * z * (dq + e6)
            d = push + jnp.concatenate([dx, dy, dz, jnp.zeros((5, 128), F32)], axis=0)
            centre = d if centre is None else centre + d
            d_high = d.astype(BF16).astype(F32)
            rows = jnp.concatenate([d_high, d - d_high], axis=0).astype(BF16)
            term = dot_t(rows, spots(k))
            back = term if back is None else back + term
            yield
        return back[0:8] + back[8:16], centre

    def own_tile(t):
        return third(
            du_two[t], slope_one[t], lambda l: mom_one[t, l], lambda k: gp[t, k], lambda k: ys[t, k],
            lambda k: dvec[t, k], lambda k: hot[t, :, k * 128 : (k + 1) * 128],
        )

    def mixed(ref, *at):
        right, left = ref[(4,) + at], ref[(1,) + at]
        keep = lax.broadcasted_iota(jnp.int32, right.shape, 1) < 64
        return jnp.where(keep, right, left)

    def mixed_spots(k):
        at = (slice(128, 256), slice(k * 128, (k + 1) * 128))
        keep = lanes(128) < 64
        return jnp.where(keep, hot[(4,) + at].astype(F32), hot[(1,) + at].astype(F32)).astype(BF16)

    rim = third(
        mixed(du_two), mixed(slope_one), lambda l: mixed(mom_one, l), lambda k: mixed(gp, k), lambda k: mixed(ys, k),
        lambda k: mixed(dvec, k), mixed_spots,
    )
    (back2, centre2), (back3, centre3), (rim, _) = abreast([own_tile(2), own_tile(3), rim])
    f2 = centre2 - back2[:, 0:128] - jnp.where(low, rim, back3[:, 128:256])
    f3 = centre3 - back3[:, 0:128] - jnp.where(low, back2[:, 128:256], rim)
    row = lax.broadcasted_iota(jnp.int32, (8, 128), 0)
    for t, f in enumerate((f2, f3)):
        coords, drift = pk[t + 3, 0:8], pltpu.roll(moment[t], 3, 0)
        out[2 * t] = jnp.where(row < 3, jnp.where(low, f, turn(coords)), drift)
        out[2 * t + 1] = jnp.where(row < 3, jnp.where(low, turn(f), coords), turn(drift))


def finish_kernel(got, pos_out, mom_out, force_out):
    _, side, _ = whereabouts()
    for b in range(4):
        block = got[b ^ (2 * side)]
        turned = turn(block)
        for c in range(3):
            force = block[c : c + 1, 0:64]
            pos_out[c, b : b + 1] = turned[c : c + 1, 0:64]
            mom_out[c, b : b + 1] = block[3 + c : 4 + c, 0:64] + 0.5 * force
            force_out[c, b : b + 1] = force


def shape(*dims):
    return jax.ShapeDtypeStruct(dims, F32)


def room(mib):
    return pltpu.CompilerParams(vmem_limit_bytes=mib << 20)


def near(*dims, dtype=F32):
    return pltpu.VMEM(dims, dtype)


def far(x):
    return pltpu.with_memory_space_constraint(x, pltpu.HBM)


def keep(x):
    return pltpu.with_memory_space_constraint(x, pltpu.VMEM)


def on_device(
    positions, momenta, forces, species, neighbours, counts, ghost_rows,
    embed, radial_one, radial_two, mix_one, mix_two, projection, readout,
):
    count = lax.axis_size("space")
    both = ("bead", "space")
    planes = [[b * count + z * 8 + i for b in range(4) for i in range(8)] for z in range(count // 8)]
    quads = [[b * count + h * 4 + i for i in range(4)] for b in range(4) for h in range(count // 4)]
    beside = []
    for b in range(4):
        for z in range(count // 8):
            for i in range(4):
                here = b * count + z * 8 + i
                back = b * count + (z * 8 - 4) % count + (i ^ 2)
                beside += [(here, back), (back, here)]

    turned = [jnp.transpose(x, (1, 0, 2)) for x in (positions, momenta, forces)]
    sent = pl.pallas_call(
        pack_kernel, out_shape=shape(32, 8, 128), in_specs=[VM] * 8, out_specs=VM, name="pack",
    )(*[far(x) for x in (jnp.asarray(mode_tables()), *turned, species[None, :], neighbours, counts, ghost_rows)])
    got = keep(lax.all_to_all(sent, both, 0, 0, axis_index_groups=planes))
    forms = pl.pallas_call(
        forms_kernel,
        out_shape=(
            near(2, 384, 384, dtype=BF16), near(2, 128, 1152, dtype=BF16),
            near(2, 128, 384, dtype=BF16), near(4, 128, 128), near(128, 48, dtype=BF16),
            near(16, 384, dtype=BF16), near(128, 32, dtype=BF16), near(8, 384, dtype=BF16),
        ),
        in_specs=[pl.BlockSpec(memory_space=pl.ANY)] + [VM] * 7,
        out_specs=(VM,) * 8,
        compiler_params=room(8),
        cost_estimate=pl.CostEstimate(flops=2_000_000_000, bytes_accessed=4_000_000, transcendentals=0),
        name="forms",
    )(*[far(x) for x in (sent, embed, radial_one, radial_two, mix_one, mix_two, projection, readout)])
    packed, own, moment = pl.pallas_call(
        modes_kernel,
        out_shape=(near(4, 16, 128), near(2, 16, 128), near(2, 8, 128)),
        in_specs=[VM],
        out_specs=(VM,) * 3,
        compiler_params=room(16),
        name="modes",
    )(got)
    kept = (
        near(TILES, 256, 512, dtype=BF16),
        near(TILES, 4, 8, 128),
        near(TILES, 4, 16, 128),
        near(TILES, 9, 128, 128),
        near(TILES, 128, 128),
        near(TILES, 128, 128),
        near(TILES, 128, 128),
        near(TILES, 4, 8, 128),
    )

    def scratch():
        return [near(8, 16, 128)] + [near(2, 4, 128, 128)] * 5 + [near(2, 384, 128)]

    own, *state = pl.pallas_call(
        early_kernel,
        out_shape=(near(2, 16, 128),) + kept[:6],
        in_specs=[VM] * 10,
        out_specs=(VM,) * 7,
        scratch_shapes=[near(8, 16, 128)],
        input_output_aliases={9: 0},
        compiler_params=room(24),
        name="early",
    )(packed, *forms, own)
    across = keep(lax.ppermute(own, both, beside))
    state = pl.pallas_call(
        late_kernel,
        out_shape=kept,
        in_specs=[VM] * 15,
        out_specs=(VM,) * 8,
        scratch_shapes=scratch(),
        input_output_aliases={9 + i: i for i in range(6)},
        compiler_params=room(24),
        cost_estimate=pl.CostEstimate(flops=4_000_000_000, bytes_accessed=8_000_000, transcendentals=0),
        name="late",
    )(packed, *forms, *state)
    grad = pl.pallas_call(
        force_kernel,
        out_shape=(near(4, 8, 128),) + kept,
        in_specs=[VM] * 19,
        out_specs=(VM,) * 9,
        scratch_shapes=scratch(),
        input_output_aliases={11 + i: 1 + i for i in range(8)},
        compiler_params=room(24),
        name="force",
    )(packed, across, moment, *forms, *state)[0]
    back = keep(lax.all_to_all(grad, both, 0, 0, axis_index_groups=quads))
    outs = pl.pallas_call(
        finish_kernel,
        out_shape=(shape(3, 4, 64),) * 3,
        in_specs=[VM],
        out_specs=(VM,) * 3,
        compiler_params=room(8),
        name="finish",
    )(back)
    return tuple(jnp.transpose(x, (1, 0, 2)) for x in outs)


def solution(mesh):
    spread = P("bead", None, "space")
    placed = (
        spread, spread, spread, P("space"), spread, P("bead", "space"), P("space", None, None),
    ) + (P(),) * 7
    return jax.shard_map(
        on_device, mesh=mesh, in_specs=placed, out_specs=(spread,) * 3, check_vma=False
    )
```

```python
import numpy as np

import jax
import jax.numpy as jnp
from jax import lax
from jax.experimental import pallas as pl
from jax.experimental.pallas import tpu as pltpu
from jax.sharding import PartitionSpec as P


F32 = jnp.float32
BF16 = jnp.bfloat16
BEADS = 16
TILES = 6
ROOT3 = float(np.sqrt(3.0))
VM = pl.BlockSpec(memory_space=pltpu.VMEM)
RATES = 0.25 * 16.0 ** (np.arange(8) / 7.0)


def propagators():
    n = BEADS
    b = np.arange(n)
    phase = 2.0 * np.pi * np.outer(b, b) / n
    matrix = np.where(b[None] < n // 2, np.cos(phase), np.sin(phase)) * np.sqrt(2.0 / n)
    matrix[:, n // 2] = np.where(b % 2 == 0, 1.0, -1.0) / np.sqrt(n)
    matrix[:, 0] = 1.0 / np.sqrt(n)
    w = 1.5 * np.sin(np.pi * b / n)
    drift = np.where(b == 0, 1.0, np.sin(w) / np.where(b == 0, 1.0, w))
    return [(matrix * d) @ matrix.T for d in (np.cos(w), drift, w * np.sin(w))]


def mode_tables():
    cosine, drift, stiff = propagators()
    rows = np.zeros((4, 4, 64, 16))
    for sender in range(4):
        for bead in range(BEADS):
            for c in range(3):
                for b in range(4):
                    for n, values in enumerate((cosine, drift, cosine, stiff)):
                        rows[sender, n, 4 * bead + c, 4 * c + b] = values[bead, 4 * sender + b]
    rows = rows.astype(np.float32).reshape(4, 2, 128, 16)
    one = rows.astype(BF16)
    two = (rows - one.astype(np.float32)).astype(BF16)
    three = (rows - one.astype(np.float32) - two.astype(np.float32)).astype(BF16)
    return np.concatenate([one, one, two, two, one, three], axis=-1)


def parts_of(x):
    one = x.astype(BF16)
    rest = x - one.astype(F32)
    two = rest.astype(BF16)
    three = (rest - two.astype(F32)).astype(BF16)
    return jnp.concatenate([one, two, one, two, three, one], axis=0)

def split(x):
    high = x.astype(BF16)
    return high, (x - high.astype(F32)).astype(BF16)


def dot(a, b):
    return lax.dot_general(a, b, (((1,), (0,)), ((), ())), preferred_element_type=F32)


def dot_t(a, b):
    return lax.dot_general(a, b, (((1,), (1,)), ((), ())), preferred_element_type=F32)


def thrice(x):
    high, lo = split(x)
    return jnp.concatenate([high, high, lo], axis=1)


def dot3(a, b):
    high, lo = split(b)
    return dot(a, jnp.concatenate([high, lo, high], axis=0))


def lanes(rows):
    return lax.broadcasted_iota(jnp.int32, (rows, 128), 1)


def turn(x):
    return pltpu.roll(x, 64, 1)


def pick(y):
    return (y % 4) ^ (2 * (y // 4))


def whereabouts():
    s = lax.axis_index("space")
    return lax.axis_index("bead"), (s & 7) >> 2, s


def pack_kernel(table, pos, mom, force, species, nbr, counts, ghost, out):
    r, _, _ = whereabouts()
    low = lanes(64) < 64
    kind = species[...].astype(F32)
    mass = 1.0 + 15.0 * kind
    blank = jnp.zeros((4, 64), F32)
    coords = jnp.concatenate([pos[0], pos[1], pos[2], blank], axis=0)
    kicked = jnp.concatenate([mom[c] + 0.5 * force[c] for c in range(3)] + [blank], axis=0)
    moved = dot(table[r, 0], parts_of(jnp.concatenate([coords, kicked / mass], axis=1)))
    driven = dot(table[r, 1], parts_of(jnp.concatenate([mass * coords, kicked], axis=1)))
    shares = jnp.where(low, moved[0:64] + turn(moved[64:128]), driven[0:64] - turn(driven[64:128]))
    ghosts = ghost[0].astype(F32)
    last = jnp.concatenate([ghosts[0:1], ghosts[1:2], jnp.zeros((1, 96), F32)], axis=1)
    row = lax.broadcasted_iota(jnp.int32, (8, 128), 0)
    for bead in range(4):
        e = nbr[bead].astype(F32)
        info = jnp.concatenate(
            [
                jnp.zeros((3, 128), F32),
                jnp.concatenate([counts[bead : bead + 1].astype(F32), kind], axis=1),
                jnp.concatenate([e[0:1], e[1:2]], axis=1),
                jnp.concatenate([e[2:3], e[3:4]], axis=1),
                last,
                jnp.zeros((1, 128), F32),
            ],
            axis=0,
        )
        for to in range(4):
            n = (4 * to + bead) // 2
            share = shares[8 * n : 8 * n + 8]
            if bead % 2:
                share = pltpu.roll(share, 4, 0)
            block = jnp.where(row < 3, share, info)
            for y in range(8):
                if pick(y) == bead:
                    out[to * 8 + y] = block


def modes_kernel(got, packed, own, moment):
    r, side, _ = whereabouts()
    low = lanes(8) < 64
    row = lax.broadcasted_iota(jnp.int32, (8, 128), 0)
    moments = []
    for t in range(4):
        even, odd = (
            (got[d] + got[8 + d]) + (got[16 + d] + got[24 + d]) for d in (2 * t, 2 * t + 1)
        )
        info_even, info_odd = got[r * 8 + 2 * t], got[r * 8 + 2 * t + 1]
        left = jnp.where(low, info_even, turn(info_odd))
        right = jnp.where(low, turn(info_even), info_odd)
        coords = jnp.where(low, even, turn(odd))
        moments.append(jnp.where(low, turn(even), odd))
        packed[t, 0:8] = jnp.where(row < 3, coords, jnp.broadcast_to(right[3:4], (8, 128)))
        packed[t, 8:16] = jnp.where(row < 3, pltpu.roll(right, 5, 0), left)
    for t in range(2):
        moment[t] = jnp.where(side == 1, moments[2 + t], moments[t])
    own[...] = packed[pl.ds(2 * side, 2)]


ORDER = ((0, 0), (0, 1), (1, 0), (1, 1), (2, 0), (2, 1), (3, 0), (3, 1))


def rates():
    row = lax.broadcasted_iota(jnp.int32, (8, 128), 0)
    rate = jnp.zeros((8, 128), F32)
    for n in range(8):
        rate = jnp.where(row == n, float(RATES[n]), rate)
    return rate


def abreast(jobs):
    results = [None] * len(jobs)
    left = list(range(len(jobs)))
    while left:
        for n in list(left):
            try:
                next(jobs[n])
            except StopIteration as stop:
                results[n] = stop.value
                left.remove(n)
    return results


def sigmoid(v):
    return 1.0 / (1.0 + jnp.exp(-v))


def layer_one(pk, jobs, weights, hot, ys, gp, mom_one, slope_one, u_two):
    w_one_cat, mix1_t, prj_t, base_col, step_col = weights
    low = lanes(8) < 64
    low1 = lanes(1) < 64
    head = lanes(1) < 16
    rate = rates()
    spot = lax.broadcasted_iota(jnp.int32, (256, 128), 0).astype(F32)
    ghost_spot = lax.broadcasted_iota(jnp.int32, (32, 128), 0).astype(F32) + 64.0

    def thirds(wide):
        a = wide.astype(BF16).astype(F32)
        b = (wide - a).astype(BF16).astype(F32)
        c = (wide - a - b).astype(BF16).astype(F32)
        return jnp.concatenate([a, b, c, jnp.zeros((8, 256), F32)], axis=0)

    def one(job):
        whole = not isinstance(job, tuple)
        lower, upper, t, outer, mask = (job, job, job, None, None) if whole else job

        def put(ref, at, value):
            if mask is not None:
                rows = value.shape[0]
                mine = jnp.where(lanes(rows) < 64, 0, 1) == mask
                value = jnp.where(mine, value, ref[at].astype(F32))
            ref[at] = value.astype(ref.dtype)

        here_low, info = pk[lower + 1, 0:8], pk[lower + 1, 8:16]
        g_prev, g_low, g_high, g_next = (pk[n, 14:15] for n in (lower, lower + 1, upper + 1, upper + 2))
        beside = jnp.where(low, pk[upper + 2, 0:8], pk[lower, 0:8])
        parts = thirds(jnp.concatenate([here_low, beside], axis=1))
        here = here_low
        if not whole:
            here_high = pk[upper + 1, 0:8]
            here = jnp.where(low, here_low, here_high)
            info = jnp.where(low, info, pk[upper + 1, 8:16])
            parts = jnp.concatenate([parts, thirds(jnp.concatenate([here_high, beside], axis=1))], axis=0)
        parts = parts.astype(BF16)
        table = jnp.concatenate(
            [
                jnp.where(head, turn(g_prev) + 192.0, turn(g_low) + 64.0),
                jnp.where(head, g_high, g_next + 128.0),
                jnp.zeros((14, 128), F32),
            ],
            axis=0,
        )[:, 0:32].astype(BF16)
        count = info[3:4]
        sums = [None] * 9
        for k, row in enumerate((4, 1, 5, 2)):
            e = info[row : row + 1]
            hit = jnp.where(ghost_spot == e, 1.0, 0.0).astype(BF16)
            far = dot(table, hit)
            n = jnp.where(
                e < 64.0, e + jnp.where(low1, 0.0, 64.0), jnp.where(low1, far[0:1], far[1:2])
            )
            one_hot = jnp.where(spot == n, 1.0, 0.0)
            put(hot, (t, slice(None), slice(k * 128, (k + 1) * 128)), one_hot)
            got = dot(parts, one_hot.astype(BF16))
            there = got[0:8] + (got[8:16] + got[16:24])
            if not whole:
                there = jnp.where(low, there, got[32:40] + (got[40:48] + got[48:56]))
            off = there - here
            x, y, z = off[0:1], off[1:2], off[2:3]
            q = x * x + y * y + z * z
            live = jnp.where(count > float(k), 0.25, 0.0)
            g = jnp.exp(-rate * q) * live
            both = jnp.concatenate([g, g * there[3:4]], axis=0)
            harmonic = [
                None, x, y, z, ROOT3 * x * y, ROOT3 * y * z, 0.5 * (3.0 * z * z - q), ROOT3 * x * z,
                (0.5 * ROOT3) * (x * x - y * y),
            ]
            put(gp, (t, k), both)
            put(ys, (t, k), jnp.concatenate(harmonic[1:9], axis=0))
            for l in range(9):
                term = both if l == 0 else harmonic[l] * both
                sums[l] = term if sums[l] is None else sums[l] + term
            yield
        high, lo = split(jnp.concatenate(sums, axis=1))
        moments = dot(w_one_cat, jnp.concatenate([high, lo, high], axis=0))
        yield
        m = [moments[:, l * 128 : (l + 1) * 128] for l in range(9)]
        for l in range(9):
            put(mom_one, (t, l), m[l])
        inv = jnp.concatenate(
            [m[0] * m[0], sum(m[l] * m[l] for l in (1, 2, 3)), sum(m[l] * m[l] for l in range(4, 9))],
            axis=0,
        )
        v = dot3(mix1_t, inv)
        yield
        sig = sigmoid(v)
        put(slope_one, (t,), sig * (1.0 + v * (1.0 - sig)))
        h = base_col + here[3:4] * step_col + v * sig
        u = dot3(prj_t, h)
        put(u_two, (t,), u)
        if outer is not None:
            u_two[outer] = u
        yield

    abreast([one(job) for job in jobs])


def forms_kernel(
    sent, embed, radial_one, radial_two, mix_one, mix_two, proj, readout,
    mix_back, mix_fwd, prj_all, columns, first_cat, first_parts, second_cat, second_parts,
):
    del sent

    def column(row):
        return jnp.broadcast_to(row, (128, 128)).T

    columns[0] = column(embed[0:1])
    columns[1] = column(embed[1:2] - embed[0:1])
    columns[2] = column(readout[1:2])
    columns[3] = column(readout[0:1] + readout[1:2])
    for n, mix in enumerate((mix_one, mix_two)):
        mix_back[n] = thrice(mix[...])
        mix_fwd[n] = thrice(mix[...].T)
    prj_all[0] = thrice(proj[...])
    prj_all[1] = thrice(proj[...].T)
    base, step = embed[0:1], embed[1:2] - embed[0:1]
    high, lo = split(jnp.concatenate([radial_one[...] * base, radial_one[...] * step], axis=0))
    first_parts[...] = jnp.concatenate([high, high, lo], axis=1)
    first_cat[...] = jnp.concatenate([high, high, lo], axis=0).astype(F32).T.astype(BF16)
    high, lo = split(radial_two[...])
    second_parts[...] = jnp.concatenate([high, high, lo], axis=1)
    high, lo = high.astype(F32), lo.astype(F32)
    second_cat[...] = jnp.concatenate([high, high, lo, jnp.zeros((8, 128), F32)], axis=0).T.astype(BF16)


def nodes_of_edges(t, m, hot, gp, u_two, second_cat, tk, gk, rk):
    low_wide = lanes(128) < 64
    beside = jnp.where(low_wide, u_two[t + 1], u_two[t - 1])
    high, lo = split(jnp.concatenate([u_two[t], beside], axis=1))
    parts = jnp.concatenate([high, lo], axis=0)
    for k in range(4):
        got = dot(parts, hot[t, :, k * 128 : (k + 1) * 128])
        nodes = got[0:128] + got[128:256]
        g = gp[t, k, 0:8]
        gh = g.astype(BF16).astype(F32)
        rows = jnp.concatenate([gh, g - gh, gh, jnp.zeros((8, 128), F32)], axis=0).astype(BF16)
        weight = dot(second_cat[...], rows)
        gk[m, k] = nodes
        rk[m, k] = weight
        tk[m, k] = nodes * weight


def edge_sums(t, ys):
    edge = [[ys[t, k, c : c + 1] for c in range(3)] for k in range(4)]
    scalar, legendre = {}, {}
    for i in range(4):
        for j in range(i, 4):
            scalar[i, j] = scalar[j, i] = sum(edge[i][c] * edge[j][c] for c in range(3))
    for i in range(4):
        for j in range(i, 4):
            legendre[i, j] = legendre[j, i] = 1.5 * scalar[i, j] * scalar[i, j] - 0.5 * scalar[i, i] * scalar[j, j]
    return edge, scalar, legendre


def invariants_two(t, m, ys, tk, v_one, v_two):
    _, scalar, legendre = edge_sums(t, ys)
    total = (tk[m, 0] + tk[m, 1]) + (tk[m, 2] + tk[m, 3])
    inv1 = inv2 = None
    for i in range(4):
        va = sum(scalar[i, j] * tk[m, j] for j in range(4))
        vb = sum(legendre[i, j] * tk[m, j] for j in range(4))
        v_one[m, i], v_two[m, i] = va, vb
        inv1 = va * tk[m, i] if inv1 is None else inv1 + va * tk[m, i]
        inv2 = vb * tk[m, i] if inv2 is None else inv2 + vb * tk[m, i]
    return jnp.concatenate([total * total, inv1, inv2], axis=0)


def mixing_back(m, inv, mix_back, mix_fwd, columns, dinv):
    v = dot3(mix_fwd[1], inv)
    sig = sigmoid(v)
    dv = columns[2] * (sig * (1.0 + v * (1.0 - sig)))
    dinv[m] = 2.0 * dot3(mix_back[1], dv)


def edges_back(t, m, hot, ys, gp, second_parts, tk, gk, rk, v_one, v_two, dinv, du_two, dvec):
    low_wide = lanes(128) < 64
    edge, scalar, _ = edge_sums(t, ys)
    rate = rates()
    d1, d2 = dinv[m, 128:256], dinv[m, 256:384]
    d0 = dinv[m, 0:128] * ((tk[m, 0] + tk[m, 1]) + (tk[m, 2] + tk[m, 3]))
    pull, bend = {}, {}
    for i in range(4):
        wa, wb = d1 * tk[m, i], d2 * tk[m, i]
        for j in range(i, 4):
            pull[i, j] = pull[j, i] = jnp.sum(wa * tk[m, j], axis=0, keepdims=True)
            bend[i, j] = bend[j, i] = jnp.sum(wb * tk[m, j], axis=0, keepdims=True)
    back = []
    for k in range(4):
        dt = d0 + d1 * v_one[m, k] + d2 * v_two[m, k]
        dg = dot3(second_parts[...], dt * gk[m, k])
        back.append(jnp.concatenate(split(dt * rk[m, k]), axis=0))
        dq = 0.5 * pull[k, k] + bend[k, k] * scalar[k, k] - jnp.sum(rate * gp[t, k, 0:8] * dg, axis=0, keepdims=True)
        d = [None] * 3
        for j in range(4):
            if j != k:
                dq = dq - 0.5 * bend[k, j] * scalar[j, j]
                tie = pull[k, j] + 3.0 * bend[k, j] * scalar[k, j]
                d = [tie * edge[j][c] if d[c] is None else d[c] + tie * edge[j][c] for c in range(3)]
        d = [d[c] + 2.0 * dq * edge[k][c] for c in range(3)]
        dvec[t, k] = jnp.concatenate(d + [jnp.zeros((5, 128), F32)], axis=0)
    back = dot_t(jnp.concatenate(back, axis=1), hot[t])
    back = back[0:128] + back[128:256]
    du_two[t] += back[:, 0:128]
    aside = back[:, 128:256]
    du_two[t + 1] += jnp.where(low_wide, aside, 0.0)
    du_two[t - 1] += jnp.where(low_wide, 0.0, aside)


def layer_two(
    tiles, hot, ys, gp, u_two, mix_back, mix_fwd, columns, second_cat, second_parts,
    tk, gk, rk, v_one, v_two, dinv, du_two, dvec,
):
    inv = {}
    for stage, m in ORDER:
        t = tiles[m]
        if stage == 0:
            nodes_of_edges(t, m, hot, gp, u_two, second_cat, tk, gk, rk)
        elif stage == 1:
            inv[m] = invariants_two(t, m, ys, tk, v_one, v_two)
        elif stage == 2:
            mixing_back(m, inv[m], mix_back, mix_fwd, columns, dinv)
        else:
            edges_back(t, m, hot, ys, gp, second_parts, tk, gk, rk, v_one, v_two, dinv, du_two, dvec)


def plane_first(packed, forms, pk, *state):
    mix_fwd, prj_all, columns, first_cat = forms[1:5]
    _, side, _ = whereabouts()
    pk[pl.ds(3 - 2 * side, 4)] = packed[...]
    weights = (first_cat[...], mix_fwd[0], prj_all[1], columns[0], columns[1])
    start = 3 - 2 * side
    halves = (5 - 2 * side, 2 - 2 * side, 2 + side, 5 - 5 * side, None)
    layer_one(pk, [start, start + 1, halves], weights, *state)


def plane_second(forms, hot, ys, gp, u_two, du_two, dvec, *scratch):
    mix_back, mix_fwd, _, columns, _, _, second_cat, second_parts = forms
    _, side, _ = whereabouts()
    du_two[...] = jnp.zeros_like(du_two)
    layer_two(
        [3 - 2 * side, 4 - 2 * side], hot, ys, gp, u_two, mix_back, mix_fwd, columns, second_cat, second_parts,
        *scratch, du_two, dvec,
    )


def is_early(s):
    return s < 4


def early_kernel(packed, *refs):
    forms, state, pk = refs[0:8], refs[10:16], refs[16]

    @pl.when(is_early(whereabouts()[2]))
    def _():
        plane_first(packed, forms, pk, *state)


def late_kernel(packed, *refs):
    forms = refs[0:8]
    hot, ys, gp, mom_one, slope_one, u_two, du_two, dvec, pk = refs[14:23]

    @pl.when(jnp.logical_not(is_early(whereabouts()[2])))
    def _():
        plane_first(packed, forms, pk, hot, ys, gp, mom_one, slope_one, u_two)

    plane_second(forms, hot, ys, gp, u_two, du_two, dvec, *refs[23:])


def force_kernel(packed, across, moment, *refs):
    mix_back, mix_fwd, prj_all, columns, first_cat, first_parts, second_cat, second_parts = refs[0:8]
    out, hot, ys, gp, mom_one, slope_one, u_two, du_two, dvec, pk, tk, gk, rk, v_one, v_two, dinv = refs[16:]
    _, side, _ = whereabouts()
    low = lanes(8) < 64
    pk[pl.ds(3 - 2 * side, 4)] = packed[...]
    pk[pl.ds(4 * side + 1, 2)] = across[...]
    weights = (first_cat[...], mix_fwd[0], prj_all[1], columns[0], columns[1])
    halves = (2 + 3 * side, 3 * side, 2 + side, 5 * side, side)
    layer_one(pk, [1 + 3 * side, halves], weights, hot, ys, gp, mom_one, slope_one, u_two)
    layer_two(
        [1 + 2 * side, 2 + 2 * side], hot, ys, gp, u_two, mix_back, mix_fwd, columns, second_cat, second_parts,
        tk, gk, rk, v_one, v_two, dinv, du_two, dvec,
    )
    rate = rates()

    def third(du, slope, mom, gs, harmonics, pushes, spots):
        dh = columns[3] + dot3(prj_all[0], du)
        yield
        dinv = 2.0 * dot3(mix_back[0], dh * slope)
        yield
        parts = []
        for l in range(9):
            part = 0 if l == 0 else 1 if l < 4 else 2
            parts.append(mom(l) * dinv[part * 128 : (part + 1) * 128])
        dm = dot3(first_parts[...], jnp.concatenate(parts, axis=1))
        yield
        dm = [dm[:, l * 128 : (l + 1) * 128] for l in range(9)]
        rate2 = jnp.concatenate([rate, rate], axis=0)
        back = None
        centre = None
        for k in range(4):
            g, yk, push = gs(k), harmonics(k), pushes(k)
            dg = dm[0]
            dys = []
            for l in range(1, 9):
                dg = dg + yk[l - 1 : l] * dm[l]
                dys.append(jnp.sum(g * dm[l], axis=0, keepdims=True))
            dq = -jnp.sum(rate2 * g * dg, axis=0, keepdims=True)
            x, y, z = yk[0:1], yk[1:2], yk[2:3]
            e1, e2, e3, e4, e5, e6, e7, e8 = dys
            dx = e1 + ROOT3 * (y * e4 + z * e7 + x * e8) + x * (2.0 * dq - e6)
            dy = e2 + ROOT3 * (x * e4 + z * e5 - y * e8) + y * (2.0 * dq - e6)
            dz = e3 + ROOT3 * (y * e5 + x * e7) + 2.0 * z * (dq + e6)
            d = push + jnp.concatenate([dx, dy, dz, jnp.zeros((5, 128), F32)], axis=0)
            centre = d if centre is None else centre + d
            d_high = d.astype(BF16).astype(F32)
            rows = jnp.concatenate([d_high, d - d_high], axis=0).astype(BF16)
            term = dot_t(rows, spots(k))
            back = term if back is None else back + term
            yield
        return back[0:8] + back[8:16], centre

    def own_tile(t):
        return third(
            du_two[t], slope_one[t], lambda l: mom_one[t, l], lambda k: gp[t, k], lambda k: ys[t, k],
            lambda k: dvec[t, k], lambda k: hot[t, :, k * 128 : (k + 1) * 128],
        )

    def mixed(ref, *at):
        right, left = ref[(4,) + at], ref[(1,) + at]
        keep = lax.broadcasted_iota(jnp.int32, right.shape, 1) < 64
        return jnp.where(keep, right, left)

    def mixed_spots(k):
        at = (slice(128, 256), slice(k * 128, (k + 1) * 128))
        keep = lanes(128) < 64
        return jnp.where(keep, hot[(4,) + at].astype(F32), hot[(1,) + at].astype(F32)).astype(BF16)

    rim = third(
        mixed(du_two), mixed(slope_one), lambda l: mixed(mom_one, l), lambda k: mixed(gp, k), lambda k: mixed(ys, k),
        lambda k: mixed(dvec, k), mixed_spots,
    )
    (back2, centre2), (back3, centre3), (rim, _) = abreast([own_tile(2), own_tile(3), rim])
    f2 = centre2 - back2[:, 0:128] - jnp.where(low, rim, back3[:, 128:256])
    f3 = centre3 - back3[:, 0:128] - jnp.where(low, back2[:, 128:256], rim)
    row = lax.broadcasted_iota(jnp.int32, (8, 128), 0)
    for t, f in enumerate((f2, f3)):
        coords, drift = pk[t + 3, 0:8], pltpu.roll(moment[t], 3, 0)
        out[2 * t] = jnp.where(row < 3, jnp.where(low, f, turn(coords)), drift)
        out[2 * t + 1] = jnp.where(row < 3, jnp.where(low, turn(f), coords), turn(drift))


def finish_kernel(got, pos_out, mom_out, force_out):
    _, side, _ = whereabouts()
    for b in range(4):
        block = got[b ^ (2 * side)]
        turned = turn(block)
        for c in range(3):
            force = block[c : c + 1, 0:64]
            pos_out[c, b : b + 1] = turned[c : c + 1, 0:64]
            mom_out[c, b : b + 1] = block[3 + c : 4 + c, 0:64] + 0.5 * force
            force_out[c, b : b + 1] = force


def shape(*dims):
    return jax.ShapeDtypeStruct(dims, F32)


def room(mib):
    return pltpu.CompilerParams(vmem_limit_bytes=mib << 20)


def near(*dims, dtype=F32):
    return pltpu.VMEM(dims, dtype)


def far(x):
    return pltpu.with_memory_space_constraint(x, pltpu.HBM)


def keep(x):
    return pltpu.with_memory_space_constraint(x, pltpu.VMEM)


def on_device(
    positions, momenta, forces, species, neighbours, counts, ghost_rows,
    embed, radial_one, radial_two, mix_one, mix_two, projection, readout,
):
    count = lax.axis_size("space")
    both = ("bead", "space")
    planes = [[b * count + z * 8 + i for b in range(4) for i in range(8)] for z in range(count // 8)]
    quads = [[b * count + h * 4 + i for i in range(4)] for b in range(4) for h in range(count // 4)]
    beside = []
    for b in range(4):
        for z in range(count // 8):
            for i in range(4):
                here = b * count + z * 8 + i
                back = b * count + (z * 8 - 4) % count + (i ^ 2)
                beside += [(here, back), (back, here)]

    turned = [jnp.transpose(x, (1, 0, 2)) for x in (positions, momenta, forces)]
    sent = pl.pallas_call(
        pack_kernel, out_shape=shape(32, 8, 128), in_specs=[VM] * 8, out_specs=VM, name="pack",
    )(*[far(x) for x in (jnp.asarray(mode_tables()), *turned, species[None, :], neighbours, counts, ghost_rows)])
    got = keep(lax.all_to_all(sent, both, 0, 0, axis_index_groups=planes))
    forms = pl.pallas_call(
        forms_kernel,
        out_shape=(
            near(2, 384, 384, dtype=BF16), near(2, 128, 1152, dtype=BF16),
            near(2, 128, 384, dtype=BF16), near(4, 128, 128), near(128, 48, dtype=BF16),
            near(16, 384, dtype=BF16), near(128, 32, dtype=BF16), near(8, 384, dtype=BF16),
        ),
        in_specs=[pl.BlockSpec(memory_space=pl.ANY)] + [VM] * 7,
        out_specs=(VM,) * 8,
        compiler_params=room(8),
        cost_estimate=pl.CostEstimate(flops=2_000_000_000, bytes_accessed=4_000_000, transcendentals=0),
        name="forms",
    )(*[far(x) for x in (sent, embed, radial_one, radial_two, mix_one, mix_two, projection, readout)])
    packed, own, moment = pl.pallas_call(
        modes_kernel,
        out_shape=(near(4, 16, 128), near(2, 16, 128), near(2, 8, 128)),
        in_specs=[VM],
        out_specs=(VM,) * 3,
        compiler_params=room(16),
        name="modes",
    )(got)
    kept = (
        near(TILES, 256, 512, dtype=BF16),
        near(TILES, 4, 8, 128),
        near(TILES, 4, 16, 128),
        near(TILES, 9, 128, 128),
        near(TILES, 128, 128),
        near(TILES, 128, 128),
        near(TILES, 128, 128),
        near(TILES, 4, 8, 128),
    )

    def scratch():
        return [near(8, 16, 128)] + [near(2, 4, 128, 128)] * 5 + [near(2, 384, 128)]

    own, *state = pl.pallas_call(
        early_kernel,
        out_shape=(near(2, 16, 128),) + kept[:6],
        in_specs=[VM] * 10,
        out_specs=(VM,) * 7,
        scratch_shapes=[near(8, 16, 128)],
        input_output_aliases={9: 0},
        compiler_params=room(24),
        name="early",
    )(packed, *forms, own)
    across = keep(lax.ppermute(own, both, beside))
    state = pl.pallas_call(
        late_kernel,
        out_shape=kept,
        in_specs=[VM] * 15,
        out_specs=(VM,) * 8,
        scratch_shapes=scratch(),
        input_output_aliases={9 + i: i for i in range(6)},
        compiler_params=room(24),
        cost_estimate=pl.CostEstimate(flops=4_000_000_000, bytes_accessed=8_000_000, transcendentals=0),
        name="late",
    )(packed, *forms, *state)
    grad = pl.pallas_call(
        force_kernel,
        out_shape=(near(4, 8, 128),) + kept,
        in_specs=[VM] * 19,
        out_specs=(VM,) * 9,
        scratch_shapes=scratch(),
        input_output_aliases={11 + i: 1 + i for i in range(8)},
        compiler_params=room(24),
        name="force",
    )(packed, across, moment, *forms, *state)[0]
    back = keep(lax.all_to_all(grad, both, 0, 0, axis_index_groups=quads))
    outs = pl.pallas_call(
        finish_kernel,
        out_shape=(shape(3, 4, 64),) * 3,
        in_specs=[VM],
        out_specs=(VM,) * 3,
        compiler_params=room(8),
        name="finish",
    )(back)
    return tuple(jnp.transpose(x, (1, 0, 2)) for x in outs)


def solution(mesh):
    spread = P("bead", None, "space")
    placed = (
        spread, spread, spread, P("space"), spread, P("bead", "space"), P("space", None, None),
    ) + (P(),) * 7
    return jax.shard_map(
        on_device, mesh=mesh, in_specs=placed, out_specs=(spread,) * 3, check_vma=False
    )
```

```python
import numpy as np

import jax
import jax.numpy as jnp
from jax import lax
from jax.experimental import pallas as pl
from jax.experimental.pallas import tpu as pltpu
from jax.sharding import PartitionSpec as P


F32 = jnp.float32
BF16 = jnp.bfloat16
BEADS = 16
TILES = 6
ROOT3 = float(np.sqrt(3.0))
VM = pl.BlockSpec(memory_space=pltpu.VMEM)
RATES = 0.25 * 16.0 ** (np.arange(8) / 7.0)


def propagators():
    n = BEADS
    b = np.arange(n)
    phase = 2.0 * np.pi * np.outer(b, b) / n
    matrix = np.where(b[None] < n // 2, np.cos(phase), np.sin(phase)) * np.sqrt(2.0 / n)
    matrix[:, n // 2] = np.where(b % 2 == 0, 1.0, -1.0) / np.sqrt(n)
    matrix[:, 0] = 1.0 / np.sqrt(n)
    w = 1.5 * np.sin(np.pi * b / n)
    drift = np.where(b == 0, 1.0, np.sin(w) / np.where(b == 0, 1.0, w))
    return [(matrix * d) @ matrix.T for d in (np.cos(w), drift, w * np.sin(w))]


def mode_tables():
    cosine, drift, stiff = propagators()
    rows = np.zeros((4, 4, 64, 16))
    for sender in range(4):
        for bead in range(BEADS):
            for c in range(3):
                for b in range(4):
                    for n, values in enumerate((cosine, drift, cosine, stiff)):
                        rows[sender, n, 4 * bead + c, 4 * c + b] = values[bead, 4 * sender + b]
    rows = rows.astype(np.float32).reshape(4, 2, 128, 16)
    one = rows.astype(BF16)
    two = (rows - one.astype(np.float32)).astype(BF16)
    three = (rows - one.astype(np.float32) - two.astype(np.float32)).astype(BF16)
    return np.concatenate([one, one, two, two, one, three], axis=-1)


def parts_of(x):
    one = x.astype(BF16)
    rest = x - one.astype(F32)
    two = rest.astype(BF16)
    three = (rest - two.astype(F32)).astype(BF16)
    return jnp.concatenate([one, two, one, two, three, one], axis=0)

def split(x):
    high = x.astype(BF16)
    return high, (x - high.astype(F32)).astype(BF16)


def dot(a, b):
    return lax.dot_general(a, b, (((1,), (0,)), ((), ())), preferred_element_type=F32)


def dot_t(a, b):
    return lax.dot_general(a, b, (((1,), (1,)), ((), ())), preferred_element_type=F32)


def thrice(x):
    high, lo = split(x)
    return jnp.concatenate([high, high, lo], axis=1)


def dot3(a, b):
    high, lo = split(b)
    return dot(a, jnp.concatenate([high, lo, high], axis=0))


def lanes(rows):
    return lax.broadcasted_iota(jnp.int32, (rows, 128), 1)


def turn(x):
    return pltpu.roll(x, 64, 1)


def pick(y):
    return (y % 4) ^ (2 * (y // 4))


def whereabouts():
    s = lax.axis_index("space")
    return lax.axis_index("bead"), (s & 7) >> 2, s


def pack_kernel(table, pos, mom, force, species, nbr, counts, ghost, out):
    r, _, _ = whereabouts()
    low = lanes(64) < 64
    kind = species[...].astype(F32)
    mass = 1.0 + 15.0 * kind
    blank = jnp.zeros((4, 64), F32)
    coords = jnp.concatenate([pos[0], pos[1], pos[2], blank], axis=0)
    kicked = jnp.concatenate([mom[c] + 0.5 * force[c] for c in range(3)] + [blank], axis=0)
    moved = dot(table[r, 0], parts_of(jnp.concatenate([coords, kicked / mass], axis=1)))
    driven = dot(table[r, 1], parts_of(jnp.concatenate([mass * coords, kicked], axis=1)))
    shares = jnp.where(low, moved[0:64] + turn(moved[64:128]), driven[0:64] - turn(driven[64:128]))
    ghosts = ghost[0].astype(F32)
    last = jnp.concatenate([ghosts[0:1], ghosts[1:2], jnp.zeros((1, 96), F32)], axis=1)
    row = lax.broadcasted_iota(jnp.int32, (8, 128), 0)
    for bead in range(4):
        e = nbr[bead].astype(F32)
        info = jnp.concatenate(
            [
                jnp.zeros((3, 128), F32),
                jnp.concatenate([counts[bead : bead + 1].astype(F32), kind], axis=1),
                jnp.concatenate([e[0:1], e[1:2]], axis=1),
                jnp.concatenate([e[2:3], e[3:4]], axis=1),
                last,
                jnp.zeros((1, 128), F32),
            ],
            axis=0,
        )
        for to in range(4):
            n = (4 * to + bead) // 2
            share = shares[8 * n : 8 * n + 8]
            if bead % 2:
                share = pltpu.roll(share, 4, 0)
            block = jnp.where(row < 3, share, info)
            for y in range(8):
                if pick(y) == bead:
                    out[to * 8 + y] = block


def modes_kernel(got, packed, own, moment):
    r, side, _ = whereabouts()
    low = lanes(8) < 64
    row = lax.broadcasted_iota(jnp.int32, (8, 128), 0)
    moments = []
    for t in range(4):
        even, odd = (
            (got[d] + got[8 + d]) + (got[16 + d] + got[24 + d]) for d in (2 * t, 2 * t + 1)
        )
        info_even, info_odd = got[r * 8 + 2 * t], got[r * 8 + 2 * t + 1]
        left = jnp.where(low, info_even, turn(info_odd))
        right = jnp.where(low, turn(info_even), info_odd)
        coords = jnp.where(low, even, turn(odd))
        moments.append(jnp.where(low, turn(even), odd))
        packed[t, 0:8] = jnp.where(row < 3, coords, jnp.broadcast_to(right[3:4], (8, 128)))
        packed[t, 8:16] = jnp.where(row < 3, pltpu.roll(right, 5, 0), left)
    for t in range(2):
        moment[t] = jnp.where(side == 1, moments[2 + t], moments[t])
    own[...] = packed[pl.ds(2 * side, 2)]


ORDER = ((0, 0), (0, 1), (1, 0), (1, 1), (2, 0), (2, 1), (3, 0), (3, 1))


def rates():
    row = lax.broadcasted_iota(jnp.int32, (8, 128), 0)
    rate = jnp.zeros((8, 128), F32)
    for n in range(8):
        rate = jnp.where(row == n, float(RATES[n]), rate)
    return rate


def abreast(jobs):
    results = [None] * len(jobs)
    left = list(range(len(jobs)))
    while left:
        for n in list(left):
            try:
                next(jobs[n])
            except StopIteration as stop:
                results[n] = stop.value
                left.remove(n)
    return results


def sigmoid(v):
    return 1.0 / (1.0 + jnp.exp(-v))


def layer_one(pk, jobs, weights, hot, ys, gp, mom_one, slope_one, u_two):
    w_one_cat, mix1_t, prj_t, base_col, step_col = weights
    low = lanes(8) < 64
    low1 = lanes(1) < 64
    head = lanes(1) < 16
    rate = rates()
    spot = lax.broadcasted_iota(jnp.int32, (256, 128), 0).astype(F32)
    ghost_spot = lax.broadcasted_iota(jnp.int32, (32, 128), 0).astype(F32) + 64.0

    def thirds(wide):
        a = wide.astype(BF16).astype(F32)
        b = (wide - a).astype(BF16).astype(F32)
        c = (wide - a - b).astype(BF16).astype(F32)
        return jnp.concatenate([a, b, c, jnp.zeros((8, 256), F32)], axis=0)

    def one(job):
        whole = not isinstance(job, tuple)
        lower, upper, t, outer, mask = (job, job, job, None, None) if whole else job

        def put(ref, at, value):
            if mask is not None:
                rows = value.shape[0]
                mine = jnp.where(lanes(rows) < 64, 0, 1) == mask
                value = jnp.where(mine, value, ref[at].astype(F32))
            ref[at] = value.astype(ref.dtype)

        here_low, info = pk[lower + 1, 0:8], pk[lower + 1, 8:16]
        g_prev, g_low, g_high, g_next = (pk[n, 14:15] for n in (lower, lower + 1, upper + 1, upper + 2))
        beside = jnp.where(low, pk[upper + 2, 0:8], pk[lower, 0:8])
        parts = thirds(jnp.concatenate([here_low, beside], axis=1))
        here = here_low
        if not whole:
            here_high = pk[upper + 1, 0:8]
            here = jnp.where(low, here_low, here_high)
            info = jnp.where(low, info, pk[upper + 1, 8:16])
            parts = jnp.concatenate([parts, thirds(jnp.concatenate([here_high, beside], axis=1))], axis=0)
        parts = parts.astype(BF16)
        table = jnp.concatenate(
            [
                jnp.where(head, turn(g_prev) + 192.0, turn(g_low) + 64.0),
                jnp.where(head, g_high, g_next + 128.0),
                jnp.zeros((14, 128), F32),
            ],
            axis=0,
        )[:, 0:32].astype(BF16)
        count = info[3:4]
        sums = [None] * 9
        for k, row in enumerate((4, 1, 5, 2)):
            e = info[row : row + 1]
            hit = jnp.where(ghost_spot == e, 1.0, 0.0).astype(BF16)
            far = dot(table, hit)
            n = jnp.where(
                e < 64.0, e + jnp.where(low1, 0.0, 64.0), jnp.where(low1, far[0:1], far[1:2])
            )
            one_hot = jnp.where(spot == n, 1.0, 0.0)
            put(hot, (t, slice(None), slice(k * 128, (k + 1) * 128)), one_hot)
            got = dot(parts, one_hot.astype(BF16))
            there = got[0:8] + (got[8:16] + got[16:24])
            if not whole:
                there = jnp.where(low, there, got[32:40] + (got[40:48] + got[48:56]))
            off = there - here
            x, y, z = off[0:1], off[1:2], off[2:3]
            q = x * x + y * y + z * z
            live = jnp.where(count > float(k), 0.25, 0.0)
            g = jnp.exp(-rate * q) * live
            both = jnp.concatenate([g, g * there[3:4]], axis=0)
            harmonic = [
                None, x, y, z, ROOT3 * x * y, ROOT3 * y * z, 0.5 * (3.0 * z * z - q), ROOT3 * x * z,
                (0.5 * ROOT3) * (x * x - y * y),
            ]
            put(gp, (t, k), both)
            put(ys, (t, k), jnp.concatenate(harmonic[1:9], axis=0))
            for l in range(9):
                term = both if l == 0 else harmonic[l] * both
                sums[l] = term if sums[l] is None else sums[l] + term
        yield
        high, lo = split(jnp.concatenate(sums, axis=1))
        moments = dot(w_one_cat, jnp.concatenate([high, lo, high], axis=0))
        yield
        m = [moments[:, l * 128 : (l + 1) * 128] for l in range(9)]
        for l in range(9):
            put(mom_one, (t, l), m[l])
        inv = jnp.concatenate(
            [m[0] * m[0], sum(m[l] * m[l] for l in (1, 2, 3)), sum(m[l] * m[l] for l in range(4, 9))],
            axis=0,
        )
        v = dot3(mix1_t, inv)
        yield
        sig = sigmoid(v)
        put(slope_one, (t,), sig * (1.0 + v * (1.0 - sig)))
        h = base_col + here[3:4] * step_col + v * sig
        u = dot3(prj_t, h)
        put(u_two, (t,), u)
        if outer is not None:
            u_two[outer] = u
        yield

    abreast([one(job) for job in jobs])


def forms_kernel(
    sent, embed, radial_one, radial_two, mix_one, mix_two, proj, readout,
    mix_back, mix_fwd, prj_all, columns, first_cat, first_parts, second_cat, second_parts,
):
    del sent

    def column(row):
        return jnp.broadcast_to(row, (128, 128)).T

    columns[0] = column(embed[0:1])
    columns[1] = column(embed[1:2] - embed[0:1])
    columns[2] = column(readout[1:2])
    columns[3] = column(readout[0:1] + readout[1:2])
    for n, mix in enumerate((mix_one, mix_two)):
        mix_back[n] = thrice(mix[...])
        mix_fwd[n] = thrice(mix[...].T)
    prj_all[0] = thrice(proj[...])
    prj_all[1] = thrice(proj[...].T)
    base, step = embed[0:1], embed[1:2] - embed[0:1]
    high, lo = split(jnp.concatenate([radial_one[...] * base, radial_one[...] * step], axis=0))
    first_parts[...] = jnp.concatenate([high, high, lo], axis=1)
    first_cat[...] = jnp.concatenate([high, high, lo], axis=0).astype(F32).T.astype(BF16)
    high, lo = split(radial_two[...])
    second_parts[...] = jnp.concatenate([high, high, lo], axis=1)
    high, lo = high.astype(F32), lo.astype(F32)
    second_cat[...] = jnp.concatenate([high, high, lo, jnp.zeros((8, 128), F32)], axis=0).T.astype(BF16)


def nodes_of_edges(t, m, hot, gp, u_two, second_cat, tk, gk, rk):
    low_wide = lanes(128) < 64
    beside = jnp.where(low_wide, u_two[t + 1], u_two[t - 1])
    high, lo = split(jnp.concatenate([u_two[t], beside], axis=1))
    parts = jnp.concatenate([high, lo], axis=0)
    for k in range(4):
        got = dot(parts, hot[t, :, k * 128 : (k + 1) * 128])
        nodes = got[0:128] + got[128:256]
        g = gp[t, k, 0:8]
        gh = g.astype(BF16).astype(F32)
        rows = jnp.concatenate([gh, g - gh, gh, jnp.zeros((8, 128), F32)], axis=0).astype(BF16)
        weight = dot(second_cat[...], rows)
        gk[m, k] = nodes
        rk[m, k] = weight
        tk[m, k] = nodes * weight


def edge_sums(t, ys):
    edge = [[ys[t, k, c : c + 1] for c in range(3)] for k in range(4)]
    scalar, legendre = {}, {}
    for i in range(4):
        for j in range(i, 4):
            scalar[i, j] = scalar[j, i] = sum(edge[i][c] * edge[j][c] for c in range(3))
    for i in range(4):
        for j in range(i, 4):
            legendre[i, j] = legendre[j, i] = 1.5 * scalar[i, j] * scalar[i, j] - 0.5 * scalar[i, i] * scalar[j, j]
    return edge, scalar, legendre


def invariants_two(t, m, ys, tk, v_one, v_two):
    _, scalar, legendre = edge_sums(t, ys)
    total = (tk[m, 0] + tk[m, 1]) + (tk[m, 2] + tk[m, 3])
    inv1 = inv2 = None
    for i in range(4):
        va = sum(scalar[i, j] * tk[m, j] for j in range(4))
        vb = sum(legendre[i, j] * tk[m, j] for j in range(4))
        v_one[m, i], v_two[m, i] = va, vb
        inv1 = va * tk[m, i] if inv1 is None else inv1 + va * tk[m, i]
        inv2 = vb * tk[m, i] if inv2 is None else inv2 + vb * tk[m, i]
    return jnp.concatenate([total * total, inv1, inv2], axis=0)


def mixing_back(m, inv, mix_back, mix_fwd, columns, dinv):
    v = dot3(mix_fwd[1], inv)
    sig = sigmoid(v)
    dv = columns[2] * (sig * (1.0 + v * (1.0 - sig)))
    dinv[m] = 2.0 * dot3(mix_back[1], dv)


def edges_back(t, m, hot, ys, gp, second_parts, tk, gk, rk, v_one, v_two, dinv, du_two, dvec):
    low_wide = lanes(128) < 64
    edge, scalar, _ = edge_sums(t, ys)
    rate = rates()
    d1, d2 = dinv[m, 128:256], dinv[m, 256:384]
    d0 = dinv[m, 0:128] * ((tk[m, 0] + tk[m, 1]) + (tk[m, 2] + tk[m, 3]))
    pull, bend = {}, {}
    for i in range(4):
        wa, wb = d1 * tk[m, i], d2 * tk[m, i]
        for j in range(i, 4):
            pull[i, j] = pull[j, i] = jnp.sum(wa * tk[m, j], axis=0, keepdims=True)
            bend[i, j] = bend[j, i] = jnp.sum(wb * tk[m, j], axis=0, keepdims=True)
    back = []
    for k in range(4):
        dt = d0 + d1 * v_one[m, k] + d2 * v_two[m, k]
        dg = dot3(second_parts[...], dt * gk[m, k])
        back.append(jnp.concatenate(split(dt * rk[m, k]), axis=0))
        dq = 0.5 * pull[k, k] + bend[k, k] * scalar[k, k] - jnp.sum(rate * gp[t, k, 0:8] * dg, axis=0, keepdims=True)
        d = [None] * 3
        for j in range(4):
            if j != k:
                dq = dq - 0.5 * bend[k, j] * scalar[j, j]
                tie = pull[k, j] + 3.0 * bend[k, j] * scalar[k, j]
                d = [tie * edge[j][c] if d[c] is None else d[c] + tie * edge[j][c] for c in range(3)]
        d = [d[c] + 2.0 * dq * edge[k][c] for c in range(3)]
        dvec[t, k] = jnp.concatenate(d + [jnp.zeros((5, 128), F32)], axis=0)
    back = dot_t(jnp.concatenate(back, axis=1), hot[t])
    back = back[0:128] + back[128:256]
    du_two[t] += back[:, 0:128]
    aside = back[:, 128:256]
    du_two[t + 1] += jnp.where(low_wide, aside, 0.0)
    du_two[t - 1] += jnp.where(low_wide, 0.0, aside)


def layer_two(
    tiles, hot, ys, gp, u_two, mix_back, mix_fwd, columns, second_cat, second_parts,
    tk, gk, rk, v_one, v_two, dinv, du_two, dvec,
):
    inv = {}
    for stage, m in ORDER:
        t = tiles[m]
        if stage == 0:
            nodes_of_edges(t, m, hot, gp, u_two, second_cat, tk, gk, rk)
        elif stage == 1:
            inv[m] = invariants_two(t, m, ys, tk, v_one, v_two)
        elif stage == 2:
            mixing_back(m, inv[m], mix_back, mix_fwd, columns, dinv)
        else:
            edges_back(t, m, hot, ys, gp, second_parts, tk, gk, rk, v_one, v_two, dinv, du_two, dvec)


def plane_first(packed, forms, pk, *state):
    mix_fwd, prj_all, columns, first_cat = forms[1:5]
    _, side, _ = whereabouts()
    pk[pl.ds(3 - 2 * side, 4)] = packed[...]
    weights = (first_cat[...], mix_fwd[0], prj_all[1], columns[0], columns[1])
    start = 3 - 2 * side
    halves = (5 - 2 * side, 2 - 2 * side, 2 + side, 5 - 5 * side, None)
    layer_one(pk, [start, start + 1, halves], weights, *state)


def plane_second(forms, hot, ys, gp, u_two, du_two, dvec, *scratch):
    mix_back, mix_fwd, _, columns, _, _, second_cat, second_parts = forms
    _, side, _ = whereabouts()
    du_two[...] = jnp.zeros_like(du_two)
    layer_two(
        [3 - 2 * side, 4 - 2 * side], hot, ys, gp, u_two, mix_back, mix_fwd, columns, second_cat, second_parts,
        *scratch, du_two, dvec,
    )


def is_early(s):
    return s < 4


def early_kernel(packed, *refs):
    forms, state, pk = refs[0:8], refs[10:16], refs[16]

    @pl.when(is_early(whereabouts()[2]))
    def _():
        plane_first(packed, forms, pk, *state)


def late_kernel(packed, *refs):
    forms = refs[0:8]
    hot, ys, gp, mom_one, slope_one, u_two, du_two, dvec, pk = refs[14:23]

    @pl.when(jnp.logical_not(is_early(whereabouts()[2])))
    def _():
        plane_first(packed, forms, pk, hot, ys, gp, mom_one, slope_one, u_two)

    plane_second(forms, hot, ys, gp, u_two, du_two, dvec, *refs[23:])


def force_kernel(packed, across, moment, *refs):
    mix_back, mix_fwd, prj_all, columns, first_cat, first_parts, second_cat, second_parts = refs[0:8]
    out, hot, ys, gp, mom_one, slope_one, u_two, du_two, dvec, pk, tk, gk, rk, v_one, v_two, dinv = refs[16:]
    _, side, _ = whereabouts()
    low = lanes(8) < 64
    pk[pl.ds(3 - 2 * side, 4)] = packed[...]
    pk[pl.ds(4 * side + 1, 2)] = across[...]
    weights = (first_cat[...], mix_fwd[0], prj_all[1], columns[0], columns[1])
    halves = (2 + 3 * side, 3 * side, 2 + side, 5 * side, side)
    layer_one(pk, [1 + 3 * side, halves], weights, hot, ys, gp, mom_one, slope_one, u_two)
    layer_two(
        [1 + 2 * side, 2 + 2 * side], hot, ys, gp, u_two, mix_back, mix_fwd, columns, second_cat, second_parts,
        tk, gk, rk, v_one, v_two, dinv, du_two, dvec,
    )
    rate = rates()

    def third(du, slope, mom, gs, harmonics, pushes, spots):
        dh = columns[3] + dot3(prj_all[0], du)
        yield
        dinv = 2.0 * dot3(mix_back[0], dh * slope)
        yield
        parts = []
        for l in range(9):
            part = 0 if l == 0 else 1 if l < 4 else 2
            parts.append(mom(l) * dinv[part * 128 : (part + 1) * 128])
        dm = dot3(first_parts[...], jnp.concatenate(parts, axis=1))
        yield
        dm = [dm[:, l * 128 : (l + 1) * 128] for l in range(9)]
        rate2 = jnp.concatenate([rate, rate], axis=0)
        back = None
        centre = None
        for k in range(4):
            g, yk, push = gs(k), harmonics(k), pushes(k)
            dg = dm[0]
            dys = []
            for l in range(1, 9):
                dg = dg + yk[l - 1 : l] * dm[l]
                dys.append(jnp.sum(g * dm[l], axis=0, keepdims=True))
            dq = -jnp.sum(rate2 * g * dg, axis=0, keepdims=True)
            x, y, z = yk[0:1], yk[1:2], yk[2:3]
            e1, e2, e3, e4, e5, e6, e7, e8 = dys
            dx = e1 + ROOT3 * (y * e4 + z * e7 + x * e8) + x * (2.0 * dq - e6)
            dy = e2 + ROOT3 * (x * e4 + z * e5 - y * e8) + y * (2.0 * dq - e6)
            dz = e3 + ROOT3 * (y * e5 + x * e7) + 2.0 * z * (dq + e6)
            d = push + jnp.concatenate([dx, dy, dz, jnp.zeros((5, 128), F32)], axis=0)
            centre = d if centre is None else centre + d
            d_high = d.astype(BF16).astype(F32)
            rows = jnp.concatenate([d_high, d - d_high], axis=0).astype(BF16)
            term = dot_t(rows, spots(k))
            back = term if back is None else back + term
        return back[0:8] + back[8:16], centre

    def own_tile(t):
        return third(
            du_two[t], slope_one[t], lambda l: mom_one[t, l], lambda k: gp[t, k], lambda k: ys[t, k],
            lambda k: dvec[t, k], lambda k: hot[t, :, k * 128 : (k + 1) * 128],
        )

    def mixed(ref, *at):
        right, left = ref[(4,) + at], ref[(1,) + at]
        keep = lax.broadcasted_iota(jnp.int32, right.shape, 1) < 64
        return jnp.where(keep, right, left)

    def mixed_spots(k):
        at = (slice(128, 256), slice(k * 128, (k + 1) * 128))
        keep = lanes(128) < 64
        return jnp.where(keep, hot[(4,) + at].astype(F32), hot[(1,) + at].astype(F32)).astype(BF16)

    rim = third(
        mixed(du_two), mixed(slope_one), lambda l: mixed(mom_one, l), lambda k: mixed(gp, k), lambda k: mixed(ys, k),
        lambda k: mixed(dvec, k), mixed_spots,
    )
    (back2, centre2), (back3, centre3), (rim, _) = abreast([own_tile(2), own_tile(3), rim])
    f2 = centre2 - back2[:, 0:128] - jnp.where(low, rim, back3[:, 128:256])
    f3 = centre3 - back3[:, 0:128] - jnp.where(low, back2[:, 128:256], rim)
    row = lax.broadcasted_iota(jnp.int32, (8, 128), 0)
    for t, f in enumerate((f2, f3)):
        coords, drift = pk[t + 3, 0:8], pltpu.roll(moment[t], 3, 0)
        out[2 * t] = jnp.where(row < 3, jnp.where(low, f, turn(coords)), drift)
        out[2 * t + 1] = jnp.where(row < 3, jnp.where(low, turn(f), coords), turn(drift))


def finish_kernel(got, pos_out, mom_out, force_out):
    _, side, _ = whereabouts()
    for b in range(4):
        block = got[b ^ (2 * side)]
        turned = turn(block)
        for c in range(3):
            force = block[c : c + 1, 0:64]
            pos_out[c, b : b + 1] = turned[c : c + 1, 0:64]
            mom_out[c, b : b + 1] = block[3 + c : 4 + c, 0:64] + 0.5 * force
            force_out[c, b : b + 1] = force


def shape(*dims):
    return jax.ShapeDtypeStruct(dims, F32)


def room(mib):
    return pltpu.CompilerParams(vmem_limit_bytes=mib << 20)


def near(*dims, dtype=F32):
    return pltpu.VMEM(dims, dtype)


def far(x):
    return pltpu.with_memory_space_constraint(x, pltpu.HBM)


def keep(x):
    return pltpu.with_memory_space_constraint(x, pltpu.VMEM)


def on_device(
    positions, momenta, forces, species, neighbours, counts, ghost_rows,
    embed, radial_one, radial_two, mix_one, mix_two, projection, readout,
):
    count = lax.axis_size("space")
    both = ("bead", "space")
    planes = [[b * count + z * 8 + i for b in range(4) for i in range(8)] for z in range(count // 8)]
    quads = [[b * count + h * 4 + i for i in range(4)] for b in range(4) for h in range(count // 4)]
    beside = []
    for b in range(4):
        for z in range(count // 8):
            for i in range(4):
                here = b * count + z * 8 + i
                back = b * count + (z * 8 - 4) % count + (i ^ 2)
                beside += [(here, back), (back, here)]

    turned = [jnp.transpose(x, (1, 0, 2)) for x in (positions, momenta, forces)]
    sent = pl.pallas_call(
        pack_kernel, out_shape=shape(32, 8, 128), in_specs=[VM] * 8, out_specs=VM, name="pack",
    )(*[far(x) for x in (jnp.asarray(mode_tables()), *turned, species[None, :], neighbours, counts, ghost_rows)])
    got = keep(lax.all_to_all(sent, both, 0, 0, axis_index_groups=planes))
    forms = pl.pallas_call(
        forms_kernel,
        out_shape=(
            near(2, 384, 384, dtype=BF16), near(2, 128, 1152, dtype=BF16),
            near(2, 128, 384, dtype=BF16), near(4, 128, 128), near(128, 48, dtype=BF16),
            near(16, 384, dtype=BF16), near(128, 32, dtype=BF16), near(8, 384, dtype=BF16),
        ),
        in_specs=[pl.BlockSpec(memory_space=pl.ANY)] + [VM] * 7,
        out_specs=(VM,) * 8,
        compiler_params=room(8),
        cost_estimate=pl.CostEstimate(flops=2_000_000_000, bytes_accessed=4_000_000, transcendentals=0),
        name="forms",
    )(*[far(x) for x in (sent, embed, radial_one, radial_two, mix_one, mix_two, projection, readout)])
    packed, own, moment = pl.pallas_call(
        modes_kernel,
        out_shape=(near(4, 16, 128), near(2, 16, 128), near(2, 8, 128)),
        in_specs=[VM],
        out_specs=(VM,) * 3,
        compiler_params=room(16),
        name="modes",
    )(got)
    kept = (
        near(TILES, 256, 512, dtype=BF16),
        near(TILES, 4, 8, 128),
        near(TILES, 4, 16, 128),
        near(TILES, 9, 128, 128),
        near(TILES, 128, 128),
        near(TILES, 128, 128),
        near(TILES, 128, 128),
        near(TILES, 4, 8, 128),
    )

    def scratch():
        return [near(8, 16, 128)] + [near(2, 4, 128, 128)] * 5 + [near(2, 384, 128)]

    own, *state = pl.pallas_call(
        early_kernel,
        out_shape=(near(2, 16, 128),) + kept[:6],
        in_specs=[VM] * 10,
        out_specs=(VM,) * 7,
        scratch_shapes=[near(8, 16, 128)],
        input_output_aliases={9: 0},
        compiler_params=room(24),
        name="early",
    )(packed, *forms, own)
    across = keep(lax.ppermute(own, both, beside))
    state = pl.pallas_call(
        late_kernel,
        out_shape=kept,
        in_specs=[VM] * 15,
        out_specs=(VM,) * 8,
        scratch_shapes=scratch(),
        input_output_aliases={9 + i: i for i in range(6)},
        compiler_params=room(24),
        cost_estimate=pl.CostEstimate(flops=4_000_000_000, bytes_accessed=8_000_000, transcendentals=0),
        name="late",
    )(packed, *forms, *state)
    grad = pl.pallas_call(
        force_kernel,
        out_shape=(near(4, 8, 128),) + kept,
        in_specs=[VM] * 19,
        out_specs=(VM,) * 9,
        scratch_shapes=scratch(),
        input_output_aliases={11 + i: 1 + i for i in range(8)},
        compiler_params=room(24),
        name="force",
    )(packed, across, moment, *forms, *state)[0]
    back = keep(lax.all_to_all(grad, both, 0, 0, axis_index_groups=quads))
    outs = pl.pallas_call(
        finish_kernel,
        out_shape=(shape(3, 4, 64),) * 3,
        in_specs=[VM],
        out_specs=(VM,) * 3,
        compiler_params=room(8),
        name="finish",
    )(back)
    return tuple(jnp.transpose(x, (1, 0, 2)) for x in outs)


def solution(mesh):
    spread = P("bead", None, "space")
    placed = (
        spread, spread, spread, P("space"), spread, P("bead", "space"), P("space", None, None),
    ) + (P(),) * 7
    return jax.shard_map(
        on_device, mesh=mesh, in_specs=placed, out_specs=(spread,) * 3, check_vma=False
    )
```
